256 devices in a mesh: row: 8 (over z_hi, core), col: 32 (over x, z_lo, y).
Axes of the slice: x: 4, y: 4, z: 8 (z_hi: 4, z_lo: 2; z = z_hi * 2 + z_lo), core: 2. Of those that a mesh axis runs over, the one named last changes fastest.
Arguments:
- features: bfloat16 [131072, 128], P(('row', 'col')), may hold values from -6 to 6
- weight: bfloat16 [128, 128], replicated, may hold values from -0.5 to 0.5
- bias: float32 [128], replicated, may hold values from -3 to 3
- cotangent: bfloat16 [131072, 128], P(('row', 'col')), may hold values from -6 to 6
- block_count: int32 [8, 32], P('row', 'col'), may hold values from 64 to 512
- block_rows: int32 [8, 32, 512], P('row', 'col'), may hold values from 0 to 127
- block_cols: int32 [8, 32, 512], P('row', 'col'), may hold values from 0 to 31
- edge_offsets: int32 [8, 32, 512, 128], P('row', 'col'), may hold values from 0 to 16383, as said below
- edge_weight: bfloat16 [8, 32, 512, 128], P('row', 'col'), may hold values from 0.0099487305 to 0.099609375
Outputs:
- output: bfloat16 [131072, 128], P(('row', 'col'))
- grad_features: bfloat16 [131072, 128], P(('row', 'col'))
- grad_weight: float32 [128, 128], replicated
- grad_bias: float32 [128], replicated
The draws below stay inside these ranges and needn't reach their ends.
Inputs may be any that keep to these rules, and one draw needn't show every extreme that they name: `edge_offsets`: the offsets within one slot are distinct.
All inputs are finite; a program needn't handle non-finite values.
Results may differ from the reference program's by a relative error of at most 0.013.
The reference program's roundings to bfloat16 on the way count: a program that leaves them out, or rounds other values in their place, can miss the bound.
Values may be sent and summed in bfloat16 or wider, within the bound.
A program may use at most 128 MiB of HBM per device.

```python
import math
import jax
import jax.numpy as jnp
from jax import lax

F = 128
NODE_DEV = 512
NBT = 512
E_BLK = 128
NODES = 131072
N_ROW = 8
N_COL = 32


def draw_block_count(key, part):
    levels = jnp.array([1, 2, 4, 8], dtype=jnp.int32)
    picks = jax.random.randint(jax.random.fold_in(key, 11), (N_ROW * N_COL,), 0, 4)
    fullest = jax.random.randint(jax.random.fold_in(key, 12), (), 0, N_ROW * N_COL)
    picks = jnp.where(jnp.arange(N_ROW * N_COL) == fullest, 0, picks)
    return (NBT // levels[picks]).reshape(N_ROW, N_COL).astype(jnp.int32)


def draw_edge_offsets(key, part):
    shape = (N_ROW, N_COL, NBT, E_BLK)
    stride = 16384 // E_BLK
    jitter = jax.random.randint(jax.random.fold_in(key, 21), shape, 0, stride)
    base = jnp.arange(E_BLK, dtype=jnp.int32) * stride + jitter
    factor = 2 * jax.random.randint(jax.random.fold_in(key, 22), (N_ROW, N_COL, NBT, 1), 0, 8192) + 1
    offset = jax.random.randint(jax.random.fold_in(key, 23), (N_ROW, N_COL, NBT, 1), 0, 16384)
    return ((factor * base + offset) % 16384).astype(jnp.int32)


def plant(result, own_key, smallest, top_value):
    longest = result.shape.index(max(result.shape))
    spots = []
    for shift in (0, 1):
        where = [jax.random.randint(jax.random.fold_in(own_key, axis), (), 0, length) for axis, length in enumerate(result.shape)]
        where[longest] = (where[longest] + shift) % result.shape[longest]
        spots.append(tuple(where))
    return result.at[spots[0]].set(smallest).at[spots[1]].set(top_value)


def steps_of(own_key, shape, cuts, least, largest):
    level = 1.0
    for dim, parts in cuts:
        steps = jax.random.uniform(jax.random.fold_in(jax.random.fold_in(own_key, 6), dim), (parts,), jnp.float32, least / len(cuts), largest / len(cuts))
        level = level * jnp.repeat(jnp.exp(steps), shape[dim] // parts).reshape((-1,) + (1,) * (len(shape) - 1 - dim))
    return level


def bell_draw(stream_key, shape, width, limit, pieces=(), held_as=jnp.bfloat16):
    loudness = steps_of(stream_key, shape, pieces, -0.22, 0.18) if pieces else 1.0
    entries = jax.random.normal(stream_key, shape, jnp.float32) * width * loudness
    return jnp.minimum(jnp.maximum(entries, -limit), limit).astype(held_as)


def setup_inputs(seed: int = 0) -> dict:
    keys = jax.random.split(jax.random.key(seed), 10)
    features = bell_draw(keys[0], (NODES, F), 1.0, 6.0, ((0, 256),))
    weight = bell_draw(keys[1], (F, F), F ** -0.5, 0.5)
    bias = bell_draw(keys[2], (F,), 0.5, 3.0, (), jnp.float32)
    cotangent = bell_draw(keys[3], (NODES, F), 1.0, 6.0, ((0, 256),))
    block_count = draw_block_count(jax.random.fold_in(keys[9], 71), 0)
    block_rows = plant(jax.random.randint(keys[5], (N_ROW, N_COL, NBT), 0, NODE_DEV * N_COL // 128), jax.random.fold_in(keys[5], 1), 0, (NODE_DEV * N_COL // 128) - 1).astype(jnp.int32)
    block_cols = plant(jax.random.randint(keys[6], (N_ROW, N_COL, NBT), 0, NODE_DEV * N_ROW // 128), jax.random.fold_in(keys[6], 1), 0, (NODE_DEV * N_ROW // 128) - 1).astype(jnp.int32)
    edge_offsets = draw_edge_offsets(jax.random.fold_in(keys[9], 71), 0)
    edge_weight = jnp.clip(jnp.exp(math.log(0.099609375) - 2.3038113 * jax.random.uniform(keys[8], (N_ROW, N_COL, NBT, E_BLK), jnp.float32) ** steps_of(keys[8], (N_ROW, N_COL, NBT, E_BLK), ((0, 8), (1, 32)), -0.2, 0.2)), 0.0099487305, 0.099609375).astype(jnp.bfloat16)
    return {"features": features, "weight": weight, "bias": bias, "cotangent": cotangent, "block_count": block_count, "block_rows": block_rows, "block_cols": block_cols, "edge_offsets": edge_offsets, "edge_weight": edge_weight}


def tile_edges(t, block_count, block_rows, block_cols, edge_offsets, edge_weight):
    r = t // N_COL
    c = t % N_COL
    count = block_count.reshape(-1)[t]
    brow = block_rows.reshape(-1, NBT)[t]
    bcol = block_cols.reshape(-1, NBT)[t]
    offs = edge_offsets.reshape(-1, NBT, E_BLK)[t]
    vals = edge_weight.reshape(-1, NBT, E_BLK)[t].astype(jnp.float32)
    live = jnp.arange(NBT, dtype=jnp.int32) < count
    vals = jnp.where(live[:, None], vals, jnp.zeros_like(vals))
    lrow = brow[:, None] * 128 + offs // 128
    lcol = bcol[:, None] * 128 + offs % 128
    grow = r * (NODE_DEV * N_COL) + lrow
    gcol = ((lcol // NODE_DEV) * N_COL + c) * NODE_DEV + lcol % NODE_DEV
    return grow.reshape(-1).astype(jnp.int32), gcol.reshape(-1).astype(jnp.int32), vals.reshape(-1)


def reference(features, weight, bias, cotangent, block_count, block_rows, block_cols, edge_offsets, edge_weight):
    tiles = jnp.arange(N_ROW * N_COL, dtype=jnp.int32)
    projected = jnp.dot(features, weight, preferred_element_type=jnp.float32).astype(jnp.bfloat16).astype(jnp.float32)

    def forward_step(total, t):
        rows, cols, vals = tile_edges(t, block_count, block_rows, block_cols, edge_offsets, edge_weight)
        return total.at[rows].add(vals[:, None] * projected[cols]), None

    aggregated, _ = lax.scan(forward_step, jnp.zeros((NODES, F), jnp.float32), tiles)
    pre = aggregated + bias
    output = jnp.maximum(pre, 0.0).astype(jnp.bfloat16)
    grad_pre = jnp.where(pre > 0, cotangent.astype(jnp.float32), 0.0).astype(jnp.bfloat16)
    grad_pre_f = grad_pre.astype(jnp.float32)

    def backward_step(total, t):
        rows, cols, vals = tile_edges(t, block_count, block_rows, block_cols, edge_offsets, edge_weight)
        return total.at[cols].add(vals[:, None] * grad_pre_f[rows]), None

    grad_proj, _ = lax.scan(backward_step, jnp.zeros((NODES, F), jnp.float32), tiles)
    grad_proj = grad_proj.astype(jnp.bfloat16)
    grad_features = jnp.dot(grad_proj, weight.T, preferred_element_type=jnp.float32).astype(jnp.bfloat16)
    scale = NODES ** -0.5
    grad_weight = jnp.dot(features.T, grad_proj, preferred_element_type=jnp.float32) * scale
    grad_bias = jnp.sum(grad_pre_f, axis=0) * scale
    return output, grad_features, grad_weight, grad_bias
```

```python
import functools

import jax
import jax.numpy as jnp
from jax import lax
from jax.experimental import pallas as pl
from jax.experimental.pallas import tpu as pltpu
from jax.sharding import PartitionSpec as P

MESH = pl.DeviceIdType.MESH
F32 = jnp.float32
BF16 = jnp.bfloat16
BATCH = 16
PIECE = 24


def place():
    r = lax.axis_index("row")
    c = lax.axis_index("col")
    return lax.div(c, 8), lax.rem(lax.div(c, 4), 2), lax.rem(c, 4), lax.div(r, 2), lax.rem(r, 2)


def shifted(here, dx=0, dz=0, dy=0, dh=0, dk=0):
    x, z, y, h, k = here
    x, z, y = lax.rem(x + dx, 4), lax.rem(z + dz, 2), lax.rem(y + dy, 4)
    h, k = lax.rem(h + dh, 4), lax.rem(k + dk, 2)
    return (h * 2 + k, x * 8 + z * 4 + y)


def densify_kernel(count_ref, off_ref, w_ref, d_ref):
    start = pl.program_id(0) * BATCH
    off = off_ref[...]
    hi = lax.shift_right_logical(off, 7).astype(F32)
    lo = lax.bitwise_and(off, 127).astype(F32)
    slot = start + lax.broadcasted_iota(jnp.int32, off.shape, 0)
    w = jnp.where(slot < count_ref[0], w_ref[...].astype(F32), 0.0)
    ids = (
        lax.broadcasted_iota(jnp.int32, (8, 16, 128), 0) * 16
        + lax.broadcasted_iota(jnp.int32, (8, 16, 128), 1)
    ).astype(F32).astype(BF16)
    one = jnp.ones((8, 16, 128), BF16)
    zero = jnp.zeros((8, 16, 128), BF16)

    def row(a, s):
        return jnp.broadcast_to(a[s : s + 1], (16, 128)).astype(BF16)[None]

    for s in range(BATCH):
        left = jnp.where(ids == row(hi, s), jnp.broadcast_to(row(w, s), (8, 16, 128)), zero)
        right = jnp.where(ids == row(lo, s), one, zero)
        d_ref[s] = lax.dot_general(
            right.reshape(128, 128),
            left.reshape(128, 128),
            (((1,), (1,)), ((), ())),
            preferred_element_type=F32,
        ).astype(BF16)


def densify(count, offsets, weights):
    slots = offsets.shape[0]
    return pl.pallas_call(
        densify_kernel,
        grid_spec=pltpu.PrefetchScalarGridSpec(
            num_scalar_prefetch=1,
            grid=(slots // BATCH,),
            in_specs=[
                pl.BlockSpec((BATCH, 128), lambda i, n: (i, 0)),
                pl.BlockSpec((BATCH, 128), lambda i, n: (i, 0)),
            ],
            out_specs=pl.BlockSpec((BATCH, 128, 128), lambda i, n: (i, 0, 0)),
        ),
        out_shape=jax.ShapeDtypeStruct((slots, 128, 128), BF16),
        compiler_params=pltpu.CompilerParams(vmem_limit_bytes=16 << 20),
        cost_estimate=pl.CostEstimate(
            flops=slots * 128**3 * 2 * 8, bytes_accessed=slots * 128 * 262, transcendentals=0
        ),
        name="densify",
    )(count, offsets, weights)


def forward_kernel(count_ref, row_ref, col_ref, d_ref, x_ref, t_ref):
    step = pl.program_id(0)

    @pl.when(step == 0)
    def _():
        t_ref[...] = jnp.zeros_like(t_ref)

    @pl.when(step * BATCH < count_ref[0])
    def _():
        for s in range(BATCH):
            r = row_ref[step * BATCH + s]
            c = col_ref[step * BATCH + s]
            t_ref[r] += jnp.dot(x_ref[c], d_ref[s], preferred_element_type=F32)


def backward_kernel(count_ref, row_ref, col_ref, d_ref, y_ref, t_ref):
    step = pl.program_id(0)

    @pl.when(step == 0)
    def _():
        t_ref[...] = jnp.zeros_like(t_ref)

    @pl.when(step * BATCH < count_ref[0])
    def _():
        for s in range(BATCH):
            r = row_ref[step * BATCH + s]
            c = col_ref[step * BATCH + s]
            t_ref[c] += jnp.dot(d_ref[s], y_ref[r], preferred_element_type=F32)


def block_sums(kernel, name, count, brow, bcol, dense, panel, blocks):
    slots = dense.shape[0]
    return pl.pallas_call(
        kernel,
        grid_spec=pltpu.PrefetchScalarGridSpec(
            num_scalar_prefetch=3,
            grid=(slots // BATCH,),
            in_specs=[
                pl.BlockSpec((BATCH, 128, 128), lambda i, *_: (i, 0, 0)),
                pl.BlockSpec(memory_space=pltpu.VMEM),
            ],
            out_specs=pl.BlockSpec(memory_space=pltpu.VMEM),
        ),
        out_shape=jax.ShapeDtypeStruct((blocks, 128, 128), F32),
        compiler_params=pltpu.CompilerParams(vmem_limit_bytes=24 << 20),
        cost_estimate=pl.CostEstimate(
            flops=slots * 128**3 * 2, bytes_accessed=slots * 128 * 256, transcendentals=0
        ),
        name=name,
    )(count, brow, bcol, dense, panel)


class Copies:
    def __init__(self, send, recv):
        self.send, self.recv, self.used = send, recv, 0

    def start(self, src, dst, device):
        copy = pltpu.make_async_remote_copy(
            src_ref=src,
            dst_ref=dst,
            send_sem=self.send.at[self.used],
            recv_sem=self.recv.at[self.used],
            device_id=device,
            device_id_type=MESH,
        )
        self.used += 1
        copy.start()
        return copy


def ring_sum(copies, pick, me, plus, minus, near, far, total):
    p1, p2, p3 = lax.rem(me + 1, 4), lax.rem(me + 2, 4), lax.rem(me + 3, 4)
    first = [
        copies.start(pick(p2, 0), near.at[0], plus),
        copies.start(pick(p2, 1), near.at[1], minus),
        copies.start(pick(p1, 1), far.at[0, 1], plus),
        copies.start(pick(p3, 0), far.at[1, 0], minus),
    ]

    def middle():
        first[0].wait_recv()
        add_into(near.at[0], pick(p1, 0))
        second = [copies.start(near.at[0], far.at[0, 0], plus)]
        first[1].wait_recv()
        add_into(near.at[1], pick(p3, 1))
        second.append(copies.start(near.at[1], far.at[1, 1], minus))
        return second

    def last(second):
        for half, one, two in ((1, first[2], second[1]), (0, first[3], second[0])):
            one.wait_recv()
            two.wait_recv()
            own, out = pick(me, half), total.at[half]
            for i in range(leading(own)):
                at = part(own, i)
                out[at] = own[at] + far.at[0, half][at] + far.at[1, half][at]
        for copy in first + second:
            copy.wait_send()

    return middle, last


def leading(ref):
    return ref.shape[0] if len(ref.shape) == 3 else 1


def part(ref, i):
    return (i,) if len(ref.shape) == 3 else (Ellipsis,)


def add_into(out, other):
    for i in range(leading(out)):
        at = part(out, i)
        out[at] = out[at] + other[at]


def reduce_gather_kernel(
    t_ref, bias_ref, cot_ref, out_ref, g_ref, bsum_ref,
    near_a, far_a, sum_a, near_b, far_b, sum_b,
    near_c, far_c, sum_c, near_d, far_d, sum_d, pair, send, recv,
):
    here = place()
    x, z, y, h, k = here
    xp, xm = shifted(here, dx=1), shifted(here, dx=3)
    yp, ym = shifted(here, dy=1), shifted(here, dy=3)
    zp = shifted(here, dz=1)
    barrier = pltpu.get_barrier_semaphore()
    for peer in (xp, xm, yp, ym, zp):
        pl.semaphore_signal(barrier, inc=1, device_id=peer, device_id_type=MESH)
    pl.semaphore_wait(barrier, 5)
    copies = Copies(send, recv)

    mid_a, end_a = ring_sum(
        copies, lambda p, q: t_ref.at[p, q, :, 0:256, :], x, xp, xm, near_a, far_a, sum_a
    )
    mid_b, end_b = ring_sum(
        copies, lambda p, q: t_ref.at[:, q, p, 256:512, :], y, yp, ym, near_b, far_b, sum_b
    )
    second_a, second_b = mid_a(), mid_b()
    end_a(second_a)
    mid_c, end_c = ring_sum(copies, lambda p, q: sum_a.at[q, p], y, yp, ym, near_c, far_c, sum_c)
    end_b(second_b)
    mid_d, end_d = ring_sum(copies, lambda p, q: sum_b.at[q, p], x, xp, xm, near_d, far_d, sum_d)
    second_c, second_d = mid_c(), mid_d()
    other = 1 - z
    end_c(second_c)
    pair_c = copies.start(sum_c.at[other], pair.at[0], zp)
    end_d(second_d)
    pair_d = copies.start(sum_d.at[other], pair.at[1], zp)
    bias = bias_ref[...]
    lost = jnp.zeros((1, 128), F32)
    for i, (copy, total) in enumerate(((pair_c, sum_c), (pair_d, sum_d))):
        copy.wait()
        own = total[z] + pair[i]
        for b in range(2):
            pre = own[b * 128 : (b + 1) * 128].T + bias
            rows = slice((2 * i + b) * 128, (2 * i + b + 1) * 128)
            out_ref[rows] = jnp.maximum(pre, 0.0).astype(BF16)
            grad = jnp.where(pre > 0, cot_ref[rows].astype(F32), 0.0)
            lost = lost + jnp.sum(grad, axis=0, keepdims=True)
            g_ref[x, z, y, rows] = grad.astype(BF16)
    bsum_ref[...] = lost

    copies.start(g_ref.at[x, z, y], g_ref.at[x, z, y], zp).wait()
    top, low = pl.ds(0, 256), pl.ds(256, 256)
    x1, x3 = lax.rem(x + 1, 4), lax.rem(x + 3, 4)
    y1, y3 = lax.rem(y + 1, 4), lax.rem(y + 3, 4)

    def ring_gather(mine, before, after, plus, minus):
        sent = [copies.start(mine, mine, plus), copies.start(mine, mine, minus)]

        def middle():
            sent[0].wait_recv()
            sent.append(copies.start(before, before, plus))
            sent[1].wait_recv()
            sent.append(copies.start(after, after, minus))

        def last():
            sent[2].wait_recv()
            sent[3].wait_recv()
            for copy in sent:
                copy.wait_send()

        return middle, last

    mid_a, end_a = ring_gather(
        g_ref.at[x, :, y, top], g_ref.at[x, 0, y3, top], g_ref.at[x, 1, y1, top], yp, ym
    )
    mid_b, end_b = ring_gather(
        g_ref.at[x, :, y, low], g_ref.at[x3, 0, y, low], g_ref.at[x1, 1, y, low], xp, xm
    )
    mid_a()
    mid_b()
    end_a()
    mid_c, end_c = ring_gather(
        g_ref.at[x, :, :, top], g_ref.at[x3, 0, :, top], g_ref.at[x1, 1, :, top], xp, xm
    )
    end_b()
    mid_d, end_d = ring_gather(
        g_ref.at[:, :, y, low], g_ref.at[:, 0, y3, low], g_ref.at[:, 1, y1, low], yp, ym
    )
    mid_c()
    mid_d()
    end_c()
    end_d()


def reduce_gather(totals, bias, cotangent):
    vmem = pl.BlockSpec(memory_space=pltpu.VMEM)

    def ring(half):
        return [pltpu.VMEM((2,) + half, F32), pltpu.VMEM((2, 2) + half, F32), pltpu.VMEM((2,) + half, F32)]

    return pl.pallas_call(
        reduce_gather_kernel,
        out_shape=(
            jax.ShapeDtypeStruct((512, 128), BF16),
            jax.ShapeDtypeStruct((4, 2, 4, 512, 128), BF16),
            jax.ShapeDtypeStruct((1, 128), F32),
        ),
        in_specs=[vmem] * 3,
        out_specs=(vmem,) * 3,
        scratch_shapes=ring((4, 256, 128)) * 2
        + ring((256, 128)) * 2
        + [
            pltpu.VMEM((2, 256, 128), F32),
            pltpu.SemaphoreType.DMA((48,)),
            pltpu.SemaphoreType.DMA((48,)),
        ],
        compiler_params=pltpu.CompilerParams(
            collective_id=0, has_side_effects=True, vmem_limit_bytes=48 << 20
        ),
        name="reduce_gather",
    )(totals, bias, cotangent)


def finish_kernel(
    t_ref, feat_ref, weight_ref, bsum_ref, gf_ref, gw_ref,
    from_core, outgoing, from_chip, local, row_parts, total, col_parts, whole, send, recv,
):
    here = place()
    x, z, y, h, k = here
    r, c = lax.axis_index("row"), lax.axis_index("col")
    row_shifts = [(dh, dk) for dh in range(4) for dk in range(2) if (dh, dk) != (0, 0)]
    col_shifts = [
        (dx, dz, dy) for dx in range(4) for dz in range(2) for dy in range(4) if (dx, dz, dy) != (0, 0, 0)
    ]
    row_peers = [shifted(here, dh=dh, dk=dk) for dh, dk in row_shifts]
    col_peers = [shifted(here, dx=dx, dz=dz, dy=dy) for dx, dz, dy in col_shifts]
    barrier = pltpu.get_barrier_semaphore()
    for peer in row_peers + col_peers:
        pl.semaphore_signal(barrier, inc=1, device_id=peer, device_id_type=MESH)
    pl.semaphore_wait(barrier, len(row_peers) + len(col_peers))
    copies = Copies(send, recv)

    other = 1 - k
    partner = shifted(here, dk=1)
    pairs = []
    for dh in (2, 1, 3, 0):
        to = lax.rem(h + dh, 4)
        pairs.append((dh, to, copies.start(t_ref.at[to, other], from_core.at[to], partner)))
    chips = []
    for dh, to, copy in pairs[:3]:
        copy.wait_recv()
        outgoing[dh - 1] = (t_ref[to, k] + from_core[to]).astype(BF16)
        chips.append(copies.start(outgoing.at[dh - 1], from_chip.at[dh - 1], shifted(here, dh=dh)))
    pairs[3][2].wait_recv()
    own = t_ref[h, k] + from_core[h]
    for copy in chips:
        copy.wait_recv()
    for i in range(3):
        own = own + from_chip[i].astype(F32)
    grad = own.astype(BF16)
    local[0:128] = lax.dot_general(
        feat_ref[...], grad, (((0,), (0,)), ((), ())), preferred_element_type=F32
    )
    local[128:136] = jnp.concatenate([bsum_ref[...], jnp.zeros((7, 128), F32)], axis=0)
    local[136:192] = jnp.zeros((56, 128), F32)

    def piece(i):
        return local.at[pl.ds(pl.multiple_of(i * PIECE, 8), PIECE)]

    sent = [copies.start(piece(p[0]), row_parts.at[r], p) for p in row_peers]
    gf_ref[...] = lax.dot_general(
        grad, weight_ref[...], (((1,), (1,)), ((), ())), preferred_element_type=F32
    ).astype(BF16)
    row_parts[r] = piece(r)[...]
    for copy in sent:
        copy.wait_recv()
    acc = row_parts[0]
    for i in range(1, 8):
        acc = acc + row_parts[i]
    total[...] = acc
    col_parts[c] = acc
    spread = [copies.start(total, col_parts.at[c], p) for p in col_peers]
    for copy in spread:
        copy.wait_recv()
    acc = col_parts[0]
    for i in range(1, 32):
        acc = acc + col_parts[i]
    whole[r] = acc
    back = [copies.start(whole.at[r], whole.at[r], p) for p in row_peers]
    for copy in back:
        copy.wait_recv()
    for i in range(8):
        gw_ref[i] = whole[i] * (131072.0**-0.5)
    for copy in [p[2] for p in pairs] + chips + sent + spread + back:
        copy.wait_send()


def finish(partial, features, weight, bias_sum):
    vmem = pl.BlockSpec(memory_space=pltpu.VMEM)
    return pl.pallas_call(
        finish_kernel,
        out_shape=(
            jax.ShapeDtypeStruct((512, 128), BF16),
            jax.ShapeDtypeStruct((8, PIECE, 128), F32),
        ),
        in_specs=[vmem] * 4,
        out_specs=(vmem,) * 2,
        scratch_shapes=[
            pltpu.VMEM((4, 512, 128), F32),
            pltpu.VMEM((3, 512, 128), BF16),
            pltpu.VMEM((3, 512, 128), BF16),
            pltpu.VMEM((8 * PIECE, 128), F32),
            pltpu.VMEM((8, PIECE, 128), F32),
            pltpu.VMEM((PIECE, 128), F32),
            pltpu.VMEM((32, PIECE, 128), F32),
            pltpu.VMEM((8, PIECE, 128), F32),
            pltpu.SemaphoreType.DMA((56,)),
            pltpu.SemaphoreType.DMA((56,)),
        ],
        compiler_params=pltpu.CompilerParams(
            collective_id=1, has_side_effects=True, vmem_limit_bytes=32 << 20
        ),
        name="finish",
    )(partial, features, weight, bias_sum)


def shards(
    features, weight, bias, cotangent, block_count, block_rows, block_cols, edge_offsets, edge_weight
):
    count = block_count.reshape(1)
    brow, bcol = block_rows[0, 0], block_cols[0, 0]
    projected = lax.dot_general(
        weight, features.reshape(4, 128, 128), (((0,), (2,)), ((), ())), preferred_element_type=F32
    )
    projected = projected.transpose(1, 0, 2).astype(BF16)
    panel = lax.all_gather(projected, "row", axis=0, tiled=True)
    dense = densify(count, edge_offsets[0, 0], edge_weight[0, 0])
    totals = block_sums(forward_kernel, "forward", count, brow, bcol, dense, panel, 128)
    output, grads, bias_sum = reduce_gather(
        totals.reshape(4, 2, 4, 512, 128), bias.reshape(1, 128), cotangent
    )
    partial = block_sums(
        backward_kernel, "backward", count, brow, bcol, dense, grads.reshape(128, 128, 128), 32
    )
    grad_features, sums = finish(partial.reshape(4, 2, 512, 128), features, weight, bias_sum)
    sums = sums.reshape(8 * PIECE, 128)
    return (output, grad_features, sums[:128], sums[128])


def solution(mesh):
    return jax.shard_map(
        shards,
        mesh=mesh,
        in_specs=(
            P(("row", "col"), None),
            P(),
            P(),
            P(("row", "col"), None),
            P("row", "col"),
            P("row", "col", None),
            P("row", "col", None),
            P("row", "col", None, None),
            P("row", "col", None, None),
        ),
        out_specs=(P(("row", "col"), None), P(("row", "col"), None), P(), P()),
        check_vma=False,
    )
```

```python
import functools

import jax
import jax.numpy as jnp
from jax import lax
from jax.experimental import pallas as pl
from jax.experimental.pallas import tpu as pltpu
from jax.sharding import PartitionSpec as P

MESH = pl.DeviceIdType.MESH
F32 = jnp.float32
BF16 = jnp.bfloat16
BATCH = 16
PIECE = 24
PREP_VMEM = 4 << 20
SUMS_VMEM = 4 << 20
REDUCE_VMEM = 16 << 20
FINISH_VMEM = 12 << 20


def place():
    r = lax.axis_index("row")
    c = lax.axis_index("col")
    return lax.div(c, 8), lax.rem(lax.div(c, 4), 2), lax.rem(c, 4), lax.div(r, 2), lax.rem(r, 2)


def shifted(here, dx=0, dz=0, dy=0, dh=0, dk=0):
    x, z, y, h, k = here
    x, z, y = lax.rem(x + dx, 4), lax.rem(z + dz, 2), lax.rem(y + dy, 4)
    h, k = lax.rem(h + dh, 4), lax.rem(k + dk, 2)
    return (h * 2 + k, x * 8 + z * 4 + y)


class Copies:
    def __init__(self, send, recv):
        self.send, self.recv, self.used = send, recv, 0

    def start(self, src, dst, device):
        copy = pltpu.make_async_remote_copy(
            src_ref=src,
            dst_ref=dst,
            send_sem=self.send.at[self.used],
            recv_sem=self.recv.at[self.used],
            device_id=device,
            device_id_type=MESH,
        )
        self.used += 1
        copy.start()
        return copy


def prepare_kernel(count_ref, off_ref, w_ref, feat_ref, weight_ref, d_ref, panel_ref, send, recv):
    here = place()
    x, z, y, h, k = here
    r = lax.axis_index("row")
    partner = shifted(here, dk=1)
    chips = [shifted(here, dh=dh) for dh in (2, 1, 3)]
    barrier = pltpu.get_barrier_semaphore()
    for peer in [partner] + chips:
        pl.semaphore_signal(barrier, inc=1, device_id=peer, device_id_type=MESH)
    for b in range(4):
        rows = slice(b * 128, (b + 1) * 128)
        projected = jnp.dot(feat_ref[rows], weight_ref[...], preferred_element_type=F32)
        panel_ref[r, b] = projected.T.astype(BF16)
    pl.semaphore_wait(barrier, 4)
    copies = Copies(send, recv)
    away = [copies.start(panel_ref.at[r], panel_ref.at[r], p) for p in chips]
    beside = [copies.start(panel_ref.at[r], panel_ref.at[r], partner)]

    count = count_ref[0, 0]
    ids = (
        lax.broadcasted_iota(jnp.int32, (8, 16, 128), 0) * 16
        + lax.broadcasted_iota(jnp.int32, (8, 16, 128), 1)
    ).astype(F32).astype(BF16)
    one = jnp.ones((8, 16, 128), BF16)
    zero = jnp.zeros((8, 16, 128), BF16)

    def row(a, s):
        return jnp.broadcast_to(a[s : s + 1], (16, 128)).astype(BF16)[None]

    def densify(step, carry):
        start = pl.multiple_of(step * BATCH, BATCH)
        off = off_ref[pl.ds(start, BATCH)]
        hi = lax.shift_right_logical(off, 7).astype(F32)
        lo = lax.bitwise_and(off, 127).astype(F32)
        slot = start + lax.broadcasted_iota(jnp.int32, off.shape, 0)
        w = jnp.where(slot < count, w_ref[pl.ds(start, BATCH)].astype(F32), 0.0)
        for s in range(BATCH):
            left = jnp.where(ids == row(hi, s), jnp.broadcast_to(row(w, s), (8, 16, 128)), zero)
            right = jnp.where(ids == row(lo, s), one, zero)
            d_ref[start + s] = lax.dot_general(
                right.reshape(128, 128),
                left.reshape(128, 128),
                (((1,), (1,)), ((), ())),
                preferred_element_type=F32,
            ).astype(BF16)
        return carry

    steps = d_ref.shape[0] // BATCH
    lax.fori_loop(0, steps * 3 // 4, densify, 0)
    for dh, copy in zip((2, 1, 3), away):
        copy.wait_recv()
        got = panel_ref.at[lax.rem(h - dh + 4, 4) * 2 + k]
        beside.append(copies.start(got, got, partner))
    lax.fori_loop(steps * 3 // 4, steps, densify, 0)
    for copy in beside:
        copy.wait_recv()
    for copy in away + beside:
        copy.wait_send()


def prepare(count, offsets, weights, features, weight):
    slots = offsets.shape[0]
    vmem = pl.BlockSpec(memory_space=pltpu.VMEM)
    return pl.pallas_call(
        prepare_kernel,
        out_shape=(
            jax.ShapeDtypeStruct((slots, 128, 128), BF16),
            jax.ShapeDtypeStruct((8, 4, 128, 128), BF16),
        ),
        in_specs=[pl.BlockSpec(memory_space=pltpu.SMEM)] + [vmem] * 4,
        out_specs=(vmem,) * 2,
        scratch_shapes=[pltpu.SemaphoreType.DMA((7,)), pltpu.SemaphoreType.DMA((7,))],
        compiler_params=pltpu.CompilerParams(
            collective_id=2, has_side_effects=True, vmem_limit_bytes=PREP_VMEM
        ),
        name="prepare",
    )(count, offsets, weights, features, weight)


def forward_kernel(count_ref, row_ref, col_ref, d_ref, x_ref, t_ref):
    t_ref[...] = jnp.zeros_like(t_ref)

    def step(i, carry):
        for s in range(BATCH):
            n = i * BATCH + s
            r, c = row_ref[n], col_ref[n]
            t_ref[r] += jnp.dot(x_ref[c], d_ref[n], preferred_element_type=F32)
        return carry

    lax.fori_loop(0, lax.div(count_ref[0, 0] + (BATCH - 1), BATCH), step, 0)


def backward_kernel(count_ref, row_ref, col_ref, d_ref, y_ref, t_ref):
    t_ref[...] = jnp.zeros_like(t_ref)

    def step(i, carry):
        for s in range(BATCH):
            n = i * BATCH + s
            r, c = row_ref[n], col_ref[n]
            t_ref[c] += jnp.dot(d_ref[n], y_ref[r], preferred_element_type=F32)
        return carry

    lax.fori_loop(0, lax.div(count_ref[0, 0] + (BATCH - 1), BATCH), step, 0)


def block_sums(kernel, name, count, brow, bcol, dense, panel, blocks):
    slots = dense.shape[0]
    smem, vmem = pl.BlockSpec(memory_space=pltpu.SMEM), pl.BlockSpec(memory_space=pltpu.VMEM)
    return pl.pallas_call(
        kernel,
        in_specs=[smem] * 3 + [vmem] * 2,
        out_specs=vmem,
        out_shape=jax.ShapeDtypeStruct((blocks, 128, 128), F32),
        compiler_params=pltpu.CompilerParams(vmem_limit_bytes=SUMS_VMEM),
        name=name,
    )(count, brow, bcol, dense, panel)


def ring_sum(copies, pick, me, plus, minus, near, far, total):
    p1, p2, p3 = lax.rem(me + 1, 4), lax.rem(me + 2, 4), lax.rem(me + 3, 4)
    first = [
        copies.start(pick(p2, 0), near.at[0], plus),
        copies.start(pick(p2, 1), near.at[1], minus),
        copies.start(pick(p1, 1), far.at[0, 1], plus),
        copies.start(pick(p3, 0), far.at[1, 0], minus),
    ]

    def middle():
        first[0].wait_recv()
        add_into(near.at[0], pick(p1, 0))
        second = [copies.start(near.at[0], far.at[0, 0], plus)]
        first[1].wait_recv()
        add_into(near.at[1], pick(p3, 1))
        second.append(copies.start(near.at[1], far.at[1, 1], minus))
        return second

    def last(second):
        for half, one, two in ((1, first[2], second[1]), (0, first[3], second[0])):
            one.wait_recv()
            two.wait_recv()
            own, out = pick(me, half), total.at[half]
            for i in range(leading(own)):
                at = part(own, i)
                out[at] = own[at] + far.at[0, half][at] + far.at[1, half][at]
        for copy in first + second:
            copy.wait_send()

    return middle, last


def leading(ref):
    return ref.shape[0] if len(ref.shape) == 3 else 1


def part(ref, i):
    return (i,) if len(ref.shape) == 3 else (Ellipsis,)


def add_into(out, other):
    for i in range(leading(out)):
        at = part(out, i)
        out[at] = out[at] + other[at]


def reduce_gather_kernel(
    t_ref, bias_ref, cot_ref, out_ref, g_ref, bsum_ref,
    near_a, far_a, sum_a, near_b, far_b, sum_b,
    near_c, far_c, sum_c, near_d, far_d, sum_d, pair, send, recv,
):
    here = place()
    x, z, y, h, k = here
    xp, xm = shifted(here, dx=1), shifted(here, dx=3)
    yp, ym = shifted(here, dy=1), shifted(here, dy=3)
    zp = shifted(here, dz=1)
    barrier = pltpu.get_barrier_semaphore()
    for peer in (xp, xm, yp, ym, zp):
        pl.semaphore_signal(barrier, inc=1, device_id=peer, device_id_type=MESH)
    pl.semaphore_wait(barrier, 5)
    copies = Copies(send, recv)

    mid_a, end_a = ring_sum(
        copies, lambda p, q: t_ref.at[p, q, :, 0:256, :], x, xp, xm, near_a, far_a, sum_a
    )
    mid_b, end_b = ring_sum(
        copies, lambda p, q: t_ref.at[:, q, p, 256:512, :], y, yp, ym, near_b, far_b, sum_b
    )
    second_a, second_b = mid_a(), mid_b()
    end_a(second_a)
    mid_c, end_c = ring_sum(copies, lambda p, q: sum_a.at[q, p], y, yp, ym, near_c, far_c, sum_c)
    end_b(second_b)
    mid_d, end_d = ring_sum(copies, lambda p, q: sum_b.at[q, p], x, xp, xm, near_d, far_d, sum_d)
    second_c, second_d = mid_c(), mid_d()
    other = 1 - z
    end_c(second_c)
    pair_c = copies.start(sum_c.at[other], pair.at[0], zp)
    end_d(second_d)
    pair_d = copies.start(sum_d.at[other], pair.at[1], zp)
    bias = bias_ref[...]
    lost = jnp.zeros((1, 128), F32)
    for i, (copy, total) in enumerate(((pair_c, sum_c), (pair_d, sum_d))):
        copy.wait()
        own = total[z] + pair[i]
        for b in range(2):
            pre = own[b * 128 : (b + 1) * 128].T + bias
            rows = slice((2 * i + b) * 128, (2 * i + b + 1) * 128)
            out_ref[rows] = jnp.maximum(pre, 0.0).astype(BF16)
            grad = jnp.where(pre > 0, cot_ref[rows].astype(F32), 0.0)
            lost = lost + jnp.sum(grad, axis=0, keepdims=True)
            g_ref[x, z, y, rows] = grad.astype(BF16)
    bsum_ref[...] = lost

    copies.start(g_ref.at[x, z, y], g_ref.at[x, z, y], zp).wait()
    top, low = pl.ds(0, 256), pl.ds(256, 256)
    x1, x3 = lax.rem(x + 1, 4), lax.rem(x + 3, 4)
    y1, y3 = lax.rem(y + 1, 4), lax.rem(y + 3, 4)

    def ring_gather(mine, before, after, plus, minus):
        sent = [copies.start(mine, mine, plus), copies.start(mine, mine, minus)]

        def middle():
            sent[0].wait_recv()
            sent.append(copies.start(before, before, plus))
            sent[1].wait_recv()
            sent.append(copies.start(after, after, minus))

        def last():
            sent[2].wait_recv()
            sent[3].wait_recv()
            for copy in sent:
                copy.wait_send()

        return middle, last

    mid_a, end_a = ring_gather(
        g_ref.at[x, :, y, top], g_ref.at[x, 0, y3, top], g_ref.at[x, 1, y1, top], yp, ym
    )
    mid_b, end_b = ring_gather(
        g_ref.at[x, :, y, low], g_ref.at[x3, 0, y, low], g_ref.at[x1, 1, y, low], xp, xm
    )
    mid_a()
    mid_b()
    end_a()
    mid_c, end_c = ring_gather(
        g_ref.at[x, :, :, top], g_ref.at[x3, 0, :, top], g_ref.at[x1, 1, :, top], xp, xm
    )
    end_b()
    mid_d, end_d = ring_gather(
        g_ref.at[:, :, y, low], g_ref.at[:, 0, y3, low], g_ref.at[:, 1, y1, low], yp, ym
    )
    mid_c()
    mid_d()
    end_c()
    end_d()


def reduce_gather(totals, bias, cotangent):
    vmem = pl.BlockSpec(memory_space=pltpu.VMEM)

    def ring(half):
        return [pltpu.VMEM((2,) + half, F32), pltpu.VMEM((2, 2) + half, F32), pltpu.VMEM((2,) + half, F32)]

    return pl.pallas_call(
        reduce_gather_kernel,
        out_shape=(
            jax.ShapeDtypeStruct((512, 128), BF16),
            jax.ShapeDtypeStruct((4, 2, 4, 512, 128), BF16),
            jax.ShapeDtypeStruct((1, 128), F32),
        ),
        in_specs=[vmem] * 3,
        out_specs=(vmem,) * 3,
        scratch_shapes=ring((4, 256, 128)) * 2
        + ring((256, 128)) * 2
        + [
            pltpu.VMEM((2, 256, 128), F32),
            pltpu.SemaphoreType.DMA((48,)),
            pltpu.SemaphoreType.DMA((48,)),
        ],
        compiler_params=pltpu.CompilerParams(
            collective_id=0, has_side_effects=True, vmem_limit_bytes=REDUCE_VMEM
        ),
        name="reduce_gather",
    )(totals, bias, cotangent)


def finish_kernel(
    t_ref, feat_ref, weight_ref, bsum_ref, gf_ref, gw_ref, gb_ref,
    from_core, outgoing, from_chip, local, row_parts, total, col_parts, whole, send, recv,
):
    here = place()
    x, z, y, h, k = here
    r, c = lax.axis_index("row"), lax.axis_index("col")
    row_shifts = [(dh, dk) for dh in range(4) for dk in range(2) if (dh, dk) != (0, 0)]
    col_shifts = [
        (dx, dz, dy) for dx in range(4) for dz in range(2) for dy in range(4) if (dx, dz, dy) != (0, 0, 0)
    ]
    row_peers = [shifted(here, dh=dh, dk=dk) for dh, dk in row_shifts]
    col_peers = [shifted(here, dx=dx, dz=dz, dy=dy) for dx, dz, dy in col_shifts]
    barrier = pltpu.get_barrier_semaphore()
    for peer in row_peers + col_peers:
        pl.semaphore_signal(barrier, inc=1, device_id=peer, device_id_type=MESH)
    pl.semaphore_wait(barrier, len(row_peers) + len(col_peers))
    copies = Copies(send, recv)

    other = 1 - k
    partner = shifted(here, dk=1)
    pairs = []
    for dh in (2, 1, 3, 0):
        to = lax.rem(h + dh, 4)
        pairs.append((dh, to, copies.start(t_ref.at[to, other], from_core.at[to], partner)))
    chips = []
    for dh, to, copy in pairs[:3]:
        copy.wait_recv()
        outgoing[dh - 1] = (t_ref[to, k] + from_core[to]).astype(BF16)
        chips.append(copies.start(outgoing.at[dh - 1], from_chip.at[dh - 1], shifted(here, dh=dh)))
    pairs[3][2].wait_recv()
    own = t_ref[h, k] + from_core[h]
    for copy in chips:
        copy.wait_recv()
    for i in range(3):
        own = own + from_chip[i].astype(F32)
    grad = own.astype(BF16)
    local[0:128] = lax.dot_general(
        feat_ref[...], grad, (((0,), (0,)), ((), ())), preferred_element_type=F32
    )
    local[128:136] = jnp.concatenate([bsum_ref[...], jnp.zeros((7, 128), F32)], axis=0)
    local[136:192] = jnp.zeros((56, 128), F32)

    def piece(i):
        return local.at[pl.ds(pl.multiple_of(i * PIECE, 8), PIECE)]

    sent = [copies.start(piece(p[0]), row_parts.at[r], p) for p in row_peers]
    gf_ref[...] = lax.dot_general(
        grad, weight_ref[...], (((1,), (1,)), ((), ())), preferred_element_type=F32
    ).astype(BF16)
    row_parts[r] = piece(r)[...]
    for copy in sent:
        copy.wait_recv()
    acc = row_parts[0]
    for i in range(1, 8):
        acc = acc + row_parts[i]
    total[...] = acc
    col_parts[c] = acc
    spread = [copies.start(total, col_parts.at[c], p) for p in col_peers]
    for copy in spread:
        copy.wait_recv()
    acc = col_parts[0]
    for i in range(1, 32):
        acc = acc + col_parts[i]
    mine = whole.at[pl.ds(pl.multiple_of(r * PIECE, 8), PIECE)]
    mine[...] = acc
    back = [copies.start(mine, mine, p) for p in row_peers]
    for copy in back:
        copy.wait_recv()
    scale = 131072.0**-0.5
    gw_ref[...] = whole[0:128] * scale
    gb_ref[...] = whole[128:129] * scale
    for copy in [p[2] for p in pairs] + chips + sent + spread + back:
        copy.wait_send()


def finish(partial, features, weight, bias_sum):
    vmem = pl.BlockSpec(memory_space=pltpu.VMEM)
    return pl.pallas_call(
        finish_kernel,
        out_shape=(
            jax.ShapeDtypeStruct((512, 128), BF16),
            jax.ShapeDtypeStruct((128, 128), F32),
            jax.ShapeDtypeStruct((1, 128), F32),
        ),
        in_specs=[vmem] * 4,
        out_specs=(vmem,) * 3,
        scratch_shapes=[
            pltpu.VMEM((4, 512, 128), F32),
            pltpu.VMEM((3, 512, 128), BF16),
            pltpu.VMEM((3, 512, 128), BF16),
            pltpu.VMEM((8 * PIECE, 128), F32),
            pltpu.VMEM((8, PIECE, 128), F32),
            pltpu.VMEM((PIECE, 128), F32),
            pltpu.VMEM((32, PIECE, 128), F32),
            pltpu.VMEM((8 * PIECE, 128), F32),
            pltpu.SemaphoreType.DMA((56,)),
            pltpu.SemaphoreType.DMA((56,)),
        ],
        compiler_params=pltpu.CompilerParams(
            collective_id=1, has_side_effects=True, vmem_limit_bytes=FINISH_VMEM
        ),
        name="finish",
    )(partial, features, weight, bias_sum)


def shards(
    features, weight, bias, cotangent, block_count, block_rows, block_cols, edge_offsets, edge_weight
):
    brow, bcol = block_rows[0, 0], block_cols[0, 0]
    dense, panel = prepare(block_count, edge_offsets[0, 0], edge_weight[0, 0], features, weight)
    totals = block_sums(
        forward_kernel, "forward", block_count, brow, bcol, dense, panel.reshape(32, 128, 128), 128
    )
    output, grads, bias_sum = reduce_gather(
        totals.reshape(4, 2, 4, 512, 128), bias.reshape(1, 128), cotangent
    )
    partial = block_sums(
        backward_kernel, "backward", block_count, brow, bcol, dense, grads.reshape(128, 128, 128), 32
    )
    grad_features, grad_weight, grad_bias = finish(
        partial.reshape(4, 2, 512, 128), features, weight, bias_sum
    )
    return (output, grad_features, grad_weight, grad_bias.reshape(128))


def solution(mesh):
    return jax.shard_map(
        shards,
        mesh=mesh,
        in_specs=(
            P(("row", "col"), None),
            P(),
            P(),
            P(("row", "col"), None),
            P("row", "col"),
            P("row", "col", None),
            P("row", "col", None),
            P("row", "col", None, None),
            P("row", "col", None, None),
        ),
        out_specs=(P(("row", "col"), None), P(("row", "col"), None), P(), P()),
        check_vma=False,
    )
```

```python
import functools

import jax
import jax.numpy as jnp
from jax import lax
from jax.experimental import pallas as pl
from jax.experimental.pallas import tpu as pltpu
from jax.sharding import PartitionSpec as P

MESH = pl.DeviceIdType.MESH
F32 = jnp.float32
BF16 = jnp.bfloat16
BATCH = 16
PIECE = 24
PREP_VMEM = 4 << 20
SUMS_VMEM = 4 << 20
REDUCE_VMEM = 16 << 20
FINISH_VMEM = 12 << 20


def place():
    r = lax.axis_index("row")
    c = lax.axis_index("col")
    return lax.div(c, 8), lax.rem(lax.div(c, 4), 2), lax.rem(c, 4), lax.div(r, 2), lax.rem(r, 2)


def shifted(here, dx=0, dz=0, dy=0, dh=0, dk=0):
    x, z, y, h, k = here
    x, z, y = lax.rem(x + dx, 4), lax.rem(z + dz, 2), lax.rem(y + dy, 4)
    h, k = lax.rem(h + dh, 4), lax.rem(k + dk, 2)
    return (h * 2 + k, x * 8 + z * 4 + y)


class Copies:
    def __init__(self, send, recv):
        self.send, self.recv, self.used = send, recv, 0

    def start(self, src, dst, device):
        copy = pltpu.make_async_remote_copy(
            src_ref=src,
            dst_ref=dst,
            send_sem=self.send.at[self.used],
            recv_sem=self.recv.at[self.used],
            device_id=device,
            device_id_type=MESH,
        )
        self.used += 1
        copy.start()
        return copy


def prepare_kernel(count_ref, off_ref, w_ref, feat_ref, weight_ref, d_ref, panel_ref, send, recv):
    here = place()
    x, z, y, h, k = here
    r = lax.axis_index("row")
    partner = shifted(here, dk=1)
    chips = [shifted(here, dh=dh) for dh in (2, 1, 3)]
    barrier = pltpu.get_barrier_semaphore()
    for peer in [partner] + chips:
        pl.semaphore_signal(barrier, inc=1, device_id=peer, device_id_type=MESH)
    for b in range(4):
        rows = slice(b * 128, (b + 1) * 128)
        projected = jnp.dot(feat_ref[rows], weight_ref[...], preferred_element_type=F32)
        panel_ref[r, b] = projected.T.astype(BF16)
    pl.semaphore_wait(barrier, 4)
    copies = Copies(send, recv)
    away = [copies.start(panel_ref.at[r], panel_ref.at[r], p) for p in chips]
    beside = [copies.start(panel_ref.at[r], panel_ref.at[r], partner)]

    count = count_ref[0, 0]
    ids = (
        lax.broadcasted_iota(jnp.int32, (8, 16, 128), 0) * 16
        + lax.broadcasted_iota(jnp.int32, (8, 16, 128), 1)
    ).astype(F32).astype(BF16)
    one = jnp.ones((8, 16, 128), BF16)
    zero = jnp.zeros((8, 16, 128), BF16)

    def row(a, s):
        return jnp.broadcast_to(a[s : s + 1], (16, 128)).astype(BF16)[None]

    def densify(step, carry):
        start = pl.multiple_of(step * BATCH, BATCH)
        off = off_ref[pl.ds(start, BATCH)]
        hi = lax.shift_right_logical(off, 7).astype(F32)
        lo = lax.bitwise_and(off, 127).astype(F32)
        slot = start + lax.broadcasted_iota(jnp.int32, off.shape, 0)
        w = jnp.where(slot < count, w_ref[pl.ds(start, BATCH)].astype(F32), 0.0)
        for s in range(BATCH):
            left = jnp.where(ids == row(hi, s), jnp.broadcast_to(row(w, s), (8, 16, 128)), zero)
            right = jnp.where(ids == row(lo, s), one, zero)
            d_ref[start + s] = lax.dot_general(
                right.reshape(128, 128),
                left.reshape(128, 128),
                (((1,), (1,)), ((), ())),
                preferred_element_type=F32,
            ).astype(BF16)
        return carry

    steps = d_ref.shape[0] // BATCH
    lax.fori_loop(0, steps * 3 // 4, densify, 0)
    for dh, copy in zip((2, 1, 3), away):
        copy.wait_recv()
        got = panel_ref.at[lax.rem(h - dh + 4, 4) * 2 + k]
        beside.append(copies.start(got, got, partner))
    lax.fori_loop(steps * 3 // 4, steps, densify, 0)
    for copy in beside:
        copy.wait_recv()
    for copy in away + beside:
        copy.wait_send()


def prepare(count, offsets, weights, features, weight):
    slots = offsets.shape[0]
    vmem = pl.BlockSpec(memory_space=pltpu.VMEM)
    return pl.pallas_call(
        prepare_kernel,
        out_shape=(
            jax.ShapeDtypeStruct((slots, 128, 128), BF16),
            jax.ShapeDtypeStruct((8, 4, 128, 128), BF16),
        ),
        in_specs=[pl.BlockSpec(memory_space=pltpu.SMEM)] + [vmem] * 4,
        out_specs=(vmem,) * 2,
        scratch_shapes=[pltpu.SemaphoreType.DMA((7,)), pltpu.SemaphoreType.DMA((7,))],
        compiler_params=pltpu.CompilerParams(
            collective_id=2, has_side_effects=True, vmem_limit_bytes=PREP_VMEM
        ),
        name="prepare",
    )(count, offsets, weights, features, weight)


def forward_kernel(count_ref, row_ref, col_ref, d_ref, x_ref, t_ref):
    t_ref[...] = jnp.zeros_like(t_ref)

    def step(i, carry):
        for s in range(BATCH):
            n = i * BATCH + s
            r, c = row_ref[n], col_ref[n]
            t_ref[r] += jnp.dot(x_ref[c], d_ref[n], preferred_element_type=F32)
        return carry

    lax.fori_loop(0, lax.div(count_ref[0, 0] + (BATCH - 1), BATCH), step, 0)


def backward_kernel(count_ref, row_ref, col_ref, d_ref, y_ref, t_ref):
    t_ref[...] = jnp.zeros_like(t_ref)

    def step(i, carry):
        for s in range(BATCH):
            n = i * BATCH + s
            r, c = row_ref[n], col_ref[n]
            t_ref[c] += jnp.dot(d_ref[n], y_ref[r], preferred_element_type=F32)
        return carry

    lax.fori_loop(0, lax.div(count_ref[0, 0] + (BATCH - 1), BATCH), step, 0)


def block_sums(kernel, name, count, brow, bcol, dense, panel, blocks):
    slots = dense.shape[0]
    smem, vmem = pl.BlockSpec(memory_space=pltpu.SMEM), pl.BlockSpec(memory_space=pltpu.VMEM)
    return pl.pallas_call(
        kernel,
        in_specs=[smem] * 3 + [vmem] * 2,
        out_specs=vmem,
        out_shape=jax.ShapeDtypeStruct((blocks, 128, 128), F32),
        compiler_params=pltpu.CompilerParams(vmem_limit_bytes=SUMS_VMEM),
        name=name,
    )(count, brow, bcol, dense, panel)


LEVELS = 32766.0


def blocks_of(ref):
    if len(ref.shape) == 2:
        return [(pl.ds(128 * b, 128),) for b in range(2)]
    return [(i, pl.ds(128 * b, 128)) for i in range(ref.shape[0]) for b in range(2)]


def encode(value, at, n, q_ref, s_ref):
    size = jnp.abs(value)
    most = jnp.maximum(jnp.max(size, axis=0, keepdims=True), 1e-30)
    level = jnp.sqrt(size * (1.0 / most)) * LEVELS + 0.5
    q_ref[at] = jnp.where(value < 0, -level, level).astype(jnp.int32).astype(jnp.int16)
    s_ref[n : n + 1] = most * (1.0 / (LEVELS * LEVELS))


def decode(at, n, q_ref, s_ref):
    level = q_ref[at].astype(jnp.int32).astype(F32)
    return level * jnp.abs(level) * s_ref[n : n + 1]


def ring_sum(copies, pick, me, plus, minus, q, scales, total):
    p1, p2, p3 = lax.rem(me + 1, 4), lax.rem(me + 2, 4), lax.rem(me + 3, 4)

    def send(value, slot, device):
        for n, at in enumerate(blocks_of(q.at[slot])):
            encode(value(n, at), at, n, q.at[slot], scales.at[slot])
        return (
            copies.start(q.at[slot], q.at[slot + 6], device),
            copies.start(scales.at[slot], scales.at[slot + 6], device),
        )

    def got(slot):
        return lambda n, at: decode(at, n, q.at[slot + 6], scales.at[slot + 6])

    def own(p, half):
        return lambda n, at: pick(p, half)[at]

    def plus_got(p, half, slot):
        return lambda n, at: own(p, half)(n, at) + got(slot)(n, at)

    first = [
        send(own(p2, 0), 0, plus),
        send(own(p2, 1), 1, minus),
        send(own(p1, 1), 2, plus),
        send(own(p3, 0), 3, minus),
    ]

    def middle():
        second = []
        for slot, p, half, device in ((0, p1, 0, plus), (1, p3, 1, minus)):
            for copy in first[slot]:
                copy.wait_recv()
            second.append(send(plus_got(p, half, slot), slot + 4, device))
        return second

    def last(second):
        for half, one, two in ((1, 2, 5), (0, 3, 4)):
            for copy in first[one] + second[two - 4]:
                copy.wait_recv()
            out = total.at[half]
            for n, at in enumerate(blocks_of(out)):
                out[at] = own(me, half)(n, at) + got(one)(n, at) + got(two)(n, at)
        for pair in first + second:
            for copy in pair:
                copy.wait_send()

    return middle, last


def reduce_gather_kernel(
    t_ref, bias_ref, cot_ref, out_ref, g_ref, bsum_ref,
    q_a, scale_a, sum_a, q_b, scale_b, sum_b, q_c, scale_c, sum_c, q_d, scale_d, sum_d, pair, send, recv,
):
    here = place()
    x, z, y, h, k = here
    xp, xm = shifted(here, dx=1), shifted(here, dx=3)
    yp, ym = shifted(here, dy=1), shifted(here, dy=3)
    zp = shifted(here, dz=1)
    barrier = pltpu.get_barrier_semaphore()
    for peer in (xp, xm, yp, ym, zp):
        pl.semaphore_signal(barrier, inc=1, device_id=peer, device_id_type=MESH)
    pl.semaphore_wait(barrier, 5)
    copies = Copies(send, recv)

    mid_a, end_a = ring_sum(
        copies, lambda p, q: t_ref.at[p, q, :, 0:256, :], x, xp, xm, q_a, scale_a, sum_a
    )
    mid_b, end_b = ring_sum(
        copies, lambda p, q: t_ref.at[:, q, p, 256:512, :], y, yp, ym, q_b, scale_b, sum_b
    )
    second_a, second_b = mid_a(), mid_b()
    end_a(second_a)
    mid_c, end_c = ring_sum(copies, lambda p, q: sum_a.at[q, p], y, yp, ym, q_c, scale_c, sum_c)
    end_b(second_b)
    mid_d, end_d = ring_sum(copies, lambda p, q: sum_b.at[q, p], x, xp, xm, q_d, scale_d, sum_d)
    second_c, second_d = mid_c(), mid_d()
    other = 1 - z
    end_c(second_c)
    pair_c = copies.start(sum_c.at[other], pair.at[0], zp)
    end_d(second_d)
    pair_d = copies.start(sum_d.at[other], pair.at[1], zp)
    bias = bias_ref[...]
    lost = jnp.zeros((1, 128), F32)
    for i, (copy, total) in enumerate(((pair_c, sum_c), (pair_d, sum_d))):
        copy.wait()
        own = total[z] + pair[i]
        for b in range(2):
            pre = own[b * 128 : (b + 1) * 128].T + bias
            rows = slice((2 * i + b) * 128, (2 * i + b + 1) * 128)
            out_ref[rows] = jnp.maximum(pre, 0.0).astype(BF16)
            grad = jnp.where(pre > 0, cot_ref[rows].astype(F32), 0.0)
            lost = lost + jnp.sum(grad, axis=0, keepdims=True)
            g_ref[x, z, y, rows] = grad.astype(BF16)
    bsum_ref[...] = lost

    copies.start(g_ref.at[x, z, y], g_ref.at[x, z, y], zp).wait()
    top, low = pl.ds(0, 256), pl.ds(256, 256)
    x1, x3 = lax.rem(x + 1, 4), lax.rem(x + 3, 4)
    y1, y3 = lax.rem(y + 1, 4), lax.rem(y + 3, 4)

    def ring_gather(mine, before, after, plus, minus):
        sent = [copies.start(mine, mine, plus), copies.start(mine, mine, minus)]

        def middle():
            sent[0].wait_recv()
            sent.append(copies.start(before, before, plus))
            sent[1].wait_recv()
            sent.append(copies.start(after, after, minus))

        def last():
            sent[2].wait_recv()
            sent[3].wait_recv()
            for copy in sent:
                copy.wait_send()

        return middle, last

    mid_a, end_a = ring_gather(
        g_ref.at[x, :, y, top], g_ref.at[x, 0, y3, top], g_ref.at[x, 1, y1, top], yp, ym
    )
    mid_b, end_b = ring_gather(
        g_ref.at[x, :, y, low], g_ref.at[x3, 0, y, low], g_ref.at[x1, 1, y, low], xp, xm
    )
    mid_a()
    mid_b()
    end_a()
    mid_c, end_c = ring_gather(
        g_ref.at[x, :, :, top], g_ref.at[x3, 0, :, top], g_ref.at[x1, 1, :, top], xp, xm
    )
    end_b()
    mid_d, end_d = ring_gather(
        g_ref.at[:, :, y, low], g_ref.at[:, 0, y3, low], g_ref.at[:, 1, y1, low], yp, ym
    )
    mid_c()
    mid_d()
    end_c()
    end_d()


def reduce_gather(totals, bias, cotangent):
    vmem = pl.BlockSpec(memory_space=pltpu.VMEM)

    def ring(half):
        return [
            pltpu.VMEM((12,) + half, jnp.int16),
            pltpu.VMEM((12, 8, 128), F32),
            pltpu.VMEM((2,) + half, F32),
        ]

    return pl.pallas_call(
        reduce_gather_kernel,
        out_shape=(
            jax.ShapeDtypeStruct((512, 128), BF16),
            jax.ShapeDtypeStruct((4, 2, 4, 512, 128), BF16),
            jax.ShapeDtypeStruct((1, 128), F32),
        ),
        in_specs=[vmem] * 3,
        out_specs=(vmem,) * 3,
        scratch_shapes=ring((4, 256, 128)) * 2
        + ring((256, 128)) * 2
        + [
            pltpu.VMEM((2, 256, 128), F32),
            pltpu.SemaphoreType.DMA((72,)),
            pltpu.SemaphoreType.DMA((72,)),
        ],
        compiler_params=pltpu.CompilerParams(
            collective_id=0, has_side_effects=True, vmem_limit_bytes=REDUCE_VMEM
        ),
        name="reduce_gather",
    )(totals, bias, cotangent)


def finish_kernel(
    t_ref, feat_ref, weight_ref, bsum_ref, gf_ref, gw_ref, gb_ref,
    from_core, outgoing, from_chip, local, row_parts, total, col_parts, whole, send, recv,
):
    here = place()
    x, z, y, h, k = here
    r, c = lax.axis_index("row"), lax.axis_index("col")
    row_shifts = [(dh, dk) for dh in range(4) for dk in range(2) if (dh, dk) != (0, 0)]
    col_shifts = [
        (dx, dz, dy) for dx in range(4) for dz in range(2) for dy in range(4) if (dx, dz, dy) != (0, 0, 0)
    ]
    row_peers = [shifted(here, dh=dh, dk=dk) for dh, dk in row_shifts]
    col_peers = [shifted(here, dx=dx, dz=dz, dy=dy) for dx, dz, dy in col_shifts]
    barrier = pltpu.get_barrier_semaphore()
    for peer in row_peers + col_peers:
        pl.semaphore_signal(barrier, inc=1, device_id=peer, device_id_type=MESH)
    pl.semaphore_wait(barrier, len(row_peers) + len(col_peers))
    copies = Copies(send, recv)

    other = 1 - k
    partner = shifted(here, dk=1)
    pairs = []
    for dh in (2, 1, 3, 0):
        to = lax.rem(h + dh, 4)
        pairs.append((dh, to, copies.start(t_ref.at[to, other], from_core.at[to], partner)))
    chips = []
    for dh, to, copy in pairs[:3]:
        copy.wait_recv()
        outgoing[dh - 1] = (t_ref[to, k] + from_core[to]).astype(BF16)
        chips.append(copies.start(outgoing.at[dh - 1], from_chip.at[dh - 1], shifted(here, dh=dh)))
    pairs[3][2].wait_recv()
    own = t_ref[h, k] + from_core[h]
    for copy in chips:
        copy.wait_recv()
    for i in range(3):
        own = own + from_chip[i].astype(F32)
    grad = own.astype(BF16)
    local[0:128] = lax.dot_general(
        feat_ref[...], grad, (((0,), (0,)), ((), ())), preferred_element_type=F32
    )
    local[128:136] = jnp.concatenate([bsum_ref[...], jnp.zeros((7, 128), F32)], axis=0)
    local[136:192] = jnp.zeros((56, 128), F32)

    def piece(i):
        return local.at[pl.ds(pl.multiple_of(i * PIECE, 8), PIECE)]

    sent = [copies.start(piece(p[0]), row_parts.at[r], p) for p in row_peers]
    gf_ref[...] = lax.dot_general(
        grad, weight_ref[...], (((1,), (1,)), ((), ())), preferred_element_type=F32
    ).astype(BF16)
    row_parts[r] = piece(r)[...]
    for copy in sent:
        copy.wait_recv()
    acc = row_parts[0]
    for i in range(1, 8):
        acc = acc + row_parts[i]
    total[...] = acc
    col_parts[c] = acc
    spread = [copies.start(total, col_parts.at[c], p) for p in col_peers]
    for copy in spread:
        copy.wait_recv()
    acc = col_parts[0]
    for i in range(1, 32):
        acc = acc + col_parts[i]
    mine = whole.at[pl.ds(pl.multiple_of(r * PIECE, 8), PIECE)]
    mine[...] = acc
    back = [copies.start(mine, mine, p) for p in row_peers]
    for copy in back:
        copy.wait_recv()
    scale = 131072.0**-0.5
    gw_ref[...] = whole[0:128] * scale
    gb_ref[...] = whole[128:129] * scale
    for copy in [p[2] for p in pairs] + chips + sent + spread + back:
        copy.wait_send()


def finish(partial, features, weight, bias_sum):
    vmem = pl.BlockSpec(memory_space=pltpu.VMEM)
    return pl.pallas_call(
        finish_kernel,
        out_shape=(
            jax.ShapeDtypeStruct((512, 128), BF16),
            jax.ShapeDtypeStruct((128, 128), F32),
            jax.ShapeDtypeStruct((1, 128), F32),
        ),
        in_specs=[vmem] * 4,
        out_specs=(vmem,) * 3,
        scratch_shapes=[
            pltpu.VMEM((4, 512, 128), F32),
            pltpu.VMEM((3, 512, 128), BF16),
            pltpu.VMEM((3, 512, 128), BF16),
            pltpu.VMEM((8 * PIECE, 128), F32),
            pltpu.VMEM((8, PIECE, 128), F32),
            pltpu.VMEM((PIECE, 128), F32),
            pltpu.VMEM((32, PIECE, 128), F32),
            pltpu.VMEM((8 * PIECE, 128), F32),
            pltpu.SemaphoreType.DMA((56,)),
            pltpu.SemaphoreType.DMA((56,)),
        ],
        compiler_params=pltpu.CompilerParams(
            collective_id=1, has_side_effects=True, vmem_limit_bytes=FINISH_VMEM
        ),
        name="finish",
    )(partial, features, weight, bias_sum)


def shards(
    features, weight, bias, cotangent, block_count, block_rows, block_cols, edge_offsets, edge_weight
):
    brow, bcol = block_rows[0, 0], block_cols[0, 0]
    dense, panel = prepare(block_count, edge_offsets[0, 0], edge_weight[0, 0], features, weight)
    totals = block_sums(
        forward_kernel, "forward", block_count, brow, bcol, dense, panel.reshape(32, 128, 128), 128
    )
    output, grads, bias_sum = reduce_gather(
        totals.reshape(4, 2, 4, 512, 128), bias.reshape(1, 128), cotangent
    )
    partial = block_sums(
        backward_kernel, "backward", block_count, brow, bcol, dense, grads.reshape(128, 128, 128), 32
    )
    grad_features, grad_weight, grad_bias = finish(
        partial.reshape(4, 2, 512, 128), features, weight, bias_sum
    )
    return (output, grad_features, grad_weight, grad_bias.reshape(128))


def solution(mesh):
    return jax.shard_map(
        shards,
        mesh=mesh,
        in_specs=(
            P(("row", "col"), None),
            P(),
            P(),
            P(("row", "col"), None),
            P("row", "col"),
            P("row", "col", None),
            P("row", "col", None),
            P("row", "col", None, None),
            P("row", "col", None, None),
        ),
        out_specs=(P(("row", "col"), None), P(("row", "col"), None), P(), P()),
        check_vma=False,
    )
```

```python
import functools

import jax
import jax.numpy as jnp
from jax import lax
from jax.experimental import pallas as pl
from jax.experimental.pallas import tpu as pltpu
from jax.sharding import PartitionSpec as P

MESH = pl.DeviceIdType.MESH
F32 = jnp.float32
BF16 = jnp.bfloat16
BATCH = 64
PREP_VMEM = 4 << 20
SUMS_VMEM = 4 << 20
REDUCE_VMEM = 16 << 20
FINISH_VMEM = 12 << 20


def place():
    r = lax.axis_index("row")
    c = lax.axis_index("col")
    return lax.div(c, 8), lax.rem(lax.div(c, 4), 2), lax.rem(c, 4), lax.div(r, 2), lax.rem(r, 2)


def shifted(here, dx=0, dz=0, dy=0, dh=0, dk=0):
    x, z, y, h, k = here
    x, z, y = lax.rem(x + dx, 4), lax.rem(z + dz, 2), lax.rem(y + dy, 4)
    h, k = lax.rem(h + dh, 4), lax.rem(k + dk, 2)
    return (h * 2 + k, x * 8 + z * 4 + y)


class Copies:
    def __init__(self, send, recv):
        self.send, self.recv, self.used = send, recv, 0

    def start(self, src, dst, device):
        copy = pltpu.make_async_remote_copy(
            src_ref=src,
            dst_ref=dst,
            send_sem=self.send.at[self.used],
            recv_sem=self.recv.at[self.used],
            device_id=device,
            device_id_type=MESH,
        )
        self.used += 1
        copy.start()
        return copy


def prepare_kernel(
    count_ref, off_hbm, w_hbm, feat_hbm, weight_hbm, d_ref, panel_ref,
    off_ref, w_ref, feat_ref, weight_ref, load, send, recv,
):
    loads = [
        pltpu.make_async_copy(source, target, load.at[i])
        for i, (source, target) in enumerate(
            (
                (feat_hbm, feat_ref),
                (weight_hbm, weight_ref),
                (off_hbm.at[0, 0], off_ref),
                (w_hbm.at[0, 0], w_ref),
            )
        )
    ]
    for copy in loads:
        copy.start()
    here = place()
    x, z, y, h, k = here
    r = lax.axis_index("row")
    partner = shifted(here, dk=1)
    chips = [shifted(here, dh=dh) for dh in (2, 1, 3)]
    barrier = pltpu.get_barrier_semaphore()
    for peer in [partner] + chips:
        pl.semaphore_signal(barrier, inc=1, device_id=peer, device_id_type=MESH)
    loads[0].wait()
    loads[1].wait()
    for b in range(4):
        rows = slice(b * 128, (b + 1) * 128)
        projected = jnp.dot(feat_ref[rows], weight_ref[...], preferred_element_type=F32)
        panel_ref[r, b] = projected.T.astype(BF16)
    pl.semaphore_wait(barrier, 4)
    copies = Copies(send, recv)
    away = [copies.start(panel_ref.at[r], panel_ref.at[r], p) for p in chips]
    beside = [copies.start(panel_ref.at[r], panel_ref.at[r], partner)]

    loads[2].wait()
    loads[3].wait()
    count = count_ref[0, 0]
    ids = (
        lax.broadcasted_iota(jnp.int32, (8, 16, 128), 0) * 16
        + lax.broadcasted_iota(jnp.int32, (8, 16, 128), 1)
    ).astype(F32).astype(BF16)
    one = jnp.ones((8, 16, 128), BF16)
    zero = jnp.zeros((8, 16, 128), BF16)

    def row(a, s):
        return jnp.broadcast_to(a[s : s + 1], (16, 128)).astype(BF16)[None]

    def densify(step, carry):
        start = pl.multiple_of(step * BATCH, BATCH)
        off = off_ref[pl.ds(start, BATCH)]
        hi = lax.shift_right_logical(off, 7).astype(F32)
        lo = lax.bitwise_and(off, 127).astype(F32)
        slot = start + lax.broadcasted_iota(jnp.int32, off.shape, 0)
        w = jnp.where(slot < count, w_ref[pl.ds(start, BATCH)].astype(F32), 0.0)
        for s in range(BATCH):
            left = jnp.where(ids == row(hi, s), jnp.broadcast_to(row(w, s), (8, 16, 128)), zero)
            right = jnp.where(ids == row(lo, s), one, zero)
            d_ref[start + s] = lax.dot_general(
                right.reshape(128, 128),
                left.reshape(128, 128),
                (((1,), (1,)), ((), ())),
                preferred_element_type=F32,
            ).astype(BF16)
        return carry

    steps = d_ref.shape[0] // BATCH
    lax.fori_loop(0, steps * 3 // 4, densify, 0)
    for dh, copy in zip((2, 1, 3), away):
        copy.wait_recv()
        got = panel_ref.at[lax.rem(h - dh + 4, 4) * 2 + k]
        beside.append(copies.start(got, got, partner))
    lax.fori_loop(steps * 3 // 4, steps, densify, 0)
    for copy in beside:
        copy.wait_recv()
    for copy in away + beside:
        copy.wait_send()


def prepare(count, offsets, weights, features, weight):
    slots = offsets.shape[2]
    vmem = pl.BlockSpec(memory_space=pltpu.VMEM)
    hbm = pl.BlockSpec(memory_space=pltpu.HBM)
    return pl.pallas_call(
        prepare_kernel,
        out_shape=(
            jax.ShapeDtypeStruct((slots, 128, 128), BF16),
            jax.ShapeDtypeStruct((8, 4, 128, 128), BF16),
        ),
        in_specs=[pl.BlockSpec(memory_space=pltpu.SMEM)] + [hbm] * 4,
        out_specs=(vmem,) * 2,
        scratch_shapes=[
            pltpu.VMEM((slots, 128), jnp.int32),
            pltpu.VMEM((slots, 128), BF16),
            pltpu.VMEM((512, 128), BF16),
            pltpu.VMEM((128, 128), BF16),
            pltpu.SemaphoreType.DMA((4,)),
            pltpu.SemaphoreType.DMA((7,)),
            pltpu.SemaphoreType.DMA((7,)),
        ],
        compiler_params=pltpu.CompilerParams(
            collective_id=2, has_side_effects=True, vmem_limit_bytes=PREP_VMEM
        ),
        name="prepare",
    )(count, *in_hbm(offsets, weights, features, weight))


def in_hbm(*arrays):
    return [pltpu.with_memory_space_constraint(a, pltpu.HBM) for a in arrays]


def load_tables(row_hbm, col_hbm, row_ref, col_ref, sem):
    loads = [
        pltpu.make_async_copy(row_hbm, row_ref, sem.at[0]),
        pltpu.make_async_copy(col_hbm, col_ref, sem.at[1]),
    ]
    for copy in loads:
        copy.start()
    return loads


def forward_kernel(count_ref, row_hbm, col_hbm, d_ref, x_ref, t_ref, row_ref, col_ref, sem):
    loads = load_tables(row_hbm, col_hbm, row_ref, col_ref, sem)
    t_ref[...] = jnp.zeros_like(t_ref)
    for copy in loads:
        copy.wait()

    def step(i, carry):
        for s in range(BATCH):
            n = i * BATCH + s
            r, c = row_ref[0, 0, n], col_ref[0, 0, n]
            t_ref[r] += jnp.dot(x_ref[c], d_ref[n], preferred_element_type=F32)
        return carry

    lax.fori_loop(0, lax.div(count_ref[0, 0] + (BATCH - 1), BATCH), step, 0)


def backward_kernel(
    count_ref, row_hbm, col_hbm, d_ref, y_ref, result_ref, t_ref, result_hbm, row_ref, col_ref, sem
):
    loads = load_tables(row_hbm, col_hbm, row_ref, col_ref, sem)
    passed = pltpu.make_async_copy(result_ref, result_hbm, sem.at[2])
    passed.start()
    t_ref[...] = jnp.zeros_like(t_ref)
    for copy in loads:
        copy.wait()

    def step(i, carry):
        for s in range(BATCH):
            n = i * BATCH + s
            r, c = row_ref[0, 0, n], col_ref[0, 0, n]
            t_ref[c] += jnp.dot(d_ref[n], y_ref[r], preferred_element_type=F32)
        return carry

    lax.fori_loop(0, lax.div(count_ref[0, 0] + (BATCH - 1), BATCH), step, 0)
    passed.wait()


def block_sums(name, count, brow, bcol, dense, panel, blocks, result=None):
    smem, vmem = pl.BlockSpec(memory_space=pltpu.SMEM), pl.BlockSpec(memory_space=pltpu.VMEM)
    sums = jax.ShapeDtypeStruct((blocks, 128, 128), F32)
    params = pltpu.CompilerParams(vmem_limit_bytes=SUMS_VMEM)
    hbm = pl.BlockSpec(memory_space=pltpu.HBM)
    brow, bcol = in_hbm(brow, bcol)
    scratch = [
        pltpu.SMEM(brow.shape, jnp.int32),
        pltpu.SMEM(bcol.shape, jnp.int32),
        pltpu.SemaphoreType.DMA((3,)),
    ]
    if result is None:
        return pl.pallas_call(
            forward_kernel,
            in_specs=[smem, hbm, hbm] + [vmem] * 2,
            out_specs=vmem,
            scratch_shapes=scratch,
            out_shape=sums,
            compiler_params=params,
            name=name,
        )(count, brow, bcol, dense, panel)
    return pl.pallas_call(
        backward_kernel,
        in_specs=[smem, hbm, hbm] + [vmem] * 3,
        out_specs=(vmem, hbm),
        out_shape=(sums, jax.ShapeDtypeStruct(result.shape, result.dtype)),
        scratch_shapes=scratch,
        compiler_params=params,
        name=name,
    )(count, brow, bcol, dense, panel, result)


LEVELS = 32766.0


def blocks_of(ref):
    if len(ref.shape) == 2:
        return [(pl.ds(128 * b, 128),) for b in range(2)]
    return [(i, pl.ds(128 * b, 128)) for i in range(ref.shape[0]) for b in range(2)]


def encode(value, at, n, q_ref, s_ref):
    size = jnp.abs(value)
    most = jnp.maximum(jnp.max(size, axis=0, keepdims=True), 1e-30)
    level = jnp.sqrt(size * (1.0 / most)) * LEVELS + 0.5
    q_ref[at] = jnp.where(value < 0, -level, level).astype(jnp.int32).astype(jnp.int16)
    s_ref[n : n + 1] = most * (1.0 / (LEVELS * LEVELS))


def decode(at, n, q_ref, s_ref):
    level = q_ref[at].astype(jnp.int32).astype(F32)
    return level * jnp.abs(level) * s_ref[n : n + 1]


def ring_sum(copies, pick, me, plus, minus, q, scales, total):
    p1, p2, p3 = lax.rem(me + 1, 4), lax.rem(me + 2, 4), lax.rem(me + 3, 4)

    def send(value, slot, device):
        for n, at in enumerate(blocks_of(q.at[slot])):
            encode(value(n, at), at, n, q.at[slot], scales.at[slot])
        return (
            copies.start(q.at[slot], q.at[slot + 6], device),
            copies.start(scales.at[slot], scales.at[slot + 6], device),
        )

    def got(slot):
        return lambda n, at: decode(at, n, q.at[slot + 6], scales.at[slot + 6])

    def own(p, half):
        return lambda n, at: pick(p, half)[at]

    def plus_got(p, half, slot):
        return lambda n, at: own(p, half)(n, at) + got(slot)(n, at)

    first = [
        send(own(p2, 0), 0, plus),
        send(own(p2, 1), 1, minus),
        send(own(p1, 1), 2, plus),
        send(own(p3, 0), 3, minus),
    ]

    def middle():
        second = []
        for slot, p, half, device in ((0, p1, 0, plus), (1, p3, 1, minus)):
            for copy in first[slot]:
                copy.wait_recv()
            second.append(send(plus_got(p, half, slot), slot + 4, device))
        return second

    def last(second):
        for half, one, two in ((1, 2, 5), (0, 3, 4)):
            for copy in first[one] + second[two - 4]:
                copy.wait_recv()
            out = total.at[half]
            for n, at in enumerate(blocks_of(out)):
                out[at] = own(me, half)(n, at) + got(one)(n, at) + got(two)(n, at)
        for pair in first + second:
            for copy in pair:
                copy.wait_send()

    return middle, last


def reduce_gather_kernel(
    t_ref, bias_ref, cot_ref, out_ref, g_ref, bsum_ref,
    q_a, scale_a, sum_a, q_b, scale_b, sum_b, q_c, scale_c, sum_c, q_d, scale_d, sum_d, pair, send, recv,
):
    here = place()
    x, z, y, h, k = here
    xp, xm = shifted(here, dx=1), shifted(here, dx=3)
    yp, ym = shifted(here, dy=1), shifted(here, dy=3)
    zp = shifted(here, dz=1)
    barrier = pltpu.get_barrier_semaphore()
    for peer in (xp, xm, yp, ym, zp):
        pl.semaphore_signal(barrier, inc=1, device_id=peer, device_id_type=MESH)
    pl.semaphore_wait(barrier, 5)
    copies = Copies(send, recv)

    mid_a, end_a = ring_sum(
        copies, lambda p, q: t_ref.at[p, q, :, 0:256, :], x, xp, xm, q_a, scale_a, sum_a
    )
    mid_b, end_b = ring_sum(
        copies, lambda p, q: t_ref.at[:, q, p, 256:512, :], y, yp, ym, q_b, scale_b, sum_b
    )
    second_a, second_b = mid_a(), mid_b()
    end_a(second_a)
    mid_c, end_c = ring_sum(copies, lambda p, q: sum_a.at[q, p], y, yp, ym, q_c, scale_c, sum_c)
    end_b(second_b)
    mid_d, end_d = ring_sum(copies, lambda p, q: sum_b.at[q, p], x, xp, xm, q_d, scale_d, sum_d)
    second_c, second_d = mid_c(), mid_d()
    other = 1 - z
    end_c(second_c)
    pair_c = copies.start(sum_c.at[other], pair.at[0], zp)
    end_d(second_d)
    pair_d = copies.start(sum_d.at[other], pair.at[1], zp)
    bias = bias_ref[...]
    lost = jnp.zeros((1, 128), F32)
    for i, (copy, total) in enumerate(((pair_c, sum_c), (pair_d, sum_d))):
        copy.wait()
        own = total[z] + pair[i]
        for b in range(2):
            pre = own[b * 128 : (b + 1) * 128].T + bias
            rows = slice((2 * i + b) * 128, (2 * i + b + 1) * 128)
            out_ref[rows] = jnp.maximum(pre, 0.0).astype(BF16)
            grad = jnp.where(pre > 0, cot_ref[rows].astype(F32), 0.0)
            lost = lost + jnp.sum(grad, axis=0, keepdims=True)
            g_ref[x, z, y, rows] = grad.astype(BF16)
    bsum_ref[...] = lost

    copies.start(g_ref.at[x, z, y], g_ref.at[x, z, y], zp).wait()
    top, low = pl.ds(0, 256), pl.ds(256, 256)
    x1, x3 = lax.rem(x + 1, 4), lax.rem(x + 3, 4)
    y1, y3 = lax.rem(y + 1, 4), lax.rem(y + 3, 4)

    def ring_gather(mine, before, after, plus, minus):
        sent = [copies.start(mine, mine, plus), copies.start(mine, mine, minus)]

        def middle():
            sent[0].wait_recv()
            sent.append(copies.start(before, before, plus))
            sent[1].wait_recv()
            sent.append(copies.start(after, after, minus))

        def last():
            sent[2].wait_recv()
            sent[3].wait_recv()
            for copy in sent:
                copy.wait_send()

        return middle, last

    mid_a, end_a = ring_gather(
        g_ref.at[x, :, y, top], g_ref.at[x, 0, y3, top], g_ref.at[x, 1, y1, top], yp, ym
    )
    mid_b, end_b = ring_gather(
        g_ref.at[x, :, y, low], g_ref.at[x3, 0, y, low], g_ref.at[x1, 1, y, low], xp, xm
    )
    mid_a()
    mid_b()
    end_a()
    mid_c, end_c = ring_gather(
        g_ref.at[x, :, :, top], g_ref.at[x3, 0, :, top], g_ref.at[x1, 1, :, top], xp, xm
    )
    end_b()
    mid_d, end_d = ring_gather(
        g_ref.at[:, :, y, low], g_ref.at[:, 0, y3, low], g_ref.at[:, 1, y1, low], yp, ym
    )
    mid_c()
    mid_d()
    end_c()
    end_d()


def reduce_gather(totals, bias, cotangent):
    vmem = pl.BlockSpec(memory_space=pltpu.VMEM)

    def ring(half):
        return [
            pltpu.VMEM((12,) + half, jnp.int16),
            pltpu.VMEM((12, 8, 128), F32),
            pltpu.VMEM((2,) + half, F32),
        ]

    return pl.pallas_call(
        reduce_gather_kernel,
        out_shape=(
            jax.ShapeDtypeStruct((512, 128), BF16),
            jax.ShapeDtypeStruct((4, 2, 4, 512, 128), BF16),
            jax.ShapeDtypeStruct((1, 128), F32),
        ),
        in_specs=[vmem] * 3,
        out_specs=(vmem,) * 3,
        scratch_shapes=ring((4, 256, 128)) * 2
        + ring((256, 128)) * 2
        + [
            pltpu.VMEM((2, 256, 128), F32),
            pltpu.SemaphoreType.DMA((72,)),
            pltpu.SemaphoreType.DMA((72,)),
        ],
        compiler_params=pltpu.CompilerParams(
            collective_id=0, has_side_effects=True, vmem_limit_bytes=REDUCE_VMEM
        ),
        name="reduce_gather",
    )(totals, bias, cotangent)


def finish_kernel(
    t_ref, feat_ref, weight_ref, bsum_ref, gf_ref, gw_ref, gb_ref,
    from_core, outgoing, from_chip, local, plane_parts, total, line_parts, whole,
    lost, plane_lost, total_lost, line_lost, send, recv,
):
    here = place()
    x, z, y, h, k = here
    mine, line = x * 4 + y, (h * 2 + k) * 2 + z
    plane = [
        (shifted(here, dx=dx, dy=dy), lax.rem(x + dx, 4) * 4 + lax.rem(y + dy, 4))
        for dx in range(4)
        for dy in range(4)
        if (dx, dy) != (0, 0)
    ]
    column = [
        shifted(here, dz=dz, dh=dh, dk=dk)
        for dh in range(4)
        for dz in range(2)
        for dk in range(2)
        if (dz, dh, dk) != (0, 0, 0)
    ]
    barrier = pltpu.get_barrier_semaphore()
    for peer in column + [p for p, _ in plane]:
        pl.semaphore_signal(barrier, inc=1, device_id=peer, device_id_type=MESH)
    lost[...] = jnp.concatenate([bsum_ref[...], jnp.zeros((7, 128), F32)], axis=0)
    pl.semaphore_wait(barrier, 30)
    copies = Copies(send, recv)

    other = 1 - k
    partner = shifted(here, dk=1)
    pairs = []
    for dh in (2, 1, 3, 0):
        to = lax.rem(h + dh, 4)
        pairs.append((dh, to, copies.start(t_ref.at[to, other], from_core.at[to], partner)))
    bias_plane = [copies.start(lost, plane_lost.at[mine], p) for p, _ in plane]
    plane_lost[mine] = lost[...]
    chips = []
    for dh, to, copy in pairs[:3]:
        copy.wait_recv()
        outgoing[dh - 1] = (t_ref[to, k] + from_core[to]).astype(BF16)
        chips.append(copies.start(outgoing.at[dh - 1], from_chip.at[dh - 1], shifted(here, dh=dh)))
    for copy in bias_plane:
        copy.wait_recv()
    total_lost[...] = sum_of(plane_lost)
    bias_line = [copies.start(total_lost, line_lost.at[line], p) for p in column]
    line_lost[line] = total_lost[...]
    pairs[3][2].wait_recv()
    own = t_ref[h, k] + from_core[h]
    for copy in chips:
        copy.wait_recv()
    for i in range(3):
        own = own + from_chip[i].astype(F32)
    grad = own.astype(BF16)
    local[...] = lax.dot_general(
        feat_ref[...], grad, (((0,), (0,)), ((), ())), preferred_element_type=F32
    )

    def rows(i):
        return pl.ds(pl.multiple_of(i * 8, 8), 8)

    sent = [copies.start(local.at[rows(i)], plane_parts.at[mine], p) for p, i in plane]
    plane_parts[mine] = local[rows(mine)]
    gf_ref[...] = lax.dot_general(
        grad, weight_ref[...], (((1,), (1,)), ((), ())), preferred_element_type=F32
    ).astype(BF16)
    scale = 131072.0**-0.5
    for copy in bias_line:
        copy.wait_recv()
    gb_ref[...] = sum_of(line_lost)[0:1] * scale
    for copy in sent:
        copy.wait_recv()
    total[...] = sum_of(plane_parts)
    spread = [copies.start(total, line_parts.at[line], p) for p in column]
    line_parts[line] = total[...]
    for copy in spread:
        copy.wait_recv()
    whole[rows(mine)] = sum_of(line_parts) * scale
    back = [copies.start(whole.at[rows(mine)], whole.at[rows(mine)], p) for p, _ in plane]
    for copy in back:
        copy.wait_recv()
    gw_ref[...] = whole[...]
    for copy in [p[2] for p in pairs] + bias_plane + chips + bias_line + sent + spread + back:
        copy.wait_send()


def sum_of(ref):
    parts = [ref[i] for i in range(ref.shape[0])]
    while len(parts) > 1:
        parts = [a + b for a, b in zip(parts[::2], parts[1::2])]
    return parts[0]


def finish(partial, features, weight, bias_sum):
    vmem = pl.BlockSpec(memory_space=pltpu.VMEM)
    sums = [
        pltpu.VMEM((16, 8, 128), F32),
        pltpu.VMEM((8, 128), F32),
        pltpu.VMEM((16, 8, 128), F32),
    ]
    return pl.pallas_call(
        finish_kernel,
        out_shape=(
            jax.ShapeDtypeStruct((512, 128), BF16),
            jax.ShapeDtypeStruct((128, 128), F32),
            jax.ShapeDtypeStruct((1, 128), F32),
        ),
        in_specs=[vmem] * 4,
        out_specs=(vmem,) * 3,
        scratch_shapes=[
            pltpu.VMEM((4, 512, 128), F32),
            pltpu.VMEM((3, 512, 128), BF16),
            pltpu.VMEM((3, 512, 128), BF16),
            pltpu.VMEM((128, 128), F32),
            *sums,
            pltpu.VMEM((128, 128), F32),
            pltpu.VMEM((8, 128), F32),
            *sums,
            pltpu.SemaphoreType.DMA((82,)),
            pltpu.SemaphoreType.DMA((82,)),
        ],
        compiler_params=pltpu.CompilerParams(
            collective_id=1, has_side_effects=True, vmem_limit_bytes=FINISH_VMEM
        ),
        name="finish",
    )(partial, features, weight, bias_sum)


def shards(
    features, weight, bias, cotangent, block_count, block_rows, block_cols, edge_offsets, edge_weight
):
    tables = (block_count, block_rows, block_cols)
    dense, panel = prepare(block_count, edge_offsets, edge_weight, features, weight)
    totals = block_sums("forward", *tables, dense, panel.reshape(32, 128, 128), 128)
    output, grads, bias_sum = reduce_gather(
        totals.reshape(4, 2, 4, 512, 128), bias.reshape(1, 128), cotangent
    )
    partial, output = block_sums(
        "backward", *tables, dense, grads.reshape(128, 128, 128), 32, output
    )
    grad_features, grad_weight, grad_bias = finish(
        partial.reshape(4, 2, 512, 128), features, weight, bias_sum
    )
    return (output, grad_features, grad_weight, grad_bias.reshape(128))


def solution(mesh):
    return jax.shard_map(
        shards,
        mesh=mesh,
        in_specs=(
            P(("row", "col"), None),
            P(),
            P(),
            P(("row", "col"), None),
            P("row", "col"),
            P("row", "col", None),
            P("row", "col", None),
            P("row", "col", None, None),
            P("row", "col", None, None),
        ),
        out_specs=(P(("row", "col"), None), P(("row", "col"), None), P(), P()),
        check_vma=False,
    )
```

```python
import functools

import jax
import jax.numpy as jnp
from jax import lax
from jax.experimental import pallas as pl
from jax.experimental.pallas import tpu as pltpu
from jax.sharding import PartitionSpec as P

MESH = pl.DeviceIdType.MESH
F32 = jnp.float32
BF16 = jnp.bfloat16
BATCH = 64
PREP_VMEM = 4 << 20
SUMS_VMEM = 4 << 20
REDUCE_VMEM = 16 << 20
FINISH_VMEM = 12 << 20


def place():
    r = lax.axis_index("row")
    c = lax.axis_index("col")
    return lax.div(c, 8), lax.rem(lax.div(c, 4), 2), lax.rem(c, 4), lax.div(r, 2), lax.rem(r, 2)


def shifted(here, dx=0, dz=0, dy=0, dh=0, dk=0):
    x, z, y, h, k = here
    x, z, y = lax.rem(x + dx, 4), lax.rem(z + dz, 2), lax.rem(y + dy, 4)
    h, k = lax.rem(h + dh, 4), lax.rem(k + dk, 2)
    return (h * 2 + k, x * 8 + z * 4 + y)


class RingGather:
    def __init__(self, copies, mine, from_minus, from_plus, plus, minus):
        self.copies, self.plus, self.minus = copies, plus, minus
        self.from_minus, self.from_plus = from_minus, from_plus
        self.sent = [copies.start(mine, mine, plus), copies.start(mine, mine, minus)]

    def pass_on(self):
        self.sent[0].wait_recv()
        self.sent.append(self.copies.start(self.from_minus, self.from_minus, self.plus))
        self.sent[1].wait_recv()
        self.sent.append(self.copies.start(self.from_plus, self.from_plus, self.minus))

    def arrive(self):
        self.sent[2].wait_recv()
        self.sent[3].wait_recv()

    def drain(self):
        for copy in self.sent:
            copy.wait_send()


class Copies:
    def __init__(self, send, recv):
        self.send, self.recv, self.used = send, recv, 0

    def start(self, src, dst, device):
        copy = pltpu.make_async_remote_copy(
            src_ref=src,
            dst_ref=dst,
            send_sem=self.send.at[self.used],
            recv_sem=self.recv.at[self.used],
            device_id=device,
            device_id_type=MESH,
        )
        self.used += 1
        copy.start()
        return copy


def prepare_kernel(
    count_ref, off_hbm, w_hbm, feat_hbm, weight_hbm, d_ref, panel_ref,
    off_ref, w_ref, feat_ref, weight_ref, load, send, recv,
):
    loads = [
        pltpu.make_async_copy(source, target, load.at[i])
        for i, (source, target) in enumerate(
            (
                (feat_hbm, feat_ref),
                (weight_hbm, weight_ref),
                (off_hbm.at[0, 0], off_ref),
                (w_hbm.at[0, 0], w_ref),
            )
        )
    ]
    for copy in loads:
        copy.start()
    here = place()
    x, z, y, h, k = here
    r = lax.axis_index("row")
    partner = shifted(here, dk=1)
    above, below = shifted(here, dh=1), shifted(here, dh=3)
    barrier = pltpu.get_barrier_semaphore()
    for peer in (partner, above, below):
        pl.semaphore_signal(barrier, inc=1, device_id=peer, device_id_type=MESH)
    loads[0].wait()
    loads[1].wait()
    for b in range(4):
        rows = slice(b * 128, (b + 1) * 128)
        projected = jnp.dot(feat_ref[rows], weight_ref[...], preferred_element_type=F32)
        panel_ref[r, b] = projected.T.astype(BF16)
    pl.semaphore_wait(barrier, 3)
    copies = Copies(send, recv)
    h1, h2, h3 = (lax.rem(h + i, 4) * 2 + k for i in (1, 2, 3))
    ring = RingGather(
        copies, panel_ref.at[r], panel_ref.at[h3, 0:2], panel_ref.at[h1, 2:4], above, below
    )

    def pass_over(i):
        return copies.start(panel_ref.at[i], panel_ref.at[i], partner)

    beside = [pass_over(r)]

    loads[2].wait()
    loads[3].wait()
    count = count_ref[0, 0]
    ids = (
        lax.broadcasted_iota(jnp.int32, (8, 16, 128), 0) * 16
        + lax.broadcasted_iota(jnp.int32, (8, 16, 128), 1)
    ).astype(F32).astype(BF16)
    one = jnp.ones((8, 16, 128), BF16)
    zero = jnp.zeros((8, 16, 128), BF16)

    def row(a, s):
        return jnp.broadcast_to(a[s : s + 1], (16, 128)).astype(BF16)[None]

    def densify(step, carry):
        start = pl.multiple_of(step * BATCH, BATCH)
        off = off_ref[pl.ds(start, BATCH)]
        hi = lax.shift_right_logical(off, 7).astype(F32)
        lo = lax.bitwise_and(off, 127).astype(F32)
        slot = start + lax.broadcasted_iota(jnp.int32, off.shape, 0)
        w = jnp.where(slot < count, w_ref[pl.ds(start, BATCH)].astype(F32), 0.0)
        for s in range(BATCH):
            left = jnp.where(ids == row(hi, s), jnp.broadcast_to(row(w, s), (8, 16, 128)), zero)
            right = jnp.where(ids == row(lo, s), one, zero)
            d_ref[start + s] = lax.dot_general(
                right.reshape(128, 128),
                left.reshape(128, 128),
                (((1,), (1,)), ((), ())),
                preferred_element_type=F32,
            ).astype(BF16)
        return carry

    steps = d_ref.shape[0] // BATCH
    lax.fori_loop(0, steps // 2, densify, 0)
    ring.pass_on()
    beside += [pass_over(h3), pass_over(h1)]
    lax.fori_loop(steps // 2, steps * 7 // 8, densify, 0)
    ring.arrive()
    beside.append(pass_over(h2))
    lax.fori_loop(steps * 7 // 8, steps, densify, 0)
    for copy in beside:
        copy.wait()
    ring.drain()


def prepare(count, offsets, weights, features, weight):
    slots = offsets.shape[2]
    vmem = pl.BlockSpec(memory_space=pltpu.VMEM)
    hbm = pl.BlockSpec(memory_space=pltpu.HBM)
    return pl.pallas_call(
        prepare_kernel,
        out_shape=(
            jax.ShapeDtypeStruct((slots, 128, 128), BF16),
            jax.ShapeDtypeStruct((8, 4, 128, 128), BF16),
        ),
        in_specs=[pl.BlockSpec(memory_space=pltpu.SMEM)] + [hbm] * 4,
        out_specs=(vmem,) * 2,
        scratch_shapes=[
            pltpu.VMEM((slots, 128), jnp.int32),
            pltpu.VMEM((slots, 128), BF16),
            pltpu.VMEM((512, 128), BF16),
            pltpu.VMEM((128, 128), BF16),
            pltpu.SemaphoreType.DMA((4,)),
            pltpu.SemaphoreType.DMA((8,)),
            pltpu.SemaphoreType.DMA((8,)),
        ],
        compiler_params=pltpu.CompilerParams(
            collective_id=2, has_side_effects=True, vmem_limit_bytes=PREP_VMEM
        ),
        name="prepare",
    )(count, *in_hbm(offsets, weights, features, weight))


def in_hbm(*arrays):
    return [pltpu.with_memory_space_constraint(a, pltpu.HBM) for a in arrays]


def load_tables(row_hbm, col_hbm, row_ref, col_ref, sem):
    loads = [
        pltpu.make_async_copy(row_hbm, row_ref, sem.at[0]),
        pltpu.make_async_copy(col_hbm, col_ref, sem.at[1]),
    ]
    for copy in loads:
        copy.start()
    return loads


def forward_kernel(count_ref, row_hbm, col_hbm, d_ref, x_ref, t_ref, row_ref, col_ref, sem):
    loads = load_tables(row_hbm, col_hbm, row_ref, col_ref, sem)
    t_ref[...] = jnp.zeros_like(t_ref)
    for copy in loads:
        copy.wait()

    def step(i, carry):
        for s in range(BATCH):
            n = i * BATCH + s
            r, c = row_ref[0, 0, n], col_ref[0, 0, n]
            t_ref[r] += jnp.dot(x_ref[c], d_ref[n], preferred_element_type=F32)
        return carry

    lax.fori_loop(0, lax.div(count_ref[0, 0] + (BATCH - 1), BATCH), step, 0)


def backward_kernel(
    count_ref, row_hbm, col_hbm, d_ref, y_ref, result_ref, t_ref, result_hbm, row_ref, col_ref, sem
):
    loads = load_tables(row_hbm, col_hbm, row_ref, col_ref, sem)
    passed = pltpu.make_async_copy(result_ref, result_hbm, sem.at[2])
    passed.start()
    t_ref[...] = jnp.zeros_like(t_ref)
    for copy in loads:
        copy.wait()

    def step(i, carry):
        for s in range(BATCH):
            n = i * BATCH + s
            r, c = row_ref[0, 0, n], col_ref[0, 0, n]
            t_ref[c] += jnp.dot(d_ref[n], y_ref[r], preferred_element_type=F32)
        return carry

    lax.fori_loop(0, lax.div(count_ref[0, 0] + (BATCH - 1), BATCH), step, 0)
    passed.wait()


def block_sums(name, count, brow, bcol, dense, panel, blocks, result=None):
    smem, vmem = pl.BlockSpec(memory_space=pltpu.SMEM), pl.BlockSpec(memory_space=pltpu.VMEM)
    sums = jax.ShapeDtypeStruct((blocks, 128, 128), F32)
    params = pltpu.CompilerParams(vmem_limit_bytes=SUMS_VMEM)
    hbm = pl.BlockSpec(memory_space=pltpu.HBM)
    brow, bcol = in_hbm(brow, bcol)
    scratch = [
        pltpu.SMEM(brow.shape, jnp.int32),
        pltpu.SMEM(bcol.shape, jnp.int32),
        pltpu.SemaphoreType.DMA((3,)),
    ]
    if result is None:
        return pl.pallas_call(
            forward_kernel,
            in_specs=[smem, hbm, hbm] + [vmem] * 2,
            out_specs=vmem,
            scratch_shapes=scratch,
            out_shape=sums,
            compiler_params=params,
            name=name,
        )(count, brow, bcol, dense, panel)
    return pl.pallas_call(
        backward_kernel,
        in_specs=[smem, hbm, hbm] + [vmem] * 3,
        out_specs=(vmem, hbm),
        out_shape=(sums, jax.ShapeDtypeStruct(result.shape, result.dtype)),
        scratch_shapes=scratch,
        compiler_params=params,
        name=name,
    )(count, brow, bcol, dense, panel, result)


LEVELS = 32766.0


def blocks_of(ref):
    if len(ref.shape) == 2:
        return [(pl.ds(128 * b, 128),) for b in range(2)]
    return [(i, pl.ds(128 * b, 128)) for i in range(ref.shape[0]) for b in range(2)]


def encode(value, at, n, q_ref, s_ref):
    size = jnp.abs(value)
    most = jnp.maximum(jnp.max(size, axis=0, keepdims=True), 1e-30)
    level = jnp.sqrt(size * (1.0 / most)) * LEVELS + 0.5
    q_ref[at] = jnp.where(value < 0, -level, level).astype(jnp.int32).astype(jnp.int16)
    s_ref[n : n + 1] = most * (1.0 / (LEVELS * LEVELS))


def decode(at, n, q_ref, s_ref):
    level = q_ref[at].astype(jnp.int32).astype(F32)
    return level * jnp.abs(level) * s_ref[n : n + 1]


def ring_sum(copies, pick, me, plus, minus, q, scales, total):
    p1, p2, p3 = lax.rem(me + 1, 4), lax.rem(me + 2, 4), lax.rem(me + 3, 4)

    def send(value, slot, device):
        for n, at in enumerate(blocks_of(q.at[slot])):
            encode(value(n, at), at, n, q.at[slot], scales.at[slot])
        return (
            copies.start(q.at[slot], q.at[slot + 6], device),
            copies.start(scales.at[slot], scales.at[slot + 6], device),
        )

    def got(slot):
        return lambda n, at: decode(at, n, q.at[slot + 6], scales.at[slot + 6])

    def own(p, half):
        return lambda n, at: pick(p, half)[at]

    def plus_got(p, half, slot):
        return lambda n, at: own(p, half)(n, at) + got(slot)(n, at)

    first = [
        send(own(p2, 0), 0, plus),
        send(own(p2, 1), 1, minus),
        send(own(p1, 1), 2, plus),
        send(own(p3, 0), 3, minus),
    ]

    def middle():
        second = []
        for slot, p, half, device in ((0, p1, 0, plus), (1, p3, 1, minus)):
            for copy in first[slot]:
                copy.wait_recv()
            second.append(send(plus_got(p, half, slot), slot + 4, device))
        return second

    def last(second):
        for half, one, two in ((1, 2, 5), (0, 3, 4)):
            for copy in first[one] + second[two - 4]:
                copy.wait_recv()
            out = total.at[half]
            for n, at in enumerate(blocks_of(out)):
                out[at] = own(me, half)(n, at) + got(one)(n, at) + got(two)(n, at)
        for pair in first + second:
            for copy in pair:
                copy.wait_send()

    return middle, last


def reduce_gather_kernel(
    t_ref, bias_ref, cot_ref, out_ref, g_ref, bsum_ref,
    q_a, scale_a, sum_a, q_b, scale_b, sum_b, q_c, scale_c, sum_c, q_d, scale_d, sum_d, pair, send, recv,
):
    here = place()
    x, z, y, h, k = here
    xp, xm = shifted(here, dx=1), shifted(here, dx=3)
    yp, ym = shifted(here, dy=1), shifted(here, dy=3)
    zp = shifted(here, dz=1)
    barrier = pltpu.get_barrier_semaphore()
    for peer in (xp, xm, yp, ym, zp):
        pl.semaphore_signal(barrier, inc=1, device_id=peer, device_id_type=MESH)
    pl.semaphore_wait(barrier, 5)
    copies = Copies(send, recv)

    mid_a, end_a = ring_sum(
        copies, lambda p, q: t_ref.at[p, q, :, 0:256, :], x, xp, xm, q_a, scale_a, sum_a
    )
    mid_b, end_b = ring_sum(
        copies, lambda p, q: t_ref.at[:, q, p, 256:512, :], y, yp, ym, q_b, scale_b, sum_b
    )
    second_a, second_b = mid_a(), mid_b()
    end_a(second_a)
    mid_c, end_c = ring_sum(copies, lambda p, q: sum_a.at[q, p], y, yp, ym, q_c, scale_c, sum_c)
    end_b(second_b)
    mid_d, end_d = ring_sum(copies, lambda p, q: sum_b.at[q, p], x, xp, xm, q_d, scale_d, sum_d)
    second_c, second_d = mid_c(), mid_d()
    other = 1 - z
    end_c(second_c)
    pair_c = copies.start(sum_c.at[other], pair.at[0], zp)
    end_d(second_d)
    pair_d = copies.start(sum_d.at[other], pair.at[1], zp)
    bias = bias_ref[...]
    lost = jnp.zeros((1, 128), F32)
    for i, (copy, total) in enumerate(((pair_c, sum_c), (pair_d, sum_d))):
        copy.wait()
        own = total[z] + pair[i]
        for b in range(2):
            pre = own[b * 128 : (b + 1) * 128].T + bias
            rows = slice((2 * i + b) * 128, (2 * i + b + 1) * 128)
            out_ref[rows] = jnp.maximum(pre, 0.0).astype(BF16)
            grad = jnp.where(pre > 0, cot_ref[rows].astype(F32), 0.0)
            lost = lost + jnp.sum(grad, axis=0, keepdims=True)
            g_ref[x, z, y, rows] = grad.astype(BF16)
    bsum_ref[...] = lost

    half_a, half_b, late_a, late_b = pl.ds(0, 192), pl.ds(192, 192), pl.ds(384, 64), pl.ds(448, 64)
    x1, x2, x3 = (lax.rem(x + i, 4) for i in (1, 2, 3))
    y1, y2, y3 = (lax.rem(y + i, 4) for i in (1, 2, 3))

    def over_z(ref):
        return copies.start(ref, ref, zp)

    first_z = over_z(g_ref.at[x, z, y, 0:384])
    near_e = RingGather(
        copies, g_ref.at[x, z, y, late_a], g_ref.at[x, z, y3, 384:416], g_ref.at[x, z, y1, 416:448], yp, ym
    )
    near_f = RingGather(
        copies, g_ref.at[x, z, y, late_b], g_ref.at[x3, z, y, 448:480], g_ref.at[x1, z, y, 480:512], xp, xm
    )
    first_z.wait_recv()
    near_a = RingGather(
        copies, g_ref.at[x, :, y, half_a], g_ref.at[x, 0, y3, half_a], g_ref.at[x, 1, y1, half_a], yp, ym
    )
    near_b = RingGather(
        copies, g_ref.at[x, :, y, half_b], g_ref.at[x3, 0, y, half_b], g_ref.at[x1, 1, y, half_b], xp, xm
    )
    near_e.pass_on()
    near_f.pass_on()
    near_a.pass_on()
    near_b.pass_on()
    near_e.arrive()
    far_e = RingGather(
        copies, g_ref.at[x, z, :, late_a], g_ref.at[x3, z, 0:2, late_a], g_ref.at[x1, z, 2:4, late_a], xp, xm
    )
    last_z = [over_z(g_ref.at[x, z, :, late_a])]
    near_f.arrive()
    far_f = RingGather(
        copies, g_ref.at[:, z, y, late_b], g_ref.at[0:2, z, y3, late_b], g_ref.at[2:4, z, y1, late_b], yp, ym
    )
    last_z.append(over_z(g_ref.at[:, z, y, late_b]))
    near_a.arrive()
    far_a = RingGather(
        copies, g_ref.at[x, :, :, half_a], g_ref.at[x3, 0, :, half_a], g_ref.at[x1, 1, :, half_a], xp, xm
    )
    near_b.arrive()
    far_b = RingGather(
        copies, g_ref.at[:, :, y, half_b], g_ref.at[:, 0, y3, half_b], g_ref.at[:, 1, y1, half_b], yp, ym
    )
    far_e.pass_on()
    last_z += [over_z(g_ref.at[x3, z, :, late_a]), over_z(g_ref.at[x1, z, :, late_a])]
    far_f.pass_on()
    last_z += [over_z(g_ref.at[:, z, y3, late_b]), over_z(g_ref.at[:, z, y1, late_b])]
    far_e.arrive()
    last_z.append(over_z(g_ref.at[x2, z, :, late_a]))
    far_f.arrive()
    last_z.append(over_z(g_ref.at[:, z, y2, late_b]))
    far_a.pass_on()
    far_b.pass_on()
    far_a.arrive()
    far_b.arrive()
    for copy in last_z:
        copy.wait_recv()
    for copy in [first_z] + last_z:
        copy.wait_send()
    for ring in (near_a, near_b, near_e, near_f, far_a, far_b, far_e, far_f):
        ring.drain()


def reduce_gather(totals, bias, cotangent):
    vmem = pl.BlockSpec(memory_space=pltpu.VMEM)

    def ring(half):
        return [
            pltpu.VMEM((12,) + half, jnp.int16),
            pltpu.VMEM((12, 8, 128), F32),
            pltpu.VMEM((2,) + half, F32),
        ]

    return pl.pallas_call(
        reduce_gather_kernel,
        out_shape=(
            jax.ShapeDtypeStruct((512, 128), BF16),
            jax.ShapeDtypeStruct((4, 2, 4, 512, 128), BF16),
            jax.ShapeDtypeStruct((1, 128), F32),
        ),
        in_specs=[vmem] * 3,
        out_specs=(vmem,) * 3,
        scratch_shapes=ring((4, 256, 128)) * 2
        + ring((256, 128)) * 2
        + [
            pltpu.VMEM((2, 256, 128), F32),
            pltpu.SemaphoreType.DMA((92,)),
            pltpu.SemaphoreType.DMA((92,)),
        ],
        compiler_params=pltpu.CompilerParams(
            collective_id=0, has_side_effects=True, vmem_limit_bytes=REDUCE_VMEM
        ),
        name="reduce_gather",
    )(totals, bias, cotangent)


def finish_kernel(
    t_ref, feat_ref, weight_ref, bsum_ref, gf_ref, gw_ref, gb_ref,
    from_core, outgoing, from_chip, local, plane_parts, total, line_parts, whole,
    lost, plane_lost, total_lost, line_lost, send, recv,
):
    here = place()
    x, z, y, h, k = here
    mine, line = x * 4 + y, (h * 2 + k) * 2 + z
    plane = [
        (shifted(here, dx=dx, dy=dy), lax.rem(x + dx, 4) * 4 + lax.rem(y + dy, 4))
        for dx in range(4)
        for dy in range(4)
        if (dx, dy) != (0, 0)
    ]
    column = [
        shifted(here, dz=dz, dh=dh, dk=dk)
        for dh in range(4)
        for dz in range(2)
        for dk in range(2)
        if (dz, dh, dk) != (0, 0, 0)
    ]
    barrier = pltpu.get_barrier_semaphore()
    for peer in column + [p for p, _ in plane]:
        pl.semaphore_signal(barrier, inc=1, device_id=peer, device_id_type=MESH)
    lost[...] = jnp.concatenate([bsum_ref[...], jnp.zeros((7, 128), F32)], axis=0)
    pl.semaphore_wait(barrier, 30)
    copies = Copies(send, recv)

    other = 1 - k
    partner = shifted(here, dk=1)
    pairs = {}
    for dh in (2, 1, 3, 0):
        to = lax.rem(h + dh, 4)
        pairs[dh] = copies.start(t_ref.at[to, other], from_core.at[to], partner)
    bias_plane = [copies.start(lost, plane_lost.at[mine], p) for p, _ in plane]
    plane_lost[mine] = lost[...]
    above, below = shifted(here, dh=1), shifted(here, dh=3)
    chips = []

    def both(dh, part):
        to = lax.rem(h + dh, 4)
        return t_ref[to, k, part] + from_core[to, part]

    def send(value, slot, device):
        outgoing[slot] = value.astype(BF16)
        chips.append(copies.start(outgoing.at[slot], from_chip.at[slot], device))

    upper, lower = slice(0, 256), slice(256, 512)
    pairs[2].wait_recv()
    send(both(2, upper), 0, above)
    send(both(2, lower), 1, below)
    pairs[1].wait_recv()
    send(both(1, lower), 2, above)
    pairs[3].wait_recv()
    send(both(3, upper), 3, below)
    for copy in bias_plane:
        copy.wait_recv()
    total_lost[...] = sum_of(plane_lost)
    bias_line = [copies.start(total_lost, line_lost.at[line], p) for p in column]
    line_lost[line] = total_lost[...]
    pairs[0].wait_recv()
    chips[0].wait_recv()
    send(both(1, upper) + from_chip[0].astype(F32), 4, above)
    chips[1].wait_recv()
    send(both(3, lower) + from_chip[1].astype(F32), 5, below)
    for copy in chips[2:]:
        copy.wait_recv()
    own = jnp.concatenate(
        [
            both(0, upper) + from_chip[3].astype(F32) + from_chip[4].astype(F32),
            both(0, lower) + from_chip[2].astype(F32) + from_chip[5].astype(F32),
        ],
        axis=0,
    )
    grad = own.astype(BF16)
    local[...] = lax.dot_general(
        feat_ref[...], grad, (((0,), (0,)), ((), ())), preferred_element_type=F32
    )

    def rows(i):
        return pl.ds(pl.multiple_of(i * 8, 8), 8)

    sent = [copies.start(local.at[rows(i)], plane_parts.at[mine], p) for p, i in plane]
    plane_parts[mine] = local[rows(mine)]
    gf_ref[...] = lax.dot_general(
        grad, weight_ref[...], (((1,), (1,)), ((), ())), preferred_element_type=F32
    ).astype(BF16)
    scale = 131072.0**-0.5
    for copy in bias_line:
        copy.wait_recv()
    gb_ref[...] = sum_of(line_lost)[0:1] * scale
    for copy in sent:
        copy.wait_recv()
    total[...] = sum_of(plane_parts)
    spread = [copies.start(total, line_parts.at[line], p) for p in column]
    line_parts[line] = total[...]
    for copy in spread:
        copy.wait_recv()
    whole[rows(mine)] = sum_of(line_parts) * scale
    back = [copies.start(whole.at[rows(mine)], whole.at[rows(mine)], p) for p, _ in plane]
    for copy in back:
        copy.wait_recv()
    gw_ref[...] = whole[...]
    for copy in [pairs[dh] for dh in range(4)] + bias_plane + chips + bias_line + sent + spread + back:
        copy.wait_send()


def sum_of(ref):
    parts = [ref[i] for i in range(ref.shape[0])]
    while len(parts) > 1:
        parts = [a + b for a, b in zip(parts[::2], parts[1::2])]
    return parts[0]


def finish(partial, features, weight, bias_sum):
    vmem = pl.BlockSpec(memory_space=pltpu.VMEM)
    sums = [
        pltpu.VMEM((16, 8, 128), F32),
        pltpu.VMEM((8, 128), F32),
        pltpu.VMEM((16, 8, 128), F32),
    ]
    return pl.pallas_call(
        finish_kernel,
        out_shape=(
            jax.ShapeDtypeStruct((512, 128), BF16),
            jax.ShapeDtypeStruct((128, 128), F32),
            jax.ShapeDtypeStruct((1, 128), F32),
        ),
        in_specs=[vmem] * 4,
        out_specs=(vmem,) * 3,
        scratch_shapes=[
            pltpu.VMEM((4, 512, 128), F32),
            pltpu.VMEM((6, 256, 128), BF16),
            pltpu.VMEM((6, 256, 128), BF16),
            pltpu.VMEM((128, 128), F32),
            *sums,
            pltpu.VMEM((128, 128), F32),
            pltpu.VMEM((8, 128), F32),
            *sums,
            pltpu.SemaphoreType.DMA((85,)),
            pltpu.SemaphoreType.DMA((85,)),
        ],
        compiler_params=pltpu.CompilerParams(
            collective_id=1, has_side_effects=True, vmem_limit_bytes=FINISH_VMEM
        ),
        name="finish",
    )(partial, features, weight, bias_sum)


def shards(
    features, weight, bias, cotangent, block_count, block_rows, block_cols, edge_offsets, edge_weight
):
    tables = (block_count, block_rows, block_cols)
    dense, panel = prepare(block_count, edge_offsets, edge_weight, features, weight)
    totals = block_sums("forward", *tables, dense, panel.reshape(32, 128, 128), 128)
    output, grads, bias_sum = reduce_gather(
        totals.reshape(4, 2, 4, 512, 128), bias.reshape(1, 128), cotangent
    )
    partial, output = block_sums(
        "backward", *tables, dense, grads.reshape(128, 128, 128), 32, output
    )
    grad_features, grad_weight, grad_bias = finish(
        partial.reshape(4, 2, 512, 128), features, weight, bias_sum
    )
    return (output, grad_features, grad_weight, grad_bias.reshape(128))


def solution(mesh):
    return jax.shard_map(
        shards,
        mesh=mesh,
        in_specs=(
            P(("row", "col"), None),
            P(),
            P(),
            P(("row", "col"), None),
            P("row", "col"),
            P("row", "col", None),
            P("row", "col", None),
            P("row", "col", None, None),
            P("row", "col", None, None),
        ),
        out_specs=(P(("row", "col"), None), P(("row", "col"), None), P(), P()),
        check_vma=False,
    )
```

```python
import functools

import jax
import jax.numpy as jnp
from jax import lax
from jax.experimental import pallas as pl
from jax.experimental.pallas import tpu as pltpu
from jax.sharding import PartitionSpec as P

MESH = pl.DeviceIdType.MESH
F32 = jnp.float32
BF16 = jnp.bfloat16
BATCH = 64
PREP_VMEM = 4 << 20
SUMS_VMEM = 4 << 20
REDUCE_VMEM = 16 << 20
FINISH_VMEM = 12 << 20


def place():
    r = lax.axis_index("row")
    c = lax.axis_index("col")
    return lax.div(c, 8), lax.rem(lax.div(c, 4), 2), lax.rem(c, 4), lax.div(r, 2), lax.rem(r, 2)


def shifted(here, dx=0, dz=0, dy=0, dh=0, dk=0):
    x, z, y, h, k = here
    x, z, y = lax.rem(x + dx, 4), lax.rem(z + dz, 2), lax.rem(y + dy, 4)
    h, k = lax.rem(h + dh, 4), lax.rem(k + dk, 2)
    return (h * 2 + k, x * 8 + z * 4 + y)


class RingGather:
    def __init__(self, copies, mine, from_minus, from_plus, plus, minus):
        self.copies, self.plus, self.minus = copies, plus, minus
        self.from_minus, self.from_plus = from_minus, from_plus
        self.sent = [copies.start(mine, mine, plus), copies.start(mine, mine, minus)]

    def pass_on(self):
        self.sent[0].wait_recv()
        self.sent.append(self.copies.start(self.from_minus, self.from_minus, self.plus))
        self.sent[1].wait_recv()
        self.sent.append(self.copies.start(self.from_plus, self.from_plus, self.minus))

    def arrive(self):
        self.sent[2].wait_recv()
        self.sent[3].wait_recv()

    def drain(self):
        for copy in self.sent:
            copy.wait_send()


class Copies:
    def __init__(self, send, recv):
        self.send, self.recv, self.used = send, recv, 0

    def start(self, src, dst, device):
        copy = pltpu.make_async_remote_copy(
            src_ref=src,
            dst_ref=dst,
            send_sem=self.send.at[self.used],
            recv_sem=self.recv.at[self.used],
            device_id=device,
            device_id_type=MESH,
        )
        self.used += 1
        copy.start()
        return copy


def prepare_kernel(
    count_ref, off_hbm, w_hbm, feat_hbm, weight_hbm, d_ref, panel_ref,
    off_ref, w_ref, feat_ref, weight_ref, load, send, recv,
):
    loads = [
        pltpu.make_async_copy(source, target, load.at[i])
        for i, (source, target) in enumerate(
            (
                (feat_hbm, feat_ref),
                (weight_hbm, weight_ref),
                (off_hbm.at[0, 0], off_ref),
                (w_hbm.at[0, 0], w_ref),
            )
        )
    ]
    for copy in loads:
        copy.start()
    here = place()
    x, z, y, h, k = here
    r = lax.axis_index("row")
    partner = shifted(here, dk=1)
    above, below = shifted(here, dh=1), shifted(here, dh=3)
    barrier = pltpu.get_barrier_semaphore()
    for peer in (partner, above, below):
        pl.semaphore_signal(barrier, inc=1, device_id=peer, device_id_type=MESH)
    loads[0].wait()
    loads[1].wait()
    for b in range(4):
        rows = slice(b * 128, (b + 1) * 128)
        projected = jnp.dot(feat_ref[rows], weight_ref[...], preferred_element_type=F32)
        panel_ref[r, b] = projected.T.astype(BF16)
    pl.semaphore_wait(barrier, 3)
    copies = Copies(send, recv)
    h1, h2, h3 = (lax.rem(h + i, 4) * 2 + k for i in (1, 2, 3))
    ring = RingGather(
        copies, panel_ref.at[r], panel_ref.at[h3, 0:2], panel_ref.at[h1, 2:4], above, below
    )

    def pass_over(i):
        return copies.start(panel_ref.at[i], panel_ref.at[i], partner)

    beside = [pass_over(r)]

    loads[2].wait()
    loads[3].wait()
    count = count_ref[0, 0]
    ids = (
        lax.broadcasted_iota(jnp.int32, (8, 16, 128), 0) * 16
        + lax.broadcasted_iota(jnp.int32, (8, 16, 128), 1)
    ).astype(F32).astype(BF16)
    one = jnp.ones((8, 16, 128), BF16)
    zero = jnp.zeros((8, 16, 128), BF16)

    def row(a, s):
        return jnp.broadcast_to(a[s : s + 1], (16, 128)).astype(BF16)[None]

    def densify(step, carry):
        start = pl.multiple_of(step * BATCH, BATCH)
        off = off_ref[pl.ds(start, BATCH)]
        hi = lax.shift_right_logical(off, 7).astype(F32)
        lo = lax.bitwise_and(off, 127).astype(F32)
        slot = start + lax.broadcasted_iota(jnp.int32, off.shape, 0)
        w = jnp.where(slot < count, w_ref[pl.ds(start, BATCH)].astype(F32), 0.0)
        for s in range(BATCH):
            left = jnp.where(ids == row(hi, s), jnp.broadcast_to(row(w, s), (8, 16, 128)), zero)
            right = jnp.where(ids == row(lo, s), one, zero)
            d_ref[start + s] = lax.dot_general(
                right.reshape(128, 128),
                left.reshape(128, 128),
                (((1,), (1,)), ((), ())),
                preferred_element_type=F32,
            ).astype(BF16)
        return carry

    steps = d_ref.shape[0] // BATCH
    lax.fori_loop(0, steps // 2, densify, 0)
    ring.pass_on()
    beside += [pass_over(h3), pass_over(h1)]
    lax.fori_loop(steps // 2, steps * 7 // 8, densify, 0)
    ring.arrive()
    beside.append(pass_over(h2))
    lax.fori_loop(steps * 7 // 8, steps, densify, 0)
    for copy in beside:
        copy.wait()
    ring.drain()


def prepare(count, offsets, weights, features, weight):
    slots = offsets.shape[2]
    vmem = pl.BlockSpec(memory_space=pltpu.VMEM)
    hbm = pl.BlockSpec(memory_space=pltpu.HBM)
    return pl.pallas_call(
        prepare_kernel,
        out_shape=(
            jax.ShapeDtypeStruct((slots, 128, 128), BF16),
            jax.ShapeDtypeStruct((8, 4, 128, 128), BF16),
        ),
        in_specs=[pl.BlockSpec(memory_space=pltpu.SMEM)] + [hbm] * 4,
        out_specs=(vmem,) * 2,
        scratch_shapes=[
            pltpu.VMEM((slots, 128), jnp.int32),
            pltpu.VMEM((slots, 128), BF16),
            pltpu.VMEM((512, 128), BF16),
            pltpu.VMEM((128, 128), BF16),
            pltpu.SemaphoreType.DMA((4,)),
            pltpu.SemaphoreType.DMA((8,)),
            pltpu.SemaphoreType.DMA((8,)),
        ],
        compiler_params=pltpu.CompilerParams(
            collective_id=2, has_side_effects=True, vmem_limit_bytes=PREP_VMEM
        ),
        name="prepare",
    )(count, *in_hbm(offsets, weights, features, weight))


def in_hbm(*arrays):
    return [pltpu.with_memory_space_constraint(a, pltpu.HBM) for a in arrays]


def load_tables(row_hbm, col_hbm, row_ref, col_ref, sem):
    loads = [
        pltpu.make_async_copy(row_hbm, row_ref, sem.at[0]),
        pltpu.make_async_copy(col_hbm, col_ref, sem.at[1]),
    ]
    for copy in loads:
        copy.start()
    return loads


def forward_kernel(count_ref, row_hbm, col_hbm, d_ref, x_ref, t_ref, row_ref, col_ref, sem):
    loads = load_tables(row_hbm, col_hbm, row_ref, col_ref, sem)
    t_ref[...] = jnp.zeros_like(t_ref)
    for copy in loads:
        copy.wait()

    def step(i, carry):
        for s in range(BATCH):
            n = i * BATCH + s
            r, c = row_ref[0, 0, n], col_ref[0, 0, n]
            t_ref[r] += jnp.dot(x_ref[c], d_ref[n], preferred_element_type=F32)
        return carry

    lax.fori_loop(0, lax.div(count_ref[0, 0] + (BATCH - 1), BATCH), step, 0)


def backward_kernel(
    count_ref, row_hbm, col_hbm, d_ref, y_ref, result_ref, t_ref, result_hbm, row_ref, col_ref, sem
):
    loads = load_tables(row_hbm, col_hbm, row_ref, col_ref, sem)
    passed = pltpu.make_async_copy(result_ref, result_hbm, sem.at[2])
    passed.start()
    t_ref[...] = jnp.zeros_like(t_ref)
    for copy in loads:
        copy.wait()

    def step(i, carry):
        for s in range(BATCH):
            n = i * BATCH + s
            r, c = row_ref[0, 0, n], col_ref[0, 0, n]
            t_ref[c] += jnp.dot(d_ref[n], y_ref[r], preferred_element_type=F32)
        return carry

    lax.fori_loop(0, lax.div(count_ref[0, 0] + (BATCH - 1), BATCH), step, 0)
    passed.wait()


def block_sums(name, count, brow, bcol, dense, panel, blocks, result=None):
    smem, vmem = pl.BlockSpec(memory_space=pltpu.SMEM), pl.BlockSpec(memory_space=pltpu.VMEM)
    sums = jax.ShapeDtypeStruct((blocks, 128, 128), F32)
    params = pltpu.CompilerParams(vmem_limit_bytes=SUMS_VMEM)
    hbm = pl.BlockSpec(memory_space=pltpu.HBM)
    brow, bcol = in_hbm(brow, bcol)
    scratch = [
        pltpu.SMEM(brow.shape, jnp.int32),
        pltpu.SMEM(bcol.shape, jnp.int32),
        pltpu.SemaphoreType.DMA((3,)),
    ]
    if result is None:
        return pl.pallas_call(
            forward_kernel,
            in_specs=[smem, hbm, hbm] + [vmem] * 2,
            out_specs=vmem,
            scratch_shapes=scratch,
            out_shape=sums,
            compiler_params=params,
            name=name,
        )(count, brow, bcol, dense, panel)
    return pl.pallas_call(
        backward_kernel,
        in_specs=[smem, hbm, hbm] + [vmem] * 3,
        out_specs=(vmem, hbm),
        out_shape=(sums, jax.ShapeDtypeStruct(result.shape, result.dtype)),
        scratch_shapes=scratch,
        compiler_params=params,
        name=name,
    )(count, brow, bcol, dense, panel, result)


LEVELS = 32766.0


def blocks_of(ref):
    if len(ref.shape) == 2:
        return [(Ellipsis,)]
    return [(i, Ellipsis) for i in range(ref.shape[0])]


def encode(value, at, n, q_ref, s_ref):
    size = jnp.abs(value)
    most = jnp.maximum(jnp.max(size, axis=0, keepdims=True), 1e-30)
    level = jnp.sqrt(size * (1.0 / most)) * LEVELS + 0.5
    q_ref[at] = jnp.where(value < 0, -level, level).astype(jnp.int32).astype(jnp.int16)
    s_ref[n : n + 1] = most * (1.0 / (LEVELS * LEVELS))


def decode(at, n, q_ref, s_ref):
    level = q_ref[at].astype(jnp.int32).astype(F32)
    return level * jnp.abs(level) * s_ref[pl.ds(n, 1)]


class RingSum:
    def __init__(self, copies, value, me, plus, minus, q, scales):
        self.copies, self.value, self.q, self.scales = copies, value, q, scales
        self.me, self.p1, self.p2, self.p3 = me, lax.rem(me + 1, 4), lax.rem(me + 2, 4), lax.rem(me + 3, 4)
        self.plus, self.minus = plus, minus
        self.sent = {}

    def code(self, value, slot):
        for n, at in enumerate(blocks_of(self.q.at[slot])):
            encode(value(n, at), at, n, self.q.at[slot], self.scales.at[slot])

    def start(self, slot, device):
        self.sent[slot] = (
            self.copies.start(self.q.at[slot], self.q.at[slot + 6], device),
            self.copies.start(self.scales.at[slot], self.scales.at[slot + 6], device),
        )

    def got(self, slot, n, at):
        return decode(at, n, self.q.at[slot + 6], self.scales.at[slot + 6])

    def wait(self, *slots):
        for slot in slots:
            for copy in self.sent[slot]:
                copy.wait_recv()

    def code_far(self, half):
        self.code(self.value(self.p2, half), half)

    def send_far(self, half):
        self.start(half, (self.plus, self.minus)[half])

    def send_near(self, half):
        self.code(self.value((self.p3, self.p1)[half], half), 3 - half)
        self.start(3 - half, (self.minus, self.plus)[half])

    def pass_on(self, half):
        self.wait(half)
        own = self.value((self.p1, self.p3)[half], half)
        self.code(lambda n, at: own(n, at) + self.got(half, n, at), half + 4)
        self.start(half + 4, (self.plus, self.minus)[half])

    def arrive(self):
        self.wait(2, 3, 4, 5)

    def total(self, half, n, at):
        return (
            self.value(self.me, half)(n, at)
            + self.got(3 - half, n, at)
            + self.got(half + 4, n, at)
        )

    def drain(self):
        for pair in self.sent.values():
            for copy in pair:
                copy.wait_send()


def reduce_gather_kernel(
    t_ref, bias_ref, cot_ref, out_ref, g_ref, bsum_ref,
    first_q, first_scale, second_q, second_scale, sums, pair, send, recv,
):
    here = place()
    x, z, y, h, k = here
    xp, xm = shifted(here, dx=1), shifted(here, dx=3)
    yp, ym = shifted(here, dy=1), shifted(here, dy=3)
    zp = shifted(here, dz=1)
    barrier = pltpu.get_barrier_semaphore()
    for peer in (xp, xm, yp, ym, zp):
        pl.semaphore_signal(barrier, inc=1, device_id=peer, device_id_type=MESH)
    copies = Copies(send, recv)

    def ring_over_x(number, q, scale, value):
        return RingSum(copies, value, x, xp, xm, q.at[number], scale.at[number])

    def ring_over_y(number, q, scale, value):
        return RingSum(copies, value, y, yp, ym, q.at[number], scale.at[number])

    def part_a(b):
        rows = slice(b * 128, (b + 1) * 128)
        return lambda p, half: lambda n, at: t_ref.at[p, half, :, rows, :][at]

    def part_b(b):
        rows = slice((2 + b) * 128, (3 + b) * 128)
        return lambda p, half: lambda n, at: t_ref.at[:, half, p, rows, :][at]

    def then(ring):
        return lambda p, half: lambda n, at: ring.total(half, p, (p, Ellipsis))

    first, second = [], []
    for b in range(2):
        over_x = ring_over_x(2 * b, first_q, first_scale, part_a(b))
        over_y = ring_over_y(2 * b + 1, first_q, first_scale, part_b(b))
        first.append((over_x, over_y))
        second.append(
            (
                ring_over_y(2 * b, second_q, second_scale, then(over_x)),
                ring_over_x(2 * b + 1, second_q, second_scale, then(over_y)),
            )
        )

    def each(rings, *steps):
        for half in range(2):
            for ring in rings:
                for step in steps:
                    getattr(ring, step)(half)

    def arrive(rings):
        for ring in rings:
            ring.arrive()

    def start(rings):
        each(rings, "code_far", "send_far")
        each(rings, "send_near")

    other = 1 - z

    def pair_up(b):
        for i, ring in enumerate(second[b]):
            for half in range(2):
                sums[b, half, i] = ring.total(half, 0, (Ellipsis,))
        return copies.start(sums.at[b, other], pair.at[b], zp)

    bias = bias_ref[...]

    def owner(b, lost):
        for i in range(2):
            pre = (sums[b, z, i] + pair[b, i]).T + bias
            rows = slice((2 * i + b) * 128, (2 * i + b + 1) * 128)
            out_ref[rows] = jnp.maximum(pre, 0.0).astype(BF16)
            grad = jnp.where(pre > 0, cot_ref[rows].astype(F32), 0.0)
            lost = lost + jnp.sum(grad, axis=0, keepdims=True)
            g_ref[x, z, y, rows] = grad.astype(BF16)
        return lost

    x1, x3 = lax.rem(x + 1, 4), lax.rem(x + 3, 4)
    y1, y3 = lax.rem(y + 1, 4), lax.rem(y + 3, 4)

    def rows_of(b):
        return pl.ds(b * 128, 128), pl.ds((2 + b) * 128, 128)

    def over_z(b):
        return [
            copies.start(g_ref.at[x, z, y, rows], g_ref.at[x, z, y, rows], zp) for rows in rows_of(b)
        ]

    def near(b, sent):
        ra, rb = rows_of(b)
        sent[0].wait_recv()
        ring_a = RingGather(
            copies, g_ref.at[x, :, y, ra], g_ref.at[x, 0, y3, ra], g_ref.at[x, 1, y1, ra], yp, ym
        )
        sent[1].wait_recv()
        ring_b = RingGather(
            copies, g_ref.at[x, :, y, rb], g_ref.at[x3, 0, y, rb], g_ref.at[x1, 1, y, rb], xp, xm
        )
        return ring_a, ring_b

    def far(b, rings):
        ra, rb = rows_of(b)
        rings[0].arrive()
        ring_a = RingGather(
            copies, g_ref.at[x, :, :, ra], g_ref.at[x3, 0, :, ra], g_ref.at[x1, 1, :, ra], xp, xm
        )
        rings[1].arrive()
        ring_b = RingGather(
            copies, g_ref.at[:, :, y, rb], g_ref.at[:, 0, y3, rb], g_ref.at[:, 1, y1, rb], yp, ym
        )
        return ring_a, ring_b

    def pass_on(rings):
        for ring in rings:
            ring.pass_on()

    each(first[0], "code_far")
    pl.semaphore_wait(barrier, 5)
    each(first[0], "send_far")
    each(first[0], "send_near")
    start(first[1])
    each(first[0], "pass_on")
    arrive(first[0])
    start(second[0])
    each(first[1], "pass_on")
    each(second[0], "pass_on")
    arrive(first[1])
    start(second[1])
    arrive(second[0])
    pair_0 = pair_up(0)
    each(second[1], "pass_on")
    pair_0.wait()
    lost = owner(0, jnp.zeros((1, 128), F32))
    z_0 = over_z(0)
    arrive(second[1])
    pair_1 = pair_up(1)
    near_0 = near(0, z_0)
    pair_1.wait()
    bsum_ref[...] = owner(1, lost)
    z_1 = over_z(1)
    pass_on(near_0)
    near_1 = near(1, z_1)
    far_0 = far(0, near_0)
    pass_on(near_1)
    far_1 = far(1, near_1)
    pass_on(far_0)
    pass_on(far_1)
    arrive(far_0)
    arrive(far_1)
    for copy in z_0 + z_1:
        copy.wait_send()
    for rings in first + second + [near_0, near_1, far_0, far_1]:
        for ring in rings:
            ring.drain()


def reduce_gather(totals, bias, cotangent):
    vmem = pl.BlockSpec(memory_space=pltpu.VMEM)
    return pl.pallas_call(
        reduce_gather_kernel,
        out_shape=(
            jax.ShapeDtypeStruct((512, 128), BF16),
            jax.ShapeDtypeStruct((4, 2, 4, 512, 128), BF16),
            jax.ShapeDtypeStruct((1, 128), F32),
        ),
        in_specs=[vmem] * 3,
        out_specs=(vmem,) * 3,
        scratch_shapes=[
            pltpu.VMEM((4, 12, 4, 128, 128), jnp.int16),
            pltpu.VMEM((4, 12, 8, 128), F32),
            pltpu.VMEM((4, 12, 128, 128), jnp.int16),
            pltpu.VMEM((4, 12, 8, 128), F32),
            pltpu.VMEM((2, 2, 2, 128, 128), F32),
            pltpu.VMEM((2, 2, 128, 128), F32),
            pltpu.SemaphoreType.DMA((140,)),
            pltpu.SemaphoreType.DMA((140,)),
        ],
        compiler_params=pltpu.CompilerParams(
            collective_id=0, has_side_effects=True, vmem_limit_bytes=REDUCE_VMEM
        ),
        name="reduce_gather",
    )(totals, bias, cotangent)


def finish_kernel(
    t_ref, feat_ref, weight_ref, bsum_ref, gf_ref, gw_ref, gb_ref,
    from_core, outgoing, from_chip, local, plane_parts, total, line_parts, whole,
    lost, plane_lost, total_lost, line_lost, send, recv,
):
    here = place()
    x, z, y, h, k = here
    mine, line = x * 4 + y, h * 2 + z
    plane = [
        (shifted(here, dx=dx, dy=dy), lax.rem(x + dx, 4) * 4 + lax.rem(y + dy, 4))
        for dx in range(4)
        for dy in range(4)
        if (dx, dy) != (0, 0)
    ]
    column = [shifted(here, dz=dz, dh=dh) for dh in range(4) for dz in range(2) if (dz, dh) != (0, 0)]
    partner = shifted(here, dk=1)
    barrier = pltpu.get_barrier_semaphore()
    for peer in [partner] + column + [p for p, _ in plane]:
        pl.semaphore_signal(barrier, inc=1, device_id=peer, device_id_type=MESH)
    lost[...] = jnp.concatenate([bsum_ref[...], jnp.zeros((7, 128), F32)], axis=0)
    pl.semaphore_wait(barrier, 23)
    copies = Copies(send, recv)

    other = 1 - k
    pairs = {}
    for dh in (2, 1, 3, 0):
        to = lax.rem(h + dh, 4)
        pairs[dh] = copies.start(t_ref.at[to, other], from_core.at[to], partner)
    above, below = shifted(here, dh=1), shifted(here, dh=3)
    chips = []

    def both(dh, part):
        to = lax.rem(h + dh, 4)
        return t_ref[to, k, part] + from_core[to, part]

    def send(value, slot, device):
        outgoing[slot] = value.astype(BF16)
        chips.append(copies.start(outgoing.at[slot], from_chip.at[slot], device))

    upper, lower = slice(0, 256), slice(256, 512)
    pairs[2].wait_recv()
    send(both(2, upper), 0, above)
    send(both(2, lower), 1, below)
    pairs[1].wait_recv()
    send(both(1, lower), 2, above)
    pairs[3].wait_recv()
    send(both(3, upper), 3, below)
    pairs[0].wait_recv()
    bias_plane = [copies.start(lost, plane_lost.at[mine], p) for p, _ in plane]
    plane_lost[mine] = lost[...]
    chips[0].wait_recv()
    send(both(1, upper) + from_chip[0].astype(F32), 4, above)
    chips[1].wait_recv()
    send(both(3, lower) + from_chip[1].astype(F32), 5, below)
    for copy in bias_plane:
        copy.wait_recv()
    total_lost[0] = sum_of(plane_lost)
    bias_line = [copies.start(total_lost.at[0], total_lost.at[1], partner)]
    bias_line[0].wait_recv()
    total_lost[2] = total_lost[0] + total_lost[1]
    bias_line += [copies.start(total_lost.at[2], line_lost.at[line], p) for p in column]
    line_lost[line] = total_lost[2]
    for copy in chips[2:]:
        copy.wait_recv()
    own = jnp.concatenate(
        [
            both(0, upper) + from_chip[3].astype(F32) + from_chip[4].astype(F32),
            both(0, lower) + from_chip[2].astype(F32) + from_chip[5].astype(F32),
        ],
        axis=0,
    )
    grad = own.astype(BF16)
    local[...] = lax.dot_general(
        feat_ref[...], grad, (((0,), (0,)), ((), ())), preferred_element_type=F32
    )

    def rows(i):
        return pl.ds(pl.multiple_of(i * 8, 8), 8)

    sent = [copies.start(local.at[rows(i)], plane_parts.at[mine], p) for p, i in plane]
    plane_parts[mine] = local[rows(mine)]
    gf_ref[...] = lax.dot_general(
        grad, weight_ref[...], (((1,), (1,)), ((), ())), preferred_element_type=F32
    ).astype(BF16)
    scale = 131072.0**-0.5
    for copy in bias_line[1:]:
        copy.wait_recv()
    gb_ref[...] = sum_of(line_lost)[0:1] * scale
    for copy in sent:
        copy.wait_recv()
    total[0] = sum_of(plane_parts)
    spread = [copies.start(total.at[0], total.at[1], partner)]
    spread[0].wait_recv()
    total[2] = total[0] + total[1]
    spread += [copies.start(total.at[2], line_parts.at[line], p) for p in column]
    line_parts[line] = total[2]
    for copy in spread[1:]:
        copy.wait_recv()
    whole[rows(mine)] = sum_of(line_parts) * scale
    back = [copies.start(whole.at[rows(mine)], whole.at[rows(mine)], p) for p, _ in plane]
    for copy in back:
        copy.wait_recv()
    gw_ref[...] = whole[...]
    for copy in [pairs[dh] for dh in range(4)] + bias_plane + chips + bias_line + sent + spread + back:
        copy.wait_send()


def sum_of(ref):
    parts = [ref[i] for i in range(ref.shape[0])]
    while len(parts) > 1:
        parts = [a + b for a, b in zip(parts[::2], parts[1::2])]
    return parts[0]


def finish(partial, features, weight, bias_sum):
    vmem = pl.BlockSpec(memory_space=pltpu.VMEM)
    sums = [
        pltpu.VMEM((16, 8, 128), F32),
        pltpu.VMEM((3, 8, 128), F32),
        pltpu.VMEM((8, 8, 128), F32),
    ]
    return pl.pallas_call(
        finish_kernel,
        out_shape=(
            jax.ShapeDtypeStruct((512, 128), BF16),
            jax.ShapeDtypeStruct((128, 128), F32),
            jax.ShapeDtypeStruct((1, 128), F32),
        ),
        in_specs=[vmem] * 4,
        out_specs=(vmem,) * 3,
        scratch_shapes=[
            pltpu.VMEM((4, 512, 128), F32),
            pltpu.VMEM((6, 256, 128), BF16),
            pltpu.VMEM((6, 256, 128), BF16),
            pltpu.VMEM((128, 128), F32),
            *sums,
            pltpu.VMEM((128, 128), F32),
            pltpu.VMEM((8, 128), F32),
            *sums,
            pltpu.SemaphoreType.DMA((85,)),
            pltpu.SemaphoreType.DMA((85,)),
        ],
        compiler_params=pltpu.CompilerParams(
            collective_id=1, has_side_effects=True, vmem_limit_bytes=FINISH_VMEM
        ),
        name="finish",
    )(partial, features, weight, bias_sum)


def shards(
    features, weight, bias, cotangent, block_count, block_rows, block_cols, edge_offsets, edge_weight
):
    tables = (block_count, block_rows, block_cols)
    dense, panel = prepare(block_count, edge_offsets, edge_weight, features, weight)
    totals = block_sums("forward", *tables, dense, panel.reshape(32, 128, 128), 128)
    output, grads, bias_sum = reduce_gather(
        totals.reshape(4, 2, 4, 512, 128), bias.reshape(1, 128), cotangent
    )
    partial, output = block_sums(
        "backward", *tables, dense, grads.reshape(128, 128, 128), 32, output
    )
    grad_features, grad_weight, grad_bias = finish(
        partial.reshape(4, 2, 512, 128), features, weight, bias_sum
    )
    return (output, grad_features, grad_weight, grad_bias.reshape(128))


def solution(mesh):
    return jax.shard_map(
        shards,
        mesh=mesh,
        in_specs=(
            P(("row", "col"), None),
            P(),
            P(),
            P(("row", "col"), None),
            P("row", "col"),
            P("row", "col", None),
            P("row", "col", None),
            P("row", "col", None, None),
            P("row", "col", None, None),
        ),
        out_specs=(P(("row", "col"), None), P(("row", "col"), None), P(), P()),
        check_vma=False,
    )
```

```python
import math

import jax
import jax.numpy as jnp
from jax import lax
from jax.experimental import pallas as pl
from jax.experimental.pallas import tpu as pltpu
from jax.sharding import PartitionSpec as P

MESH = pl.DeviceIdType.MESH
F32 = jnp.float32
BF16 = jnp.bfloat16
BATCH = 64
SUM_BATCH = 128
PREP_VMEM = 4 << 20
SUMS_VMEM = 4 << 20
REDUCE_VMEM = 16 << 20
FINISH_VMEM = 12 << 20


def place():
    r = lax.axis_index("row")
    c = lax.axis_index("col")
    return lax.div(c, 8), lax.rem(lax.div(c, 4), 2), lax.rem(c, 4), lax.div(r, 2), lax.rem(r, 2)


def shifted(here, dx=0, dz=0, dy=0, dh=0, dk=0):
    x, z, y, h, k = here
    x, z, y = lax.rem(x + dx, 4), lax.rem(z + dz, 2), lax.rem(y + dy, 4)
    h, k = lax.rem(h + dh, 4), lax.rem(k + dk, 2)
    return (h * 2 + k, x * 8 + z * 4 + y)


class RingGather:
    def __init__(self, copies, mine, from_minus, from_plus, plus, minus):
        self.copies, self.plus, self.minus = copies, plus, minus
        self.from_minus, self.from_plus = from_minus, from_plus
        self.sent = [copies.start(mine, mine, plus), copies.start(mine, mine, minus)]

    def pass_on(self):
        self.sent[0].wait_recv()
        self.sent.append(self.copies.start(self.from_minus, self.from_minus, self.plus))
        self.sent[1].wait_recv()
        self.sent.append(self.copies.start(self.from_plus, self.from_plus, self.minus))

    def arrive(self):
        self.sent[2].wait_recv()
        self.sent[3].wait_recv()

    def drain(self):
        for copy in self.sent:
            copy.wait_send()


class Copies:
    def __init__(self, send, recv):
        self.send, self.recv, self.used = send, recv, 0

    def start(self, src, dst, device):
        copy = pltpu.make_async_remote_copy(
            src_ref=src,
            dst_ref=dst,
            send_sem=self.send.at[self.used],
            recv_sem=self.recv.at[self.used],
            device_id=device,
            device_id_type=MESH,
        )
        self.used += 1
        copy.start()
        return copy


def prepare_kernel(
    count_ref, off_hbm, w_hbm, feat_hbm, weight_hbm, d_ref, panel_ref,
    off_ref, w_ref, feat_ref, weight_ref, load, send, recv,
):
    loads = [
        pltpu.make_async_copy(source, target, load.at[i])
        for i, (source, target) in enumerate(
            (
                (feat_hbm, feat_ref),
                (weight_hbm, weight_ref),
                (off_hbm.at[0, 0], off_ref),
                (w_hbm.at[0, 0], w_ref),
            )
        )
    ]
    for copy in loads:
        copy.start()
    here = place()
    x, z, y, h, k = here
    r = lax.axis_index("row")
    partner = shifted(here, dk=1)
    above, below = shifted(here, dh=1), shifted(here, dh=3)
    barrier = pltpu.get_barrier_semaphore()
    for peer in (partner, above, below):
        pl.semaphore_signal(barrier, inc=1, device_id=peer, device_id_type=MESH)
    loads[0].wait()
    loads[1].wait()
    for b in range(4):
        rows = slice(b * 128, (b + 1) * 128)
        projected = jnp.dot(feat_ref[rows], weight_ref[...], preferred_element_type=F32)
        panel_ref[r, b] = projected.T.astype(BF16)
    pl.semaphore_wait(barrier, 3)
    copies = Copies(send, recv)
    h1, h2, h3 = (lax.rem(h + i, 4) * 2 + k for i in (1, 2, 3))
    ring = RingGather(
        copies, panel_ref.at[r], panel_ref.at[h3, 0:2], panel_ref.at[h1, 2:4], above, below
    )

    def pass_over(i):
        return copies.start(panel_ref.at[i], panel_ref.at[i], partner)

    beside = [pass_over(r)]

    loads[2].wait()
    loads[3].wait()
    count = count_ref[0, 0]
    ids = (
        lax.broadcasted_iota(jnp.int32, (8, 16, 128), 0) * 16
        + lax.broadcasted_iota(jnp.int32, (8, 16, 128), 1)
    ).astype(F32).astype(BF16)
    one = jnp.ones((8, 16, 128), BF16)
    zero = jnp.zeros((8, 16, 128), BF16)

    def row(a, s):
        return jnp.broadcast_to(a[s : s + 1], (16, 128)).astype(BF16)[None]

    def densify(step, carry):
        start = pl.multiple_of(step * BATCH, BATCH)
        off = off_ref[pl.ds(start, BATCH)]
        hi = lax.shift_right_logical(off, 7).astype(F32)
        lo = lax.bitwise_and(off, 127).astype(F32)
        slot = start + lax.broadcasted_iota(jnp.int32, off.shape, 0)
        w = jnp.where(slot < count, w_ref[pl.ds(start, BATCH)].astype(F32), 0.0)
        for s in range(BATCH):
            left = jnp.where(ids == row(hi, s), jnp.broadcast_to(row(w, s), (8, 16, 128)), zero)
            right = jnp.where(ids == row(lo, s), one, zero)
            d_ref[start + s] = lax.dot_general(
                right.reshape(128, 128),
                left.reshape(128, 128),
                (((1,), (1,)), ((), ())),
                preferred_element_type=F32,
            ).astype(BF16)
        return carry

    steps = d_ref.shape[0] // BATCH
    lax.fori_loop(0, steps // 2, densify, 0)
    ring.pass_on()
    beside += [pass_over(h3), pass_over(h1)]
    lax.fori_loop(steps // 2, steps * 7 // 8, densify, 0)
    ring.arrive()
    beside.append(pass_over(h2))
    lax.fori_loop(steps * 7 // 8, steps, densify, 0)
    for copy in beside:
        copy.wait()
    ring.drain()


def prepare(count, offsets, weights, features, weight):
    slots = offsets.shape[2]
    vmem = pl.BlockSpec(memory_space=pltpu.VMEM)
    hbm = pl.BlockSpec(memory_space=pltpu.HBM)
    return pl.pallas_call(
        prepare_kernel,
        out_shape=(
            jax.ShapeDtypeStruct((slots, 128, 128), BF16),
            jax.ShapeDtypeStruct((8, 4, 128, 128), BF16),
        ),
        in_specs=[pl.BlockSpec(memory_space=pltpu.SMEM)] + [hbm] * 4,
        out_specs=(vmem,) * 2,
        scratch_shapes=[
            pltpu.VMEM((slots, 128), jnp.int32),
            pltpu.VMEM((slots, 128), BF16),
            pltpu.VMEM((512, 128), BF16),
            pltpu.VMEM((128, 128), BF16),
            pltpu.SemaphoreType.DMA((4,)),
            pltpu.SemaphoreType.DMA((8,)),
            pltpu.SemaphoreType.DMA((8,)),
        ],
        compiler_params=pltpu.CompilerParams(
            collective_id=2, has_side_effects=True, vmem_limit_bytes=PREP_VMEM
        ),
        name="prepare",
    )(count, *in_hbm(offsets, weights, features, weight))


def in_hbm(*arrays):
    return [pltpu.with_memory_space_constraint(a, pltpu.HBM) for a in arrays]


def load_tables(row_hbm, col_hbm, row_ref, col_ref, sem):
    loads = [
        pltpu.make_async_copy(row_hbm, row_ref, sem.at[0]),
        pltpu.make_async_copy(col_hbm, col_ref, sem.at[1]),
    ]
    for copy in loads:
        copy.start()
    return loads


def forward_kernel(count_ref, row_hbm, col_hbm, d_ref, x_ref, t_ref, row_ref, col_ref, sem):
    loads = load_tables(row_hbm, col_hbm, row_ref, col_ref, sem)
    t_ref[...] = jnp.zeros_like(t_ref)
    for copy in loads:
        copy.wait()

    def step(i, carry):
        for s in range(SUM_BATCH):
            n = i * SUM_BATCH + s
            r, c = row_ref[0, 0, n], col_ref[0, 0, n]
            t_ref[r] += jnp.dot(x_ref[c], d_ref[n], preferred_element_type=F32)
        return carry

    lax.fori_loop(0, lax.div(count_ref[0, 0] + (SUM_BATCH - 1), SUM_BATCH), step, 0)


def backward_kernel(
    count_ref, row_hbm, col_hbm, d_ref, y_ref, result_ref, t_ref, result_hbm, row_ref, col_ref, sem
):
    loads = load_tables(row_hbm, col_hbm, row_ref, col_ref, sem)
    passed = pltpu.make_async_copy(result_ref, result_hbm, sem.at[2])
    passed.start()
    t_ref[...] = jnp.zeros_like(t_ref)
    for copy in loads:
        copy.wait()

    def step(i, carry):
        for s in range(SUM_BATCH):
            n = i * SUM_BATCH + s
            r, c = row_ref[0, 0, n], col_ref[0, 0, n]
            t_ref[c] += jnp.dot(d_ref[n], y_ref[r], preferred_element_type=F32)
        return carry

    lax.fori_loop(0, lax.div(count_ref[0, 0] + (SUM_BATCH - 1), SUM_BATCH), step, 0)
    passed.wait()


def block_sums(name, count, brow, bcol, dense, panel, blocks, result=None):
    smem, vmem = pl.BlockSpec(memory_space=pltpu.SMEM), pl.BlockSpec(memory_space=pltpu.VMEM)
    sums = jax.ShapeDtypeStruct((blocks, 128, 128), F32)
    params = pltpu.CompilerParams(vmem_limit_bytes=SUMS_VMEM)
    hbm = pl.BlockSpec(memory_space=pltpu.HBM)
    brow, bcol = in_hbm(brow, bcol)
    scratch = [
        pltpu.SMEM(brow.shape, jnp.int32),
        pltpu.SMEM(bcol.shape, jnp.int32),
        pltpu.SemaphoreType.DMA((3,)),
    ]
    if result is None:
        return pl.pallas_call(
            forward_kernel,
            in_specs=[smem, hbm, hbm] + [vmem] * 2,
            out_specs=vmem,
            scratch_shapes=scratch,
            out_shape=sums,
            compiler_params=params,
            name=name,
        )(count, brow, bcol, dense, panel)
    return pl.pallas_call(
        backward_kernel,
        in_specs=[smem, hbm, hbm] + [vmem] * 3,
        out_specs=(vmem, hbm),
        out_shape=(sums, jax.ShapeDtypeStruct(result.shape, result.dtype)),
        scratch_shapes=scratch,
        compiler_params=params,
        name=name,
    )(count, brow, bcol, dense, panel, result)


LEVELS = 32766.0
STEPS = 64.0 / math.log(2.0)


def block_rows_of(n):
    return pl.ds(n * 128 if isinstance(n, int) else pl.multiple_of(n * 128, 128), 128)


def encode(value, n, q_ref):
    size = jnp.abs(value)
    most = jnp.maximum(jnp.max(size, axis=0, keepdims=True), 1e-30)
    step = jnp.ceil(jnp.log(most) * STEPS)
    level = jnp.sqrt(size * jnp.exp(step * (-1.0 / STEPS))) * LEVELS + 0.5
    q_ref[block_rows_of(n)] = jnp.where(value < 0, -level, level).astype(jnp.int32).astype(jnp.int16)
    return step


def decode(n, q_ref, s_ref):
    level = q_ref[block_rows_of(n)].astype(jnp.int32).astype(F32)
    return level * jnp.abs(level) * s_ref[pl.ds(n, 1)]


class RingSum:
    def __init__(self, copies, value, me, plus, minus, q, scales, blocks):
        self.blocks = blocks
        self.copies, self.value, self.q, self.scales = copies, value, q, scales
        self.me, self.p1, self.p2, self.p3 = me, lax.rem(me + 1, 4), lax.rem(me + 2, 4), lax.rem(me + 3, 4)
        self.plus, self.minus = plus, minus
        self.sent = {}

    def code(self, value, slot):
        q = self.q.at[slot]
        steps = [encode(value(n, at), n, q) for n, at in enumerate(self.blocks)]
        steps.append(jnp.zeros((16 - len(steps), 128), F32))
        tail = jnp.concatenate(steps, axis=0)
        q[pl.ds(len(self.blocks) * 128, 16)] = tail.astype(jnp.int32).astype(jnp.int16)

    def start(self, slot, device):
        self.sent[slot] = self.copies.start(self.q.at[slot], self.q.at[slot + 6], device)

    def got(self, slot, n):
        return decode(n, self.q.at[slot + 6], self.scales.at[slot])

    def wait(self, *slots):
        for slot in slots:
            self.sent[slot].wait_recv()
            tail = self.q[slot + 6, pl.ds(len(self.blocks) * 128, 16)].astype(jnp.int32).astype(F32)
            self.scales[slot] = jnp.exp(tail * (1.0 / STEPS)) * (1.0 / (LEVELS * LEVELS))

    def code_far(self, half):
        self.code(self.value(self.p2, half), half)

    def send_far(self, half):
        self.start(half, (self.plus, self.minus)[half])

    def send_near(self, half):
        self.code(self.value((self.p3, self.p1)[half], half), 3 - half)
        self.start(3 - half, (self.minus, self.plus)[half])

    def pass_on(self, half):
        self.wait(half)
        own = self.value((self.p1, self.p3)[half], half)
        self.code(lambda n, at: own(n, at) + self.got(half, n), half + 4)
        self.start(half + 4, (self.plus, self.minus)[half])

    def arrive(self):
        self.wait(2, 3, 4, 5)

    def total(self, half, n, at):
        return (
            self.value(self.me, half)(n, at)
            + self.got(3 - half, n)
            + self.got(half + 4, n)
        )

    def drain(self):
        for copy in self.sent.values():
            copy.wait_send()


def reduce_gather_kernel(
    t_ref, bias_ref, cot_ref, out_ref, g_ref, bsum_ref,
    first_q, first_scale, second_q, second_scale, sums, pair, send, recv,
):
    here = place()
    x, z, y, h, k = here
    xp, xm = shifted(here, dx=1), shifted(here, dx=3)
    yp, ym = shifted(here, dy=1), shifted(here, dy=3)
    zp = shifted(here, dz=1)
    barrier = pltpu.get_barrier_semaphore()
    for peer in (xp, xm, yp, ym, zp):
        pl.semaphore_signal(barrier, inc=1, device_id=peer, device_id_type=MESH)
    copies = Copies(send, recv)

    four, one = [(i, Ellipsis) for i in range(4)], [(Ellipsis,)]

    def ring_over_x(number, q, scale, blocks, value):
        return RingSum(copies, value, x, xp, xm, q.at[number], scale.at[number], blocks)

    def ring_over_y(number, q, scale, blocks, value):
        return RingSum(copies, value, y, yp, ym, q.at[number], scale.at[number], blocks)

    def part_a(b):
        rows = slice(b * 128, (b + 1) * 128)
        return lambda p, half: lambda n, at: t_ref.at[p, half, :, rows, :][at]

    def part_b(b):
        rows = slice((2 + b) * 128, (3 + b) * 128)
        return lambda p, half: lambda n, at: t_ref.at[:, half, p, rows, :][at]

    def then(ring):
        return lambda p, half: lambda n, at: ring.total(half, p, (p, Ellipsis))

    first, second = [], []
    for b in range(2):
        over_x = ring_over_x(2 * b, first_q, first_scale, four, part_a(b))
        over_y = ring_over_y(2 * b + 1, first_q, first_scale, four, part_b(b))
        first.append((over_x, over_y))
        second.append(
            (
                ring_over_y(2 * b, second_q, second_scale, one, then(over_x)),
                ring_over_x(2 * b + 1, second_q, second_scale, one, then(over_y)),
            )
        )

    def each(rings, *steps):
        for half in range(2):
            for ring in rings:
                for step in steps:
                    getattr(ring, step)(half)

    def arrive(rings):
        for ring in rings:
            ring.arrive()

    def start(rings):
        each(rings, "code_far", "send_far")
        each(rings, "send_near")

    other = 1 - z

    def pair_up(b):
        for i, ring in enumerate(second[b]):
            for half in range(2):
                sums[b, half, i] = ring.total(half, 0, (Ellipsis,))
        return copies.start(sums.at[b, other], pair.at[b], zp)

    bias = bias_ref[...]

    def owner(b, lost):
        for i in range(2):
            pre = (sums[b, z, i] + pair[b, i]).T + bias
            rows = slice((2 * i + b) * 128, (2 * i + b + 1) * 128)
            out_ref[rows] = jnp.maximum(pre, 0.0).astype(BF16)
            grad = jnp.where(pre > 0, cot_ref[rows].astype(F32), 0.0)
            lost = lost + jnp.sum(grad, axis=0, keepdims=True)
            g_ref[x, z, y, rows] = grad.astype(BF16)
        return lost

    x1, x3 = lax.rem(x + 1, 4), lax.rem(x + 3, 4)
    y1, y3 = lax.rem(y + 1, 4), lax.rem(y + 3, 4)

    def rows_of(b):
        return pl.ds(b * 128, 128), pl.ds((2 + b) * 128, 128)

    def over_z(b):
        return [
            copies.start(g_ref.at[x, z, y, rows], g_ref.at[x, z, y, rows], zp) for rows in rows_of(b)
        ]

    def near(b, sent):
        ra, rb = rows_of(b)
        sent[0].wait_recv()
        ring_a = RingGather(
            copies, g_ref.at[x, :, y, ra], g_ref.at[x, 0, y3, ra], g_ref.at[x, 1, y1, ra], yp, ym
        )
        sent[1].wait_recv()
        ring_b = RingGather(
            copies, g_ref.at[x, :, y, rb], g_ref.at[x3, 0, y, rb], g_ref.at[x1, 1, y, rb], xp, xm
        )
        return ring_a, ring_b

    def far(b, rings):
        ra, rb = rows_of(b)
        rings[0].arrive()
        ring_a = RingGather(
            copies, g_ref.at[x, :, :, ra], g_ref.at[x3, 0, :, ra], g_ref.at[x1, 1, :, ra], xp, xm
        )
        rings[1].arrive()
        ring_b = RingGather(
            copies, g_ref.at[:, :, y, rb], g_ref.at[:, 0, y3, rb], g_ref.at[:, 1, y1, rb], yp, ym
        )
        return ring_a, ring_b

    def pass_on(rings):
        for ring in rings:
            ring.pass_on()

    each(first[0], "code_far")
    pl.semaphore_wait(barrier, 5)
    each(first[0], "send_far")
    each(first[0], "send_near")
    start(first[1])
    each(first[0], "pass_on")
    arrive(first[0])
    start(second[0])
    each(first[1], "pass_on")
    each(second[0], "pass_on")
    arrive(first[1])
    start(second[1])
    arrive(second[0])
    pair_0 = pair_up(0)
    each(second[1], "pass_on")
    pair_0.wait()
    lost = owner(0, jnp.zeros((1, 128), F32))
    z_0 = over_z(0)
    arrive(second[1])
    pair_1 = pair_up(1)
    near_0 = near(0, z_0)
    pair_1.wait()
    bsum_ref[...] = owner(1, lost)
    z_1 = over_z(1)
    pass_on(near_0)
    near_1 = near(1, z_1)
    far_0 = far(0, near_0)
    pass_on(near_1)
    far_1 = far(1, near_1)
    pass_on(far_0)
    pass_on(far_1)
    arrive(far_0)
    arrive(far_1)
    for copy in z_0 + z_1:
        copy.wait_send()
    for rings in first + second + [near_0, near_1, far_0, far_1]:
        for ring in rings:
            ring.drain()


def reduce_gather(totals, bias, cotangent):
    vmem = pl.BlockSpec(memory_space=pltpu.VMEM)
    return pl.pallas_call(
        reduce_gather_kernel,
        out_shape=(
            jax.ShapeDtypeStruct((512, 128), BF16),
            jax.ShapeDtypeStruct((4, 2, 4, 512, 128), BF16),
            jax.ShapeDtypeStruct((1, 128), F32),
        ),
        in_specs=[vmem] * 3,
        out_specs=(vmem,) * 3,
        scratch_shapes=[
            pltpu.VMEM((4, 12, 4 * 128 + 16, 128), jnp.int16),
            pltpu.VMEM((4, 6, 16, 128), F32),
            pltpu.VMEM((4, 12, 128 + 16, 128), jnp.int16),
            pltpu.VMEM((4, 6, 16, 128), F32),
            pltpu.VMEM((2, 2, 2, 128, 128), F32),
            pltpu.VMEM((2, 2, 128, 128), F32),
            pltpu.SemaphoreType.DMA((90,)),
            pltpu.SemaphoreType.DMA((90,)),
        ],
        compiler_params=pltpu.CompilerParams(
            collective_id=0, has_side_effects=True, vmem_limit_bytes=REDUCE_VMEM
        ),
        name="reduce_gather",
    )(totals, bias, cotangent)


def finish_kernel(
    t_ref, feat_ref, weight_ref, bsum_ref, gf_ref, gw_ref, gb_ref,
    from_core, outgoing, from_chip, local, plane_parts, total, line_parts, whole,
    lost, plane_lost, total_lost, line_lost, send, recv,
):
    here = place()
    x, z, y, h, k = here
    mine, line = x * 4 + y, h * 2 + z
    plane = [
        (shifted(here, dx=dx, dy=dy), lax.rem(x + dx, 4) * 4 + lax.rem(y + dy, 4))
        for dx in range(4)
        for dy in range(4)
        if (dx, dy) != (0, 0)
    ]
    column = [shifted(here, dz=dz, dh=dh) for dh in range(4) for dz in range(2) if (dz, dh) != (0, 0)]
    partner = shifted(here, dk=1)
    barrier = pltpu.get_barrier_semaphore()
    for peer in [partner] + column + [p for p, _ in plane]:
        pl.semaphore_signal(barrier, inc=1, device_id=peer, device_id_type=MESH)
    lost[...] = jnp.concatenate([bsum_ref[...], jnp.zeros((7, 128), F32)], axis=0)
    pl.semaphore_wait(barrier, 23)
    copies = Copies(send, recv)

    other = 1 - k
    pairs = {}
    for dh in (2, 1, 3, 0):
        to = lax.rem(h + dh, 4)
        pairs[dh] = copies.start(t_ref.at[to, other], from_core.at[to], partner)
    above, below = shifted(here, dh=1), shifted(here, dh=3)
    chips = []

    def both(dh, part):
        to = lax.rem(h + dh, 4)
        return t_ref[to, k, part] + from_core[to, part]

    def send(value, slot, device):
        outgoing[slot] = value.astype(BF16)
        chips.append(copies.start(outgoing.at[slot], from_chip.at[slot], device))

    upper, lower = slice(0, 256), slice(256, 512)
    pairs[2].wait_recv()
    send(both(2, upper), 0, above)
    send(both(2, lower), 1, below)
    pairs[1].wait_recv()
    send(both(1, lower), 2, above)
    pairs[3].wait_recv()
    send(both(3, upper), 3, below)
    pairs[0].wait_recv()
    bias_plane = [copies.start(lost, plane_lost.at[mine], p) for p, _ in plane]
    plane_lost[mine] = lost[...]
    chips[0].wait_recv()
    send(both(1, upper) + from_chip[0].astype(F32), 4, above)
    chips[1].wait_recv()
    send(both(3, lower) + from_chip[1].astype(F32), 5, below)
    for copy in bias_plane:
        copy.wait_recv()
    total_lost[0] = sum_of(plane_lost)
    bias_line = [copies.start(total_lost.at[0], total_lost.at[1], partner)]
    bias_line[0].wait_recv()
    total_lost[2] = total_lost[0] + total_lost[1]
    bias_line += [copies.start(total_lost.at[2], line_lost.at[line], p) for p in column]
    line_lost[line] = total_lost[2]
    for copy in chips[2:]:
        copy.wait_recv()
    own = jnp.concatenate(
        [
            both(0, upper) + from_chip[3].astype(F32) + from_chip[4].astype(F32),
            both(0, lower) + from_chip[2].astype(F32) + from_chip[5].astype(F32),
        ],
        axis=0,
    )
    grad = own.astype(BF16)
    local[...] = lax.dot_general(
        feat_ref[...], grad, (((0,), (0,)), ((), ())), preferred_element_type=F32
    )

    def rows(i):
        return pl.ds(pl.multiple_of(i * 8, 8), 8)

    sent = [copies.start(local.at[rows(i)], plane_parts.at[mine], p) for p, i in plane]
    plane_parts[mine] = local[rows(mine)]
    gf_ref[...] = lax.dot_general(
        grad, weight_ref[...], (((1,), (1,)), ((), ())), preferred_element_type=F32
    ).astype(BF16)
    scale = 131072.0**-0.5
    for copy in bias_line[1:]:
        copy.wait_recv()
    gb_ref[...] = sum_of(line_lost)[0:1] * scale
    for copy in sent:
        copy.wait_recv()
    total[0] = sum_of(plane_parts)
    spread = [copies.start(total.at[0], total.at[1], partner)]
    spread[0].wait_recv()
    total[2] = total[0] + total[1]
    spread += [copies.start(total.at[2], line_parts.at[line], p) for p in column]
    line_parts[line] = total[2]
    for copy in spread[1:]:
        copy.wait_recv()
    whole[rows(mine)] = sum_of(line_parts) * scale
    back = [copies.start(whole.at[rows(mine)], whole.at[rows(mine)], p) for p, _ in plane]
    for copy in back:
        copy.wait_recv()
    gw_ref[...] = whole[...]
    for copy in [pairs[dh] for dh in range(4)] + bias_plane + chips + bias_line + sent + spread + back:
        copy.wait_send()


def sum_of(ref):
    parts = [ref[i] for i in range(ref.shape[0])]
    while len(parts) > 1:
        parts = [a + b for a, b in zip(parts[::2], parts[1::2])]
    return parts[0]


def finish(partial, features, weight, bias_sum):
    vmem = pl.BlockSpec(memory_space=pltpu.VMEM)
    sums = [
        pltpu.VMEM((16, 8, 128), F32),
        pltpu.VMEM((3, 8, 128), F32),
        pltpu.VMEM((8, 8, 128), F32),
    ]
    return pl.pallas_call(
        finish_kernel,
        out_shape=(
            jax.ShapeDtypeStruct((512, 128), BF16),
            jax.ShapeDtypeStruct((128, 128), F32),
            jax.ShapeDtypeStruct((1, 128), F32),
        ),
        in_specs=[vmem] * 4,
        out_specs=(vmem,) * 3,
        scratch_shapes=[
            pltpu.VMEM((4, 512, 128), F32),
            pltpu.VMEM((6, 256, 128), BF16),
            pltpu.VMEM((6, 256, 128), BF16),
            pltpu.VMEM((128, 128), F32),
            *sums,
            pltpu.VMEM((128, 128), F32),
            pltpu.VMEM((8, 128), F32),
            *sums,
            pltpu.SemaphoreType.DMA((85,)),
            pltpu.SemaphoreType.DMA((85,)),
        ],
        compiler_params=pltpu.CompilerParams(
            collective_id=1, has_side_effects=True, vmem_limit_bytes=FINISH_VMEM
        ),
        name="finish",
    )(partial, features, weight, bias_sum)


def export_kernel(*refs):
    count = len(refs) // 2
    sem = refs[-1]
    copies = [
        pltpu.make_async_copy(refs[i], refs[count + i], sem.at[i]) for i in range(count)
    ]
    for copy in copies:
        copy.start()
    for copy in copies:
        copy.wait()


def export(*arrays):
    vmem, hbm = pl.BlockSpec(memory_space=pltpu.VMEM), pl.BlockSpec(memory_space=pltpu.HBM)
    return pl.pallas_call(
        export_kernel,
        in_specs=[vmem] * len(arrays),
        out_specs=(hbm,) * len(arrays),
        out_shape=tuple(jax.ShapeDtypeStruct(a.shape, a.dtype) for a in arrays),
        scratch_shapes=[pltpu.SemaphoreType.DMA((len(arrays),))],
        compiler_params=pltpu.CompilerParams(vmem_limit_bytes=1 << 20),
        name="export",
    )(*arrays)


def shards(
    features, weight, bias, cotangent, block_count, block_rows, block_cols, edge_offsets, edge_weight
):
    tables = (block_count, block_rows, block_cols)
    dense, panel = prepare(block_count, edge_offsets, edge_weight, features, weight)
    totals = block_sums("forward", *tables, dense, panel.reshape(32, 128, 128), 128)
    output, grads, bias_sum = reduce_gather(
        totals.reshape(4, 2, 4, 512, 128), bias.reshape(1, 128), cotangent
    )
    partial, output = block_sums(
        "backward", *tables, dense, grads.reshape(128, 128, 128), 32, output
    )
    grad_features, grad_weight, grad_bias = export(
        *finish(partial.reshape(4, 2, 512, 128), features, weight, bias_sum)
    )
    return (output, grad_features, grad_weight, grad_bias.reshape(128))


def solution(mesh):
    return jax.shard_map(
        shards,
        mesh=mesh,
        in_specs=(
            P(("row", "col"), None),
            P(),
            P(),
            P(("row", "col"), None),
            P("row", "col"),
            P("row", "col", None),
            P("row", "col", None),
            P("row", "col", None, None),
            P("row", "col", None, None),
        ),
        out_specs=(P(("row", "col"), None), P(("row", "col"), None), P(), P()),
        check_vma=False,
    )
```

```python
import math

import jax
import jax.numpy as jnp
from jax import lax
from jax.experimental import pallas as pl
from jax.experimental.pallas import tpu as pltpu
from jax.sharding import PartitionSpec as P

MESH = pl.DeviceIdType.MESH
F32 = jnp.float32
BF16 = jnp.bfloat16
BATCH = 64
SUM_BATCH = 128
PREP_VMEM = 4 << 20
SUMS_VMEM = 4 << 20
REDUCE_VMEM = 16 << 20
FINISH_VMEM = 12 << 20


def place():
    r = lax.axis_index("row")
    c = lax.axis_index("col")
    return lax.div(c, 8), lax.rem(lax.div(c, 4), 2), lax.rem(c, 4), lax.div(r, 2), lax.rem(r, 2)


def shifted(here, dx=0, dz=0, dy=0, dh=0, dk=0):
    x, z, y, h, k = here
    x, z, y = lax.rem(x + dx, 4), lax.rem(z + dz, 2), lax.rem(y + dy, 4)
    h, k = lax.rem(h + dh, 4), lax.rem(k + dk, 2)
    return (h * 2 + k, x * 8 + z * 4 + y)


class RingGather:
    def __init__(self, copies, mine, from_minus, from_plus, plus, minus):
        self.copies, self.plus, self.minus = copies, plus, minus
        self.from_minus, self.from_plus = from_minus, from_plus
        self.sent = [copies.start(mine, mine, plus), copies.start(mine, mine, minus)]

    def pass_on(self):
        self.sent[0].wait_recv()
        self.sent.append(self.copies.start(self.from_minus, self.from_minus, self.plus))
        self.sent[1].wait_recv()
        self.sent.append(self.copies.start(self.from_plus, self.from_plus, self.minus))

    def arrive(self):
        self.sent[2].wait_recv()
        self.sent[3].wait_recv()

    def drain(self):
        for copy in self.sent:
            copy.wait_send()


class Copies:
    def __init__(self, send, recv):
        self.send, self.recv, self.used = send, recv, 0

    def start(self, src, dst, device):
        copy = pltpu.make_async_remote_copy(
            src_ref=src,
            dst_ref=dst,
            send_sem=self.send.at[self.used],
            recv_sem=self.recv.at[self.used],
            device_id=device,
            device_id_type=MESH,
        )
        self.used += 1
        copy.start()
        return copy


def prepare_kernel(
    count_ref, off_hbm, w_hbm, feat_hbm, weight_hbm, d_ref, panel_ref,
    off_ref, w_ref, feat_ref, weight_ref, load, send, recv,
):
    loads = [
        pltpu.make_async_copy(source, target, load.at[i])
        for i, (source, target) in enumerate(
            (
                (feat_hbm, feat_ref),
                (weight_hbm, weight_ref),
                (off_hbm.at[0, 0], off_ref),
                (w_hbm.at[0, 0], w_ref),
            )
        )
    ]
    for copy in loads:
        copy.start()
    here = place()
    x, z, y, h, k = here
    r = lax.axis_index("row")
    partner = shifted(here, dk=1)
    above, below = shifted(here, dh=1), shifted(here, dh=3)
    barrier = pltpu.get_barrier_semaphore()
    for peer in (partner, above, below):
        pl.semaphore_signal(barrier, inc=1, device_id=peer, device_id_type=MESH)
    loads[0].wait()
    loads[1].wait()
    for b in range(4):
        rows = slice(b * 128, (b + 1) * 128)
        projected = jnp.dot(feat_ref[rows], weight_ref[...], preferred_element_type=F32)
        panel_ref[r, b] = projected.T.astype(BF16)
    pl.semaphore_wait(barrier, 3)
    copies = Copies(send, recv)
    h1, h2, h3 = (lax.rem(h + i, 4) * 2 + k for i in (1, 2, 3))
    ring = RingGather(
        copies, panel_ref.at[r], panel_ref.at[h3, 0:2], panel_ref.at[h1, 2:4], above, below
    )

    def pass_over(i):
        return copies.start(panel_ref.at[i], panel_ref.at[i], partner)

    beside = [pass_over(r)]

    loads[2].wait()
    loads[3].wait()
    count = count_ref[0, 0]
    ids = (
        lax.broadcasted_iota(jnp.int32, (8, 16, 128), 0) * 16
        + lax.broadcasted_iota(jnp.int32, (8, 16, 128), 1)
    ).astype(F32).astype(BF16)
    one = jnp.ones((8, 16, 128), BF16)
    zero = jnp.zeros((8, 16, 128), BF16)

    def row(a, s):
        return jnp.broadcast_to(a[s : s + 1], (16, 128)).astype(BF16)[None]

    def densify(step, carry):
        start = pl.multiple_of(step * BATCH, BATCH)
        off = off_ref[pl.ds(start, BATCH)]
        hi = lax.shift_right_logical(off, 7).astype(F32)
        lo = lax.bitwise_and(off, 127).astype(F32)
        slot = start + lax.broadcasted_iota(jnp.int32, off.shape, 0)
        w = jnp.where(slot < count, w_ref[pl.ds(start, BATCH)].astype(F32), 0.0)
        for s in range(BATCH):
            left = jnp.where(ids == row(hi, s), jnp.broadcast_to(row(w, s), (8, 16, 128)), zero)
            right = jnp.where(ids == row(lo, s), one, zero)
            d_ref[start + s] = lax.dot_general(
                right.reshape(128, 128),
                left.reshape(128, 128),
                (((1,), (1,)), ((), ())),
                preferred_element_type=F32,
            ).astype(BF16)
        return carry

    steps = d_ref.shape[0] // BATCH
    lax.fori_loop(0, steps // 2, densify, 0)
    ring.pass_on()
    beside += [pass_over(h3), pass_over(h1)]
    lax.fori_loop(steps // 2, steps * 7 // 8, densify, 0)
    ring.arrive()
    beside.append(pass_over(h2))
    lax.fori_loop(steps * 7 // 8, steps, densify, 0)
    for copy in beside:
        copy.wait()
    ring.drain()


def prepare(count, offsets, weights, features, weight):
    slots = offsets.shape[2]
    vmem = pl.BlockSpec(memory_space=pltpu.VMEM)
    hbm = pl.BlockSpec(memory_space=pltpu.HBM)
    return pl.pallas_call(
        prepare_kernel,
        out_shape=(
            jax.ShapeDtypeStruct((slots, 128, 128), BF16),
            jax.ShapeDtypeStruct((8, 4, 128, 128), BF16),
        ),
        in_specs=[pl.BlockSpec(memory_space=pltpu.SMEM)] + [hbm] * 4,
        out_specs=(vmem,) * 2,
        scratch_shapes=[
            pltpu.VMEM((slots, 128), jnp.int32),
            pltpu.VMEM((slots, 128), BF16),
            pltpu.VMEM((512, 128), BF16),
            pltpu.VMEM((128, 128), BF16),
            pltpu.SemaphoreType.DMA((4,)),
            pltpu.SemaphoreType.DMA((8,)),
            pltpu.SemaphoreType.DMA((8,)),
        ],
        compiler_params=pltpu.CompilerParams(
            collective_id=2, has_side_effects=True, vmem_limit_bytes=PREP_VMEM
        ),
        name="prepare",
    )(count, *in_hbm(offsets, weights, features, weight))


def in_hbm(*arrays):
    return [pltpu.with_memory_space_constraint(a, pltpu.HBM) for a in arrays]


def load_tables(row_hbm, col_hbm, row_ref, col_ref, sem):
    loads = [
        pltpu.make_async_copy(row_hbm, row_ref, sem.at[0]),
        pltpu.make_async_copy(col_hbm, col_ref, sem.at[1]),
    ]
    for copy in loads:
        copy.start()
    return loads


def forward_kernel(count_ref, row_hbm, col_hbm, d_ref, x_ref, t_ref, row_ref, col_ref, sem):
    loads = load_tables(row_hbm, col_hbm, row_ref, col_ref, sem)
    t_ref[...] = jnp.zeros_like(t_ref)
    for copy in loads:
        copy.wait()

    def step(i, carry):
        for s in range(SUM_BATCH):
            n = i * SUM_BATCH + s
            r, c = row_ref[0, 0, n], col_ref[0, 0, n]
            t_ref[r] += jnp.dot(x_ref[c], d_ref[n], preferred_element_type=F32)
        return carry

    lax.fori_loop(0, lax.div(count_ref[0, 0] + (SUM_BATCH - 1), SUM_BATCH), step, 0)


def backward_kernel(
    count_ref, row_hbm, col_hbm, d_ref, y_ref, result_ref, t_ref, result_hbm, row_ref, col_ref, sem
):
    loads = load_tables(row_hbm, col_hbm, row_ref, col_ref, sem)
    passed = pltpu.make_async_copy(result_ref, result_hbm, sem.at[2])
    passed.start()
    t_ref[...] = jnp.zeros_like(t_ref)
    for copy in loads:
        copy.wait()

    def step(i, carry):
        for s in range(SUM_BATCH):
            n = i * SUM_BATCH + s
            r, c = row_ref[0, 0, n], col_ref[0, 0, n]
            t_ref[c] += jnp.dot(d_ref[n], y_ref[r], preferred_element_type=F32)
        return carry

    lax.fori_loop(0, lax.div(count_ref[0, 0] + (SUM_BATCH - 1), SUM_BATCH), step, 0)
    passed.wait()


def block_sums(name, count, brow, bcol, dense, panel, blocks, result=None):
    smem, vmem = pl.BlockSpec(memory_space=pltpu.SMEM), pl.BlockSpec(memory_space=pltpu.VMEM)
    sums = jax.ShapeDtypeStruct((blocks, 128, 128), F32)
    params = pltpu.CompilerParams(vmem_limit_bytes=SUMS_VMEM)
    hbm = pl.BlockSpec(memory_space=pltpu.HBM)
    brow, bcol = in_hbm(brow, bcol)
    scratch = [
        pltpu.SMEM(brow.shape, jnp.int32),
        pltpu.SMEM(bcol.shape, jnp.int32),
        pltpu.SemaphoreType.DMA((3,)),
    ]
    if result is None:
        return pl.pallas_call(
            forward_kernel,
            in_specs=[smem, hbm, hbm] + [vmem] * 2,
            out_specs=vmem,
            scratch_shapes=scratch,
            out_shape=sums,
            compiler_params=params,
            name=name,
        )(count, brow, bcol, dense, panel)
    return pl.pallas_call(
        backward_kernel,
        in_specs=[smem, hbm, hbm] + [vmem] * 3,
        out_specs=(vmem, hbm),
        out_shape=(sums, jax.ShapeDtypeStruct(result.shape, result.dtype)),
        scratch_shapes=scratch,
        compiler_params=params,
        name=name,
    )(count, brow, bcol, dense, panel, result)


LEVELS = 32766.0
STEPS = 64.0 / math.log(2.0)


def block_rows_of(n):
    return pl.ds(n * 128 if isinstance(n, int) else pl.multiple_of(n * 128, 128), 128)


def encode(value, n, q_ref):
    size = jnp.abs(value)
    most = jnp.maximum(jnp.max(size, axis=0, keepdims=True), 1e-30)
    step = jnp.ceil(jnp.log(most) * STEPS)
    level = jnp.sqrt(size * jnp.exp(step * (-1.0 / STEPS))) * LEVELS + 0.5
    q_ref[block_rows_of(n)] = jnp.where(value < 0, -level, level).astype(jnp.int32).astype(jnp.int16)
    return step


def decode(n, q_ref, s_ref):
    level = q_ref[block_rows_of(n)].astype(jnp.int32).astype(F32)
    return level * jnp.abs(level) * s_ref[pl.ds(n, 1)]


class RingSum:
    def __init__(self, copies, value, me, plus, minus, q, scales, blocks):
        self.blocks = blocks
        self.copies, self.value, self.q, self.scales = copies, value, q, scales
        self.me, self.p1, self.p2, self.p3 = me, lax.rem(me + 1, 4), lax.rem(me + 2, 4), lax.rem(me + 3, 4)
        self.plus, self.minus = plus, minus
        self.sent = {}

    def code(self, value, slot):
        q = self.q.at[slot]
        steps = [encode(value(n, at), n, q) for n, at in enumerate(self.blocks)]
        steps.append(jnp.zeros((16 - len(steps), 128), F32))
        tail = jnp.concatenate(steps, axis=0)
        q[pl.ds(len(self.blocks) * 128, 16)] = tail.astype(jnp.int32).astype(jnp.int16)

    def start(self, slot, device):
        self.sent[slot] = self.copies.start(self.q.at[slot], self.q.at[slot + 6], device)

    def got(self, slot, n):
        return decode(n, self.q.at[slot + 6], self.scales.at[slot])

    def wait(self, *slots):
        for slot in slots:
            self.sent[slot].wait_recv()
            tail = self.q[slot + 6, pl.ds(len(self.blocks) * 128, 16)].astype(jnp.int32).astype(F32)
            self.scales[slot] = jnp.exp(tail * (1.0 / STEPS)) * (1.0 / (LEVELS * LEVELS))

    def code_far(self, half):
        self.code(self.value(self.p2, half), half)

    def send_far(self, half):
        self.start(half, (self.plus, self.minus)[half])

    def send_near(self, half):
        self.code(self.value((self.p3, self.p1)[half], half), 3 - half)
        self.start(3 - half, (self.minus, self.plus)[half])

    def pass_on(self, half):
        self.wait(half)
        own = self.value((self.p1, self.p3)[half], half)
        self.code(lambda n, at: own(n, at) + self.got(half, n), half + 4)
        self.start(half + 4, (self.plus, self.minus)[half])

    def arrive(self):
        self.wait(2, 3, 4, 5)

    def total(self, half, n, at):
        return (
            self.value(self.me, half)(n, at)
            + self.got(3 - half, n)
            + self.got(half + 4, n)
        )

    def drain(self):
        for copy in self.sent.values():
            copy.wait_send()


def reduce_gather_kernel(
    t_ref, bias_ref, cot_ref, out_ref, g_ref, bsum_ref,
    first_q, first_scale, second_q, second_scale, sums, pair, send, recv,
):
    here = place()
    x, z, y, h, k = here
    xp, xm = shifted(here, dx=1), shifted(here, dx=3)
    yp, ym = shifted(here, dy=1), shifted(here, dy=3)
    zp = shifted(here, dz=1)
    barrier = pltpu.get_barrier_semaphore()
    for peer in (xp, xm, yp, ym, zp):
        pl.semaphore_signal(barrier, inc=1, device_id=peer, device_id_type=MESH)
    copies = Copies(send, recv)

    four, one = [(i, Ellipsis) for i in range(4)], [(Ellipsis,)]

    def ring_over_x(number, q, scale, blocks, value):
        return RingSum(copies, value, x, xp, xm, q.at[number], scale.at[number], blocks)

    def ring_over_y(number, q, scale, blocks, value):
        return RingSum(copies, value, y, yp, ym, q.at[number], scale.at[number], blocks)

    def part_a(b):
        rows = slice(b * 128, (b + 1) * 128)
        return lambda p, half: lambda n, at: t_ref.at[p, half, :, rows, :][at]

    def part_b(b):
        rows = slice((2 + b) * 128, (3 + b) * 128)
        return lambda p, half: lambda n, at: t_ref.at[:, half, p, rows, :][at]

    def then(ring):
        return lambda p, half: lambda n, at: ring.total(half, p, (p, Ellipsis))

    first, second = [], []
    for b in range(2):
        over_x = ring_over_x(2 * b, first_q, first_scale, four, part_a(b))
        over_y = ring_over_y(2 * b + 1, first_q, first_scale, four, part_b(b))
        first.append((over_x, over_y))
        second.append(
            (
                ring_over_y(2 * b, second_q, second_scale, one, then(over_x)),
                ring_over_x(2 * b + 1, second_q, second_scale, one, then(over_y)),
            )
        )

    def each(rings, *steps):
        for half in range(2):
            for ring in rings:
                for step in steps:
                    getattr(ring, step)(half)

    def arrive(rings):
        for ring in rings:
            ring.arrive()

    def start(rings):
        each(rings, "code_far", "send_far")
        each(rings, "send_near")

    other = 1 - z

    def pair_up(b):
        for i, ring in enumerate(second[b]):
            for half in range(2):
                sums[b, half, i] = ring.total(half, 0, (Ellipsis,))
        return copies.start(sums.at[b, other], pair.at[b], zp)

    bias = bias_ref[...]

    def owner(b, lost):
        for i in range(2):
            pre = (sums[b, z, i] + pair[b, i]).T + bias
            rows = slice((2 * i + b) * 128, (2 * i + b + 1) * 128)
            out_ref[rows] = jnp.maximum(pre, 0.0).astype(BF16)
            grad = jnp.where(pre > 0, cot_ref[rows].astype(F32), 0.0)
            lost = lost + jnp.sum(grad, axis=0, keepdims=True)
            g_ref[x, z, y, rows] = grad.astype(BF16)
        return lost

    x1, x2, x3 = (lax.rem(x + i, 4) for i in (1, 2, 3))
    y1, y2, y3 = (lax.rem(y + i, 4) for i in (1, 2, 3))

    def rows_of(b):
        size = 128 if b else 64
        return pl.ds(b * 128, size), pl.ds((2 + b) * 128, size)

    def late_rows(start=0, size=64):
        return pl.ds(64 + start, size), pl.ds(256 + 64 + start, size)

    def late_near():
        (re, rf), (re0, rf0), (re1, rf1) = late_rows(), late_rows(0, 32), late_rows(32, 32)
        return (
            RingGather(
                copies, g_ref.at[x, z, y, re], g_ref.at[x, z, y3, re0], g_ref.at[x, z, y1, re1], yp, ym
            ),
            RingGather(
                copies, g_ref.at[x, z, y, rf], g_ref.at[x3, z, y, rf0], g_ref.at[x1, z, y, rf1], xp, xm
            ),
        )

    late_z = []

    def late_over_z(ref):
        late_z.append(copies.start(ref, ref, zp))

    def late_far(rings):
        re, rf = late_rows()
        rings[0].arrive()
        ring_e = RingGather(
            copies, g_ref.at[x, z, :, re], g_ref.at[x3, z, 0:2, re], g_ref.at[x1, z, 2:4, re], xp, xm
        )
        late_over_z(g_ref.at[x, z, :, re])
        rings[1].arrive()
        ring_f = RingGather(
            copies, g_ref.at[:, z, y, rf], g_ref.at[0:2, z, y3, rf], g_ref.at[2:4, z, y1, rf], yp, ym
        )
        late_over_z(g_ref.at[:, z, y, rf])
        return ring_e, ring_f

    def late_pass_on(rings):
        re, rf = late_rows()
        rings[0].pass_on()
        late_over_z(g_ref.at[x3, z, :, re])
        late_over_z(g_ref.at[x1, z, :, re])
        rings[1].pass_on()
        late_over_z(g_ref.at[:, z, y3, rf])
        late_over_z(g_ref.at[:, z, y1, rf])

    def late_arrive(rings):
        re, rf = late_rows()
        rings[0].arrive()
        late_over_z(g_ref.at[x2, z, :, re])
        rings[1].arrive()
        late_over_z(g_ref.at[:, z, y2, rf])

    def over_z(b):
        return [
            copies.start(g_ref.at[x, z, y, rows], g_ref.at[x, z, y, rows], zp) for rows in rows_of(b)
        ]

    def near(b, sent):
        ra, rb = rows_of(b)
        sent[0].wait_recv()
        ring_a = RingGather(
            copies, g_ref.at[x, :, y, ra], g_ref.at[x, 0, y3, ra], g_ref.at[x, 1, y1, ra], yp, ym
        )
        sent[1].wait_recv()
        ring_b = RingGather(
            copies, g_ref.at[x, :, y, rb], g_ref.at[x3, 0, y, rb], g_ref.at[x1, 1, y, rb], xp, xm
        )
        return ring_a, ring_b

    def far(b, rings):
        ra, rb = rows_of(b)
        rings[0].arrive()
        ring_a = RingGather(
            copies, g_ref.at[x, :, :, ra], g_ref.at[x3, 0, :, ra], g_ref.at[x1, 1, :, ra], xp, xm
        )
        rings[1].arrive()
        ring_b = RingGather(
            copies, g_ref.at[:, :, y, rb], g_ref.at[:, 0, y3, rb], g_ref.at[:, 1, y1, rb], yp, ym
        )
        return ring_a, ring_b

    def pass_on(rings):
        for ring in rings:
            ring.pass_on()

    each(first[0], "code_far")
    pl.semaphore_wait(barrier, 5)
    each(first[0], "send_far")
    each(first[0], "send_near")
    start(first[1])
    each(first[0], "pass_on")
    arrive(first[0])
    start(second[0])
    each(first[1], "pass_on")
    each(second[0], "pass_on")
    arrive(first[1])
    start(second[1])
    arrive(second[0])
    pair_0 = pair_up(0)
    each(second[1], "pass_on")
    pair_0.wait()
    lost = owner(0, jnp.zeros((1, 128), F32))
    z_0, late = over_z(0), late_near()
    arrive(second[1])
    pair_1 = pair_up(1)
    near_0 = near(0, z_0)
    pair_1.wait()
    bsum_ref[...] = owner(1, lost)
    z_1 = over_z(1)
    pass_on(late)
    pass_on(near_0)
    near_1 = near(1, z_1)
    far_late = late_far(late)
    far_0 = far(0, near_0)
    pass_on(near_1)
    late_pass_on(far_late)
    far_1 = far(1, near_1)
    late_arrive(far_late)
    pass_on(far_0)
    pass_on(far_1)
    arrive(far_0)
    arrive(far_1)
    for copy in late_z:
        copy.wait_recv()
    for copy in z_0 + z_1 + late_z:
        copy.wait_send()
    for rings in first + second + [near_0, near_1, far_0, far_1, late, far_late]:
        for ring in rings:
            ring.drain()


def reduce_gather(totals, bias, cotangent):
    vmem = pl.BlockSpec(memory_space=pltpu.VMEM)
    return pl.pallas_call(
        reduce_gather_kernel,
        out_shape=(
            jax.ShapeDtypeStruct((512, 128), BF16),
            jax.ShapeDtypeStruct((4, 2, 4, 512, 128), BF16),
            jax.ShapeDtypeStruct((1, 128), F32),
        ),
        in_specs=[vmem] * 3,
        out_specs=(vmem,) * 3,
        scratch_shapes=[
            pltpu.VMEM((4, 12, 4 * 128 + 16, 128), jnp.int16),
            pltpu.VMEM((4, 6, 16, 128), F32),
            pltpu.VMEM((4, 12, 128 + 16, 128), jnp.int16),
            pltpu.VMEM((4, 6, 16, 128), F32),
            pltpu.VMEM((2, 2, 2, 128, 128), F32),
            pltpu.VMEM((2, 2, 128, 128), F32),
            pltpu.SemaphoreType.DMA((114,)),
            pltpu.SemaphoreType.DMA((114,)),
        ],
        compiler_params=pltpu.CompilerParams(
            collective_id=0, has_side_effects=True, vmem_limit_bytes=REDUCE_VMEM
        ),
        name="reduce_gather",
    )(totals, bias, cotangent)


def finish_kernel(
    t_ref, feat_ref, weight_ref, bsum_ref, gf_ref, gw_ref, gb_ref,
    from_core, outgoing, from_chip, local, plane_parts, total, line_parts, whole,
    lost, plane_lost, send, recv,
):
    here = place()
    x, z, y, h, k = here
    mine, line = x * 4 + y, h * 2 + z
    plane = [
        (shifted(here, dx=dx, dy=dy), lax.rem(x + dx, 4) * 4 + lax.rem(y + dy, 4))
        for dx in range(4)
        for dy in range(4)
        if (dx, dy) != (0, 0)
    ]
    column = [shifted(here, dz=dz, dh=dh) for dh in range(4) for dz in range(2) if (dz, dh) != (0, 0)]
    partner = shifted(here, dk=1)
    barrier = pltpu.get_barrier_semaphore()
    for peer in [partner] + column + [p for p, _ in plane]:
        pl.semaphore_signal(barrier, inc=1, device_id=peer, device_id_type=MESH)
    lost[...] = jnp.concatenate([bsum_ref[...], jnp.zeros((7, 128), F32)], axis=0)
    pl.semaphore_wait(barrier, 23)
    copies = Copies(send, recv)

    other = 1 - k
    pairs = {}
    for dh in (2, 1, 3, 0):
        to = lax.rem(h + dh, 4)
        pairs[dh] = copies.start(t_ref.at[to, other], from_core.at[to], partner)
    above, below = shifted(here, dh=1), shifted(here, dh=3)
    chips = []

    def both(dh, part):
        to = lax.rem(h + dh, 4)
        return t_ref[to, k, part] + from_core[to, part]

    def send(value, slot, device):
        outgoing[slot] = value.astype(BF16)
        chips.append(copies.start(outgoing.at[slot], from_chip.at[slot], device))

    upper, lower = slice(0, 256), slice(256, 512)
    pairs[2].wait_recv()
    send(both(2, upper), 0, above)
    send(both(2, lower), 1, below)
    pairs[1].wait_recv()
    send(both(1, lower), 2, above)
    pairs[3].wait_recv()
    send(both(3, upper), 3, below)
    pairs[0].wait_recv()
    bias_plane = [copies.start(lost, plane_lost.at[mine], p) for p, _ in plane]
    plane_lost[mine] = lost[...]
    chips[0].wait_recv()
    send(both(1, upper) + from_chip[0].astype(F32), 4, above)
    chips[1].wait_recv()
    send(both(3, lower) + from_chip[1].astype(F32), 5, below)
    for copy in chips[2:]:
        copy.wait_recv()
    own = jnp.concatenate(
        [
            both(0, upper) + from_chip[3].astype(F32) + from_chip[4].astype(F32),
            both(0, lower) + from_chip[2].astype(F32) + from_chip[5].astype(F32),
        ],
        axis=0,
    )
    grad = own.astype(BF16)
    local[...] = lax.dot_general(
        feat_ref[...], grad, (((0,), (0,)), ((), ())), preferred_element_type=F32
    )

    def rows(i):
        return pl.ds(pl.multiple_of(i * 8, 8), 8)

    sent = [copies.start(local.at[rows(i)], plane_parts.at[mine], p) for p, i in plane]
    plane_parts[mine] = local[rows(mine)]
    gf_ref[...] = lax.dot_general(
        grad, weight_ref[...], (((1,), (1,)), ((), ())), preferred_element_type=F32
    ).astype(BF16)
    scale = 131072.0**-0.5
    for copy in bias_plane:
        copy.wait_recv()
    total[0, 8:16] = sum_of(plane_lost)
    for copy in sent:
        copy.wait_recv()
    total[0, 0:8] = sum_of(plane_parts)
    spread = [copies.start(total.at[0], total.at[1], partner)]
    spread[0].wait_recv()
    total[2] = total[0] + total[1]
    spread += [copies.start(total.at[2], line_parts.at[line], p) for p in column]
    line_parts[line] = total[2]
    for copy in spread[1:]:
        copy.wait_recv()
    both_sums = sum_of(line_parts) * scale
    whole[rows(mine)] = both_sums[0:8]
    gb_ref[...] = both_sums[8:9]
    back = [copies.start(whole.at[rows(mine)], whole.at[rows(mine)], p) for p, _ in plane]
    for copy in back:
        copy.wait_recv()
    gw_ref[...] = whole[...]
    for copy in [pairs[dh] for dh in range(4)] + bias_plane + chips + sent + spread + back:
        copy.wait_send()


def sum_of(ref):
    parts = [ref[i] for i in range(ref.shape[0])]
    while len(parts) > 1:
        parts = [a + b for a, b in zip(parts[::2], parts[1::2])]
    return parts[0]


def finish(partial, features, weight, bias_sum):
    vmem = pl.BlockSpec(memory_space=pltpu.VMEM)
    return pl.pallas_call(
        finish_kernel,
        out_shape=(
            jax.ShapeDtypeStruct((512, 128), BF16),
            jax.ShapeDtypeStruct((128, 128), F32),
            jax.ShapeDtypeStruct((1, 128), F32),
        ),
        in_specs=[vmem] * 4,
        out_specs=(vmem,) * 3,
        scratch_shapes=[
            pltpu.VMEM((4, 512, 128), F32),
            pltpu.VMEM((6, 256, 128), BF16),
            pltpu.VMEM((6, 256, 128), BF16),
            pltpu.VMEM((128, 128), F32),
            pltpu.VMEM((16, 8, 128), F32),
            pltpu.VMEM((3, 16, 128), F32),
            pltpu.VMEM((8, 16, 128), F32),
            pltpu.VMEM((128, 128), F32),
            pltpu.VMEM((8, 128), F32),
            pltpu.VMEM((16, 8, 128), F32),
            pltpu.SemaphoreType.DMA((63,)),
            pltpu.SemaphoreType.DMA((63,)),
        ],
        compiler_params=pltpu.CompilerParams(
            collective_id=1, has_side_effects=True, vmem_limit_bytes=FINISH_VMEM
        ),
        name="finish",
    )(partial, features, weight, bias_sum)


def export_kernel(*refs):
    count = len(refs) // 2
    sem = refs[-1]
    copies = [
        pltpu.make_async_copy(refs[i], refs[count + i], sem.at[i]) for i in range(count)
    ]
    for copy in copies:
        copy.start()
    for copy in copies:
        copy.wait()


def export(*arrays):
    vmem, hbm = pl.BlockSpec(memory_space=pltpu.VMEM), pl.BlockSpec(memory_space=pltpu.HBM)
    return pl.pallas_call(
        export_kernel,
        in_specs=[vmem] * len(arrays),
        out_specs=(hbm,) * len(arrays),
        out_shape=tuple(jax.ShapeDtypeStruct(a.shape, a.dtype) for a in arrays),
        scratch_shapes=[pltpu.SemaphoreType.DMA((len(arrays),))],
        compiler_params=pltpu.CompilerParams(vmem_limit_bytes=1 << 20),
        name="export",
    )(*arrays)


def shards(
    features, weight, bias, cotangent, block_count, block_rows, block_cols, edge_offsets, edge_weight
):
    tables = (block_count, block_rows, block_cols)
    dense, panel = prepare(block_count, edge_offsets, edge_weight, features, weight)
    totals = block_sums("forward", *tables, dense, panel.reshape(32, 128, 128), 128)
    output, grads, bias_sum = reduce_gather(
        totals.reshape(4, 2, 4, 512, 128), bias.reshape(1, 128), cotangent
    )
    partial, output = block_sums(
        "backward", *tables, dense, grads.reshape(128, 128, 128), 32, output
    )
    grad_features, grad_weight, grad_bias = export(
        *finish(partial.reshape(4, 2, 512, 128), features, weight, bias_sum)
    )
    return (output, grad_features, grad_weight, grad_bias.reshape(128))


def solution(mesh):
    return jax.shard_map(
        shards,
        mesh=mesh,
        in_specs=(
            P(("row", "col"), None),
            P(),
            P(),
            P(("row", "col"), None),
            P("row", "col"),
            P("row", "col", None),
            P("row", "col", None),
            P("row", "col", None, None),
            P("row", "col", None, None),
        ),
        out_specs=(P(("row", "col"), None), P(("row", "col"), None), P(), P()),
        check_vma=False,
    )
```
